32 devices in a mesh: dp: 4 (over z), seq: 4 (over y, x), mp: 2 (over core).
Axes of the slice: x: 2, y: 2, z: 4, core: 2. Of those that a mesh axis runs over, the one named last changes fastest.
Arguments:
- tokens: bfloat16 [8, 1024, 768], P('dp', 'seq'), may hold values from -6 to 6
- segments: int32 [8, 1024], P('dp'), may hold values from 0 to 3, as said below
- dropped: int32 [8], replicated, may hold values from 0 to 1, as said below
- qkv_weight: bfloat16 [2, 3, 768, 768], P(None, None, None, 'mp'), may hold values from -0.21875 to 0.21875
- qv_bias: float32 [2, 2, 768], P(None, None, 'mp'), may hold values from -3 to 3
- out_weight: bfloat16 [2, 768, 768], P(None, 'mp'), may hold values from -1.5 to 1.5
- out_bias: float32 [2, 768], replicated, may hold values from -2 to 2
- norm_gain: float32 [2, 2, 768], replicated, may hold values from 0.5 to 1.5
- norm_shift: float32 [2, 2, 768], replicated, may hold values from -1.5 to 1.5
- up_weight: bfloat16 [2, 768, 3072], P(None, None, 'mp'), may hold values from -0.21875 to 0.21875
- up_bias: float32 [2, 3072], P(None, 'mp'), may hold values from -3 to 3
- down_weight: bfloat16 [2, 3072, 768], P(None, 'mp'), may hold values from -0.109375 to 0.109375
- down_bias: float32 [2, 768], replicated, may hold values from -2 to 2
- cotangent: bfloat16 [8, 1024, 768], P('dp', 'seq'), may hold values from -6 to 6
Outputs:
- outputs: float32 [8, 1024, 768], P('dp', 'seq')
- tokens_grad: float32 [8, 1024, 768], P('dp', 'seq')
- qkv_grad: float32 [2, 3, 768, 768], P(None, None, 'dp', 'mp')
- qv_bias_grad: float32 [2, 2, 768], P(None, None, 'mp')
- out_grad: float32 [2, 768, 768], P(None, 'mp', 'dp')
- out_bias_grad: float32 [2, 768], replicated
- gain_grad: float32 [2, 2, 768], replicated
- shift_grad: float32 [2, 2, 768], replicated
- up_grad: float32 [2, 768, 3072], P(None, 'dp', 'mp')
- up_bias_grad: float32 [2, 3072], P(None, 'mp')
- down_grad: float32 [2, 3072, 768], P(None, 'mp', 'dp')
- down_bias_grad: float32 [2, 768], replicated
The draws below stay inside these ranges and needn't reach their ends.
Inputs may be any that keep to these rules, and one draw needn't show every extreme that they name: `dropped`: exactly 1 row have 1. `segments`: within a row the ids never fall and every id appears.
All inputs are finite; a program needn't handle non-finite values.
Results may differ from the reference program's by a relative error of at most 0.033.
Values may be sent and summed in bfloat16 or wider, within the bound.
No kernel may reach another device: no remote copies, remote signals or barrier semaphores. Data moves between devices by JAX's collectives and lax.ppermute only.
A program may use at most 128 MiB of HBM per device.

```python
import jax
import jax.numpy as jnp
from jax import lax

D = 768
HEADS = 12
HEAD = 64
FF = 3072
LAYERS = 2
LEN = 1024
ROWS = 8
DROPPED = 1
N_SEQ = 4


def draw_dropped(key, part):
    order = jax.random.permutation(jax.random.fold_in(key, 7), ROWS)
    return (order < DROPPED).astype(jnp.int32)


def draw_segments(key, part):
    span = LEN // N_SEQ
    short_most = max(1, (span - 1) // 3)
    base = jax.random.fold_in(key, 11)
    key_long, key_short = jax.random.split(base)
    longest = jax.random.randint(key_long, (ROWS,), 0, 4)
    shorts = jax.random.randint(key_short, (ROWS, 4), 1, short_most + 1)
    which = jnp.arange(4)[None, :] == longest[:, None]
    lengths = jnp.where(which, 0, shorts)
    rest = LEN - jnp.sum(lengths, axis=1, keepdims=True)
    lengths = jnp.where(which, rest, lengths)
    ends = jnp.cumsum(lengths, axis=1)
    places = jnp.arange(LEN)
    return jnp.sum((places[None, :, None] >= ends[:, None, :3]).astype(jnp.int32), axis=2).astype(jnp.int32)


def block_levels(stream_key, dims, pieces, least, high):
    def one(position, blocks):
        heights = jax.random.uniform(jax.random.fold_in(jax.random.fold_in(stream_key, 6), position), (blocks,), jnp.float32, least / len(pieces), high / len(pieces))
        return jnp.repeat(jnp.exp(heights), dims[position] // blocks).reshape((-1,) + (1,) * (len(dims) - position - 1))

    level = one(*pieces[0])
    for cut in pieces[1:]:
        level = level * one(*cut)
    return level


def centred(stream_key, shape, scale, most, cuts=(), dtype=jnp.bfloat16):
    level = block_levels(stream_key, shape, cuts, -0.22, 0.18) if cuts else 1.0
    drawn = jax.random.normal(stream_key, shape, jnp.float32) * scale * level
    return jnp.minimum(jnp.maximum(drawn, -most), most).astype(dtype)


def setup_inputs(seed: int = 0) -> dict:
    splits = jax.random.split(jax.random.key(seed), 15)
    tokens = centred(splits[0], (ROWS, LEN, D), 1.0, 6.0, ((0, 4), (1, 4)))
    segments = draw_segments(jax.random.fold_in(splits[14], 71), 0)
    dropped = draw_dropped(jax.random.fold_in(splits[14], 71), 0)
    qkv_weight = centred(splits[3], (LAYERS, 3, D, D), D ** -0.5, 0.21875, ((3, 2),))
    qv_bias = centred(splits[4], (LAYERS, 2, D), 0.5, 3.0, ((2, 2),), jnp.float32)
    out_weight = centred(splits[5], (LAYERS, D, D), 16 ** -0.5, 1.5, ((1, 2),))
    out_bias = centred(splits[6], (LAYERS, D), 0.3, 2.0, (), jnp.float32)
    norm_gain = jnp.clip(1.0 + 0.1 * jax.random.normal(splits[7], (LAYERS, 2, D), jnp.float32), 0.5, 1.5)
    norm_shift = centred(splits[8], (LAYERS, 2, D), 0.2, 1.5, (), jnp.float32)
    up_weight = centred(splits[9], (LAYERS, D, FF), D ** -0.5, 0.21875, ((2, 2),))
    up_bias = centred(splits[10], (LAYERS, FF), 0.5, 3.0, ((1, 2),), jnp.float32)
    down_weight = centred(splits[11], (LAYERS, FF, D), FF ** -0.5, 0.109375, ((1, 2),))
    down_bias = centred(splits[12], (LAYERS, D), 0.3, 2.0, (), jnp.float32)
    cotangent = centred(splits[13], (ROWS, LEN, D), 1.0, 6.0, ((0, 4), (1, 4)))
    return {"tokens": tokens, "segments": segments, "dropped": dropped, "qkv_weight": qkv_weight, "qv_bias": qv_bias, "out_weight": out_weight, "out_bias": out_bias, "norm_gain": norm_gain, "norm_shift": norm_shift, "up_weight": up_weight, "up_bias": up_bias, "down_weight": down_weight, "down_bias": down_bias, "cotangent": cotangent}


@jax.custom_vjp
def low(v):
    return lax.optimization_barrier(v.astype(jnp.bfloat16)).astype(jnp.float32)

@jax.custom_vjp
def low_back(v):
    return v

def low_keep(v):
    return (low(v), None)

def low_pass(kept, grad):
    return (grad,)

def back_keep(v):
    return (v, None)

def back_low(kept, grad):
    return (low(grad),)
low.defvjp(low_keep, low_pass)
low_back.defvjp(back_keep, back_low)

def rounded_both(value):
    return low(low_back(value))

def product(left, right):
    return jnp.dot(left, right, precision=lax.Precision.HIGHEST)

def layer_norm(rows_in, gain, shift):
    center = rows_in - lax.optimization_barrier(jnp.mean(rows_in, axis=-1, keepdims=True))
    spread = lax.optimization_barrier(jnp.mean(center * center, axis=-1, keepdims=True))
    return center * lax.rsqrt(spread + 1e-05) * gain + shift

def layer(inputs, same, params):
    weight_qkv, bias_qv, weight_out, bias_out, gain, shift, weight_up, bias_up, weight_down, bias_down = params
    length = inputs.shape[0]
    low_in = low(inputs)
    query = rounded_both(product(low_in, weight_qkv[0]) + bias_qv[0]).reshape(length, HEADS, HEAD)
    keys = rounded_both(product(low_in, weight_qkv[1])).reshape(length, HEADS, HEAD)
    values = rounded_both(product(low_in, weight_qkv[2]) + bias_qv[1]).reshape(length, HEADS, HEAD)
    scores = jnp.einsum('qhd,khd->hqk', query, keys, precision=lax.Precision.HIGHEST) * 0.125
    scores = low_back(scores)
    scores = jnp.where(same[None], scores, -1e+30)
    weights = low(jax.nn.softmax(scores, axis=-1))
    context = jnp.einsum('hqk,khd->qhd', weights, values, precision=lax.Precision.HIGHEST)
    context = rounded_both(context.reshape(length, D))
    attended = low_back(product(context, weight_out)) + bias_out
    hidden = layer_norm(inputs + attended, gain[0], shift[0])
    low_hidden = low(hidden)
    pre_act = low_back(product(low_hidden, weight_up) + bias_up)
    active = low(jax.nn.gelu(pre_act, approximate=False))
    mixed = low_back(product(active, weight_down)) + bias_down
    return layer_norm(hidden + mixed, gain[1], shift[1])

def layer_part(index, params):
    return tuple((array[index] for array in params))

def row_forward(inputs, segment_row, drop_flag, params):
    same = segment_row[:, None] == segment_row[None, :]
    first = layer(inputs, same, layer_part(0, params))
    second = layer(first, same, layer_part(1, params))
    return jnp.where(drop_flag > 0, first, second)

def add_arrays(left_side, right_side):
    return left_side + right_side

def reference(tokens, segments, dropped, qkv_weight, qv_bias, out_weight, out_bias, norm_gain, norm_shift, up_weight, up_bias, down_weight, down_bias, cotangent):
    params = tuple((array.astype(jnp.float32) for array in (qkv_weight, qv_bias, out_weight, out_bias, norm_gain, norm_shift, up_weight, up_bias, down_weight, down_bias)))

    def one_row(totals, item):
        row_tokens, segment_row, drop_flag, row_cot = item

        def forward_fn(inputs, weights_all):
            return row_forward(inputs, segment_row, drop_flag, weights_all)
        result, pullback = jax.vjp(forward_fn, row_tokens.astype(jnp.float32), params)
        grad_inputs, grad_params = pullback(row_cot.astype(jnp.float32))
        totals = jax.tree.map(add_arrays, totals, grad_params)
        return (totals, (result, grad_inputs))
    zeros = jax.tree.map(jnp.zeros_like, params)
    totals, (outputs, tokens_grad) = lax.scan(one_row, zeros, (tokens, segments, dropped, cotangent))
    return (outputs, tokens_grad, totals[0], totals[1], totals[2], totals[3], totals[4], totals[5], totals[6], totals[7], totals[8], totals[9])
```

```python
import jax
import jax.numpy as jnp
from jax import lax
from jax.sharding import PartitionSpec as P

HEAD = 64
eps_norm = 1e-05
root_half = 0.7071067811865476
inv_root_tau = 0.3989422804014327
f32 = jnp.float32
bf16 = jnp.bfloat16


def dot_nn(left, right):
    return lax.dot_general(left, right, (((1,), (0,)), ((), ())), preferred_element_type=f32)


def dot_nt(left, right):
    return lax.dot_general(left, right, (((1,), (1,)), ((), ())), preferred_element_type=f32)


def dot_tn(left, right):
    return lax.dot_general(left, right, (((0,), (0,)), ((), ())), preferred_element_type=f32)


def swap(value, axis, mask):
    count = lax.axis_size(axis)
    return lax.ppermute(value, axis, [(i, i ^ mask) for i in range(count)])


def place_bit(axis, bit):
    return (lax.axis_index(axis) >> bit) & 1


def bits_of(axis):
    count = lax.axis_size(axis)
    number = count.bit_length() - 1
    assert 1 << number == count
    return number


def pick(value, index, axis):
    return lax.dynamic_index_in_dim(value, index, axis, keepdims=False)


def mp_sum(partial_sum):
    own = partial_sum.astype(bf16)
    return own.astype(f32) + swap(own, "mp", 1).astype(f32)


def add_low(left, right):
    return (left.astype(f32) + right.astype(f32)).astype(bf16)


def normalize(rows_in, gain, shift):
    center = rows_in - jnp.mean(rows_in, axis=-1, keepdims=True)
    scale = lax.rsqrt(jnp.mean(center * center, axis=-1, keepdims=True) + eps_norm)
    unit = center * scale
    return (unit * gain + shift, unit, scale)


def normalize_back(grad_out, unit, scale, gain):
    grad_unit = grad_out * gain
    inner = (
        grad_unit
        - jnp.mean(grad_unit, axis=-1, keepdims=True)
        - unit * jnp.mean(grad_unit * unit, axis=-1, keepdims=True)
    )
    return (inner * scale, jnp.sum(grad_out * unit, axis=0), jnp.sum(grad_out, axis=0))


def share_halves(half):
    other = swap(half, "mp", 1)
    first = lax.axis_index("mp") == 0
    return jnp.where(first, jnp.stack([half, other]), jnp.stack([other, half])).reshape(
        (2 * half.shape[0],) + half.shape[1:]
    )


def from_far(value, mask):
    count = value.shape[0] // 2
    mine = pick(value.reshape((2, count) + value.shape[1:]), lax.axis_index("mp"), 0)
    return share_halves(swap(mine, "seq", mask))


def reduce_bundle(grad, order):
    shares = lax.axis_size("dp")
    width = grad.shape[0] // shares
    keep = grad.reshape(shares, width, grad.shape[1])
    arrived = None
    steps = [("seq", order[0])] + [("dp", b) for b in range(bits_of("dp"))]
    steps += [("seq", b) for b in order[1:]]

    def part(value, axis, bit, side):
        if axis == "seq":
            half = value.shape[2] // 2
            return lax.dynamic_slice_in_dim(value, side * half, half, 2)
        shaped = value.reshape(value.shape[0] // 2, 2, width, value.shape[2])
        return pick(shaped, side, 1)

    for axis, bit in steps:
        mine = place_bit(axis, bit)
        send = part(keep, axis, bit, 1 - mine)
        keep_next = part(keep, axis, bit, mine)
        if arrived is not None:
            send = add_low(send, part(arrived, axis, bit, 1 - mine))
            keep_next = add_low(keep_next, part(arrived, axis, bit, mine))
        arrived = swap(send.astype(bf16), axis, 1 << bit)
        keep = keep_next
    total = add_low(keep, arrived)[0]
    for bit in reversed(order):
        other = swap(total, "seq", 1 << bit)
        first = place_bit("seq", bit) == 0
        total = jnp.where(
            first,
            jnp.concatenate([total, other], axis=1),
            jnp.concatenate([other, total], axis=1),
        )
    return total


def split_heads(value):
    return value.reshape(value.shape[0], value.shape[1] // HEAD, HEAD)


def attend(query, key_all, value_all, same):
    scores = (
        jnp.einsum("qhd,khd->hqk", split_heads(query), split_heads(key_all), preferred_element_type=f32)
        * 0.125
    )
    scores = jnp.where(same[None], scores, -1e30)
    peak = jnp.max(scores, axis=-1, keepdims=True)
    raised = jnp.exp(scores - peak)
    total = jnp.sum(raised, axis=-1, keepdims=True)
    weights = (raised / total).astype(bf16)
    context = jnp.einsum("hqk,khd->qhd", weights, split_heads(value_all), preferred_element_type=f32)
    return (context.astype(bf16).reshape(query.shape), peak[..., 0] + jnp.log(total[..., 0]))


def attend_back(query, key_all, value_all, same, log_total, grad_context):
    query, key_all, value_all, grad_context = map(
        split_heads, (query, key_all, value_all, grad_context)
    )
    scores = jnp.einsum("qhd,khd->hqk", query, key_all, preferred_element_type=f32) * 0.125
    chance = jnp.where(same[None], jnp.exp(scores - log_total[..., None]), 0.0)
    grad_chance = jnp.einsum("qhd,khd->hqk", grad_context, value_all, preferred_element_type=f32)
    grad_value = jnp.einsum("hqk,qhd->khd", chance.astype(bf16), grad_context, preferred_element_type=f32)
    grad_score = chance * (grad_chance - jnp.sum(grad_chance * chance, axis=-1, keepdims=True))
    grad_score = grad_score.astype(bf16)
    grad_query = jnp.einsum("hqk,khd->qhd", grad_score, key_all, preferred_element_type=f32) * 0.125
    grad_key = jnp.einsum("hqk,qhd->khd", grad_score, query, preferred_element_type=f32) * 0.125

    def joined(value):
        return value.astype(bf16).reshape(value.shape[0], -1)

    return joined(grad_query), joined(grad_key), joined(grad_value)


def layer_forward(inputs, low_own, low_others, same, params):
    (
        weight_qkv,
        bias_qv,
        weight_out,
        bias_out,
        gain,
        shift,
        weight_up,
        bias_up,
        weight_down,
        bias_down,
    ) = params
    low_all = jnp.concatenate([low_own] + low_others, axis=0)
    query = (dot_nn(low_own, weight_qkv[0]) + bias_qv[0]).astype(bf16)
    keys = dot_nn(low_all, weight_qkv[1]).astype(bf16)
    values = (dot_nn(low_all, weight_qkv[2]) + bias_qv[1]).astype(bf16)
    context, log_total = attend(query, keys, values, same)
    attended = mp_sum(dot_nn(context, weight_out)) + bias_out
    hidden, unit_one, scale_one = normalize(inputs + attended, gain[0], shift[0])
    low_hidden = hidden.astype(bf16)
    pre_act = dot_nn(low_hidden, weight_up) + bias_up
    low_act = jax.nn.gelu(pre_act, approximate=False).astype(bf16)
    mixed = mp_sum(dot_nn(low_act, weight_down)) + bias_down
    result, unit_two, scale_two = normalize(hidden + mixed, gain[1], shift[1])
    saved = (
        low_all,
        query,
        keys,
        values,
        log_total,
        context,
        unit_one,
        scale_one,
        low_hidden,
        pre_act,
        low_act,
        unit_two,
        scale_two,
    )
    return (result, saved)


def layer_backward(grad_flat, saved, same, params, orders):
    (
        weight_qkv,
        bias_qv,
        weight_out,
        bias_out,
        gain,
        shift,
        weight_up,
        bias_up,
        weight_down,
        bias_down,
    ) = params
    (
        low_all,
        query,
        keys,
        values,
        log_total,
        context,
        unit_one,
        scale_one,
        low_hidden,
        pre_act,
        low_act,
        unit_two,
        scale_two,
    ) = saved
    span = grad_flat.shape[0]
    grad_mixed, gain_two, shift_two = normalize_back(grad_flat, unit_two, scale_two, gain[1])
    grad_bias_down = jnp.sum(grad_mixed, axis=0)
    low_mixed = grad_mixed.astype(bf16)
    down_sum = reduce_bundle(dot_tn(low_mixed, low_act).astype(bf16), orders[0])
    grad_act = dot_nt(low_mixed, weight_down)
    normal_cdf = 0.5 * (1.0 + lax.erf(pre_act * root_half))
    density = jnp.exp(-0.5 * pre_act * pre_act) * inv_root_tau
    low_pre = (grad_act * (normal_cdf + pre_act * density)).astype(bf16)
    grad_bias_up = jnp.sum(low_pre.astype(f32), axis=0)
    up_sum = reduce_bundle(dot_tn(low_hidden, low_pre).astype(bf16), orders[1])
    grad_hidden = grad_mixed + mp_sum(dot_nt(low_pre, weight_up))
    grad_attended, gain_one, shift_one = normalize_back(grad_hidden, unit_one, scale_one, gain[0])
    grad_bias_out = jnp.sum(grad_attended, axis=0)
    low_attended = grad_attended.astype(bf16)
    grad_context = dot_nt(low_attended, weight_out).astype(bf16)
    grad_query, grad_key, grad_value = attend_back(query, keys, values, same, log_total, grad_context)

    low_own = low_all[:span]
    attn_sum = reduce_bundle(
        jnp.concatenate(
            [
                dot_tn(low_own, grad_query).astype(bf16),
                dot_tn(low_all, grad_key).astype(bf16),
                dot_tn(low_all, grad_value).astype(bf16),
                dot_tn(low_attended, context).astype(bf16),
            ],
            axis=1,
        ),
        orders[2],
    )
    place = lax.axis_index("mp")
    back_kv = dot_nt(grad_key, weight_qkv[1]) + dot_nt(grad_value, weight_qkv[2])
    parts = back_kv.shape[0] // span
    back_kv = back_kv.reshape(parts, 2, span // 2, back_kv.shape[1])
    back_own = back_kv[0] + dot_nt(grad_query, weight_qkv[0]).reshape(back_kv.shape[1:])

    def half_sum(value):
        send = pick(value, 1 - place, 0).astype(bf16)
        return pick(value, place, 0).astype(bf16).astype(f32) + swap(send, "mp", 1).astype(f32)

    total_half = half_sum(back_own)
    for j in range(1, parts):
        total_half = total_half + swap(half_sum(back_kv[j]).astype(bf16), "seq", 2 * j).astype(f32)
    back_total = share_halves(total_half.astype(bf16))
    grad_inputs = grad_attended + back_total.astype(f32)
    small = (
        jnp.stack(
            [jnp.sum(grad_query.astype(f32), axis=0), jnp.sum(grad_value.astype(f32), axis=0)]
        ),
        grad_bias_out,
        jnp.stack([gain_one, gain_two]),
        jnp.stack([shift_one, shift_two]),
        grad_bias_up,
        grad_bias_down,
    )
    return (grad_inputs, small, (attn_sum, up_sum, down_sum))


def layer_part(index, params):
    return tuple((array[index] for array in params))


def stack_pair(first_part, second_part):
    return jnp.stack([first_part, second_part])


def local(
    tokens,
    segments,
    dropped,
    qkv_weight,
    qv_bias,
    out_weight,
    out_bias,
    norm_gain,
    norm_shift,
    up_weight,
    up_bias,
    down_weight,
    down_bias,
    cotangent,
):
    params = (
        qkv_weight,
        qv_bias,
        out_weight,
        out_bias,
        norm_gain,
        norm_shift,
        up_weight,
        up_bias,
        down_weight,
        down_bias,
    )
    first = layer_part(0, params)
    second = layer_part(1, params)
    rows_here, span, width = tokens.shape
    assert rows_here == 2
    places = lax.axis_size("seq")
    place = lax.axis_index("seq")
    row = place & 1
    tokens_mine = pick(tokens, row, 0)
    tokens_partner = pick(tokens, 1 - row, 0)
    chunks = [tokens_mine]
    for c in range(1, places):
        chunks.append(from_far(tokens_mine if c % 2 == 0 else tokens_partner, c))
    low_own = jnp.concatenate(chunks[:2], axis=0)
    low_others = [jnp.concatenate(chunks[c : c + 2], axis=0) for c in range(2, places, 2)]
    seg_row = pick(segments, row, 0).reshape(places, span)
    for bit in range(bits_of("seq")):
        shaped = seg_row.reshape(places >> (bit + 1), 2, 1 << bit, span)
        seg_row = jnp.where(place_bit("seq", bit) == 1, shaped[:, ::-1], shaped).reshape(places, span)
    seg_keys = seg_row.reshape(places * span)
    same = seg_keys[: 2 * span, None] == seg_keys[None, :]
    cot_mine = pick(cotangent, row, 0)
    cot_far = from_far(pick(cotangent, 1 - row, 0), 1)
    cot_float = jnp.concatenate([cot_mine, cot_far], axis=0).astype(f32)
    kept = lax.dynamic_index_in_dim(dropped, lax.axis_index("dp") * rows_here + row, 0, keepdims=False) == 0

    hidden_one, saved_one = layer_forward(low_own.astype(f32), low_own, low_others, same, first)
    low_one = hidden_one.astype(bf16)
    others_one = [from_far(low_one, c) for c in range(2, places, 2)]
    result_two, saved_two = layer_forward(hidden_one, low_one, others_one, same, second)
    result = jnp.where(kept, result_two, hidden_one)

    def send_back(value):
        mine, partner = value[:span], value[span:].astype(bf16)
        arrived = from_far(partner, 1).astype(f32)
        return jnp.where(row == 0, jnp.stack([mine, arrived]), jnp.stack([arrived, mine]))

    outputs = send_back(result)
    grad_two = jnp.where(kept, cot_float, 0.0)
    up_down = list(range(bits_of("seq")))
    down_up = up_down[::-1]
    grad_in_two, small_two, big_two = layer_backward(
        grad_two, saved_two, same, second, (up_down, down_up, up_down)
    )
    grad_hidden_one = jnp.where(kept, grad_in_two, cot_float)
    grad_tokens, small_one, big_one = layer_backward(
        grad_hidden_one, saved_one, same, first, (down_up, up_down, down_up)
    )
    tokens_grad = send_back(grad_tokens)
    small = jax.tree.map(stack_pair, small_one, small_two)
    qv_sum, out_bias_sum, gain_sum, shift_sum, up_bias_sum, down_bias_sum = lax.psum(small, ("dp", "seq"))

    def attn_parts(total):
        quarter = total.shape[1] // 4
        pieces = [total[:, i * quarter : (i + 1) * quarter].astype(f32) for i in range(4)]
        return jnp.stack(pieces[:3]), pieces[3].T

    qkv_sum, out_sum = jax.tree.map(stack_pair, attn_parts(big_one[0]), attn_parts(big_two[0]))
    up_sum = jnp.stack([big_one[1].astype(f32), big_two[1].astype(f32)])
    down_sum = jnp.stack([big_one[2].astype(f32).T, big_two[2].astype(f32).T])
    return (
        outputs,
        tokens_grad,
        qkv_sum,
        qv_sum,
        out_sum,
        out_bias_sum,
        gain_sum,
        shift_sum,
        up_sum,
        up_bias_sum,
        down_sum,
        down_bias_sum,
    )


def solution(mesh):
    placed = (
        P("dp", "seq", None),
        P("dp", None),
        P(),
        P(None, None, None, "mp"),
        P(None, None, "mp"),
        P(None, "mp", None),
        P(),
        P(),
        P(),
        P(None, None, "mp"),
        P(None, "mp"),
        P(None, "mp", None),
        P(),
        P("dp", "seq", None),
    )
    return jax.shard_map(
        local,
        mesh=mesh,
        in_specs=placed,
        out_specs=(
            P("dp", "seq", None),
            P("dp", "seq", None),
            P(None, None, "dp", "mp"),
            P(None, None, "mp"),
            P(None, "mp", "dp"),
            P(),
            P(),
            P(),
            P(None, "dp", "mp"),
            P(None, "mp"),
            P(None, "mp", "dp"),
            P(),
        ),
        check_vma=False,
    )
```

```python
import jax
import jax.numpy as jnp
from jax import lax
from jax.sharding import PartitionSpec as P

HEAD = 64
eps_norm = 1e-05
root_half = 0.7071067811865476
inv_root_tau = 0.3989422804014327
f32 = jnp.float32
bf16 = jnp.bfloat16


def dot_nn(left, right):
    return lax.dot_general(left, right, (((1,), (0,)), ((), ())), preferred_element_type=f32)


def dot_nt(left, right):
    return lax.dot_general(left, right, (((1,), (1,)), ((), ())), preferred_element_type=f32)


def dot_tn(left, right):
    return lax.dot_general(left, right, (((0,), (0,)), ((), ())), preferred_element_type=f32)


def swap(value, axis, mask):
    count = lax.axis_size(axis)
    return lax.ppermute(value, axis, [(i, i ^ mask) for i in range(count)])


def place_bit(axis, bit):
    return (lax.axis_index(axis) >> bit) & 1


def bits_of(axis):
    count = lax.axis_size(axis)
    number = count.bit_length() - 1
    assert 1 << number == count
    return number


def pick(value, index, axis):
    return lax.dynamic_index_in_dim(value, index, axis, keepdims=False)


def mp_sum(partial_sum):
    own = partial_sum.astype(bf16)
    return own.astype(f32) + swap(own, "mp", 1).astype(f32)


def add_low(left, right):
    return (left.astype(f32) + right.astype(f32)).astype(bf16)


def normalize(rows_in, gain, shift):
    center = rows_in - jnp.mean(rows_in, axis=-1, keepdims=True)
    scale = lax.rsqrt(jnp.mean(center * center, axis=-1, keepdims=True) + eps_norm)
    unit = center * scale
    return (unit * gain + shift, unit, scale)


def normalize_back(grad_out, unit, scale, gain):
    grad_unit = grad_out * gain
    inner = (
        grad_unit
        - jnp.mean(grad_unit, axis=-1, keepdims=True)
        - unit * jnp.mean(grad_unit * unit, axis=-1, keepdims=True)
    )
    return (inner * scale, jnp.sum(grad_out * unit, axis=0), jnp.sum(grad_out, axis=0))


def share_halves(half):
    other = swap(half, "mp", 1)
    first = lax.axis_index("mp") == 0
    return jnp.where(first, jnp.stack([half, other]), jnp.stack([other, half])).reshape(
        (2 * half.shape[0],) + half.shape[1:]
    )


def from_far(value, mask):
    count = value.shape[0] // 2
    mine = pick(value.reshape((2, count) + value.shape[1:]), lax.axis_index("mp"), 0)
    return share_halves(swap(mine, "seq", mask))


def reduce_bundle(grad, order):
    shares = lax.axis_size("dp")
    width = grad.shape[0] // shares
    keep = grad.reshape(shares, width, grad.shape[1])
    arrived = None
    steps = [("seq", order[0])] + [("dp", b) for b in range(bits_of("dp"))]
    steps += [("seq", b) for b in order[1:]]

    def part(value, axis, bit, side):
        if axis == "seq":
            half = value.shape[2] // 2
            return lax.dynamic_slice_in_dim(value, side * half, half, 2)
        shaped = value.reshape(value.shape[0] // 2, 2, width, value.shape[2])
        return pick(shaped, side, 1)

    for axis, bit in steps:
        mine = place_bit(axis, bit)
        send = part(keep, axis, bit, 1 - mine)
        keep_next = part(keep, axis, bit, mine)
        if arrived is not None:
            send = add_low(send, part(arrived, axis, bit, 1 - mine))
            keep_next = add_low(keep_next, part(arrived, axis, bit, mine))
        arrived = swap(send.astype(bf16), axis, 1 << bit)
        keep = keep_next
    total = add_low(keep, arrived)[0]
    for bit in reversed(order):
        other = swap(total, "seq", 1 << bit)
        first = place_bit("seq", bit) == 0
        total = jnp.where(
            first,
            jnp.concatenate([total, other], axis=1),
            jnp.concatenate([other, total], axis=1),
        )
    return total


def sum_everywhere(value):
    for axis in ("seq", "dp"):
        for bit in range(bits_of(axis)):
            value = value + swap(value, axis, 1 << bit)
    return value


def split_heads(value):
    return value.reshape(value.shape[0], value.shape[1] // HEAD, HEAD)


def attend(query, key_all, value_all, same):
    scores = (
        jnp.einsum("qhd,khd->hqk", split_heads(query), split_heads(key_all), preferred_element_type=f32)
        * 0.125
    )
    scores = jnp.where(same[None], scores, -1e30)
    peak = jnp.max(scores, axis=-1, keepdims=True)
    raised = jnp.exp(scores - peak)
    total = jnp.sum(raised, axis=-1, keepdims=True)
    weights = (raised / total).astype(bf16)
    context = jnp.einsum("hqk,khd->qhd", weights, split_heads(value_all), preferred_element_type=f32)
    return (context.astype(bf16).reshape(query.shape), peak[..., 0] + jnp.log(total[..., 0]))


def attend_back(query, key_all, value_all, same, log_total, grad_context):
    query, key_all, value_all, grad_context = map(
        split_heads, (query, key_all, value_all, grad_context)
    )
    scores = jnp.einsum("qhd,khd->hqk", query, key_all, preferred_element_type=f32) * 0.125
    chance = jnp.where(same[None], jnp.exp(scores - log_total[..., None]), 0.0)
    grad_chance = jnp.einsum("qhd,khd->hqk", grad_context, value_all, preferred_element_type=f32)
    grad_value = jnp.einsum("hqk,qhd->khd", chance.astype(bf16), grad_context, preferred_element_type=f32)
    grad_score = chance * (grad_chance - jnp.sum(grad_chance * chance, axis=-1, keepdims=True))
    grad_score = grad_score.astype(bf16)
    grad_query = jnp.einsum("hqk,khd->qhd", grad_score, key_all, preferred_element_type=f32) * 0.125
    grad_key = jnp.einsum("hqk,qhd->khd", grad_score, query, preferred_element_type=f32) * 0.125

    def joined(value):
        return value.astype(bf16).reshape(value.shape[0], -1)

    return joined(grad_query), joined(grad_key), joined(grad_value)


def layer_forward(inputs, low_own, low_others, same, params):
    (
        weight_qkv,
        bias_qv,
        weight_out,
        bias_out,
        gain,
        shift,
        weight_up,
        bias_up,
        weight_down,
        bias_down,
    ) = params
    low_all = jnp.concatenate([low_own] + low_others, axis=0)
    query = (dot_nn(low_own, weight_qkv[0]) + bias_qv[0]).astype(bf16)
    keys = dot_nn(low_all, weight_qkv[1]).astype(bf16)
    values = (dot_nn(low_all, weight_qkv[2]) + bias_qv[1]).astype(bf16)
    context, log_total = attend(query, keys, values, same)
    attended = mp_sum(dot_nn(context, weight_out)) + bias_out
    hidden, unit_one, scale_one = normalize(inputs + attended, gain[0], shift[0])
    low_hidden = hidden.astype(bf16)
    pre_act = dot_nn(low_hidden, weight_up) + bias_up
    low_act = jax.nn.gelu(pre_act, approximate=False).astype(bf16)
    mixed = mp_sum(dot_nn(low_act, weight_down)) + bias_down
    result, unit_two, scale_two = normalize(hidden + mixed, gain[1], shift[1])
    saved = (
        low_all,
        query,
        keys,
        values,
        log_total,
        context,
        unit_one,
        scale_one,
        low_hidden,
        pre_act,
        low_act,
        unit_two,
        scale_two,
    )
    return (result, saved)


def layer_backward(grad_flat, saved, same, params, orders):
    (
        weight_qkv,
        bias_qv,
        weight_out,
        bias_out,
        gain,
        shift,
        weight_up,
        bias_up,
        weight_down,
        bias_down,
    ) = params
    (
        low_all,
        query,
        keys,
        values,
        log_total,
        context,
        unit_one,
        scale_one,
        low_hidden,
        pre_act,
        low_act,
        unit_two,
        scale_two,
    ) = saved
    span = grad_flat.shape[0]
    grad_mixed, gain_two, shift_two = normalize_back(grad_flat, unit_two, scale_two, gain[1])
    grad_bias_down = jnp.sum(grad_mixed, axis=0)
    low_mixed = grad_mixed.astype(bf16)
    down_sum = reduce_bundle(dot_tn(low_mixed, low_act).astype(bf16), orders[0])
    grad_act = dot_nt(low_mixed, weight_down)
    normal_cdf = 0.5 * (1.0 + lax.erf(pre_act * root_half))
    density = jnp.exp(-0.5 * pre_act * pre_act) * inv_root_tau
    low_pre = (grad_act * (normal_cdf + pre_act * density)).astype(bf16)
    grad_bias_up = jnp.sum(low_pre.astype(f32), axis=0)
    up_sum = reduce_bundle(dot_tn(low_hidden, low_pre).astype(bf16), orders[1])
    grad_hidden = grad_mixed + mp_sum(dot_nt(low_pre, weight_up))
    grad_attended, gain_one, shift_one = normalize_back(grad_hidden, unit_one, scale_one, gain[0])
    grad_bias_out = jnp.sum(grad_attended, axis=0)
    low_attended = grad_attended.astype(bf16)
    grad_context = dot_nt(low_attended, weight_out).astype(bf16)
    grad_query, grad_key, grad_value = attend_back(query, keys, values, same, log_total, grad_context)

    low_own = low_all[:span]
    attn_sum = reduce_bundle(
        jnp.concatenate(
            [
                dot_tn(low_own, grad_query).astype(bf16),
                dot_tn(low_all, grad_key).astype(bf16),
                dot_tn(low_all, grad_value).astype(bf16),
                dot_tn(low_attended, context).astype(bf16),
            ],
            axis=1,
        ),
        orders[2],
    )
    place = lax.axis_index("mp")
    back_kv = dot_nt(grad_key, weight_qkv[1]) + dot_nt(grad_value, weight_qkv[2])
    parts = back_kv.shape[0] // span
    back_kv = back_kv.reshape(parts, 2, span // 2, back_kv.shape[1])
    back_own = back_kv[0] + dot_nt(grad_query, weight_qkv[0]).reshape(back_kv.shape[1:])

    def half_sum(value):
        send = pick(value, 1 - place, 0).astype(bf16)
        return pick(value, place, 0).astype(bf16).astype(f32) + swap(send, "mp", 1).astype(f32)

    total_half = half_sum(back_own)
    for j in range(1, parts):
        total_half = total_half + swap(half_sum(back_kv[j]).astype(bf16), "seq", 2 * j).astype(f32)
    back_total = share_halves(total_half.astype(bf16))
    grad_inputs = grad_attended + back_total.astype(f32)
    small = jnp.stack(
        [
            jnp.concatenate(
                [jnp.sum(grad_query.astype(f32), axis=0), jnp.sum(grad_value.astype(f32), axis=0)]
            ),
            grad_bias_out,
            gain_one,
            gain_two,
            shift_one,
            shift_two,
            grad_bias_up[: grad_bias_up.shape[0] // 2],
            grad_bias_up[grad_bias_up.shape[0] // 2 :],
            grad_bias_down,
        ]
    )
    return (grad_inputs, small, (attn_sum, up_sum, down_sum))


def layer_part(index, params):
    return tuple((array[index] for array in params))


def stack_pair(first_part, second_part):
    return jnp.stack([first_part, second_part])


def local(
    tokens,
    segments,
    dropped,
    qkv_weight,
    qv_bias,
    out_weight,
    out_bias,
    norm_gain,
    norm_shift,
    up_weight,
    up_bias,
    down_weight,
    down_bias,
    cotangent,
):
    params = (
        qkv_weight,
        qv_bias,
        out_weight,
        out_bias,
        norm_gain,
        norm_shift,
        up_weight,
        up_bias,
        down_weight,
        down_bias,
    )
    first = layer_part(0, params)
    second = layer_part(1, params)
    rows_here, span, width = tokens.shape
    assert rows_here == 2
    places = lax.axis_size("seq")
    place = lax.axis_index("seq")
    row = place & 1
    tokens_mine = pick(tokens, row, 0)
    tokens_partner = pick(tokens, 1 - row, 0)
    chunks = [tokens_mine]
    for c in range(1, places):
        chunks.append(from_far(tokens_mine if c % 2 == 0 else tokens_partner, c))
    low_own = jnp.concatenate(chunks[:2], axis=0)
    low_others = [jnp.concatenate(chunks[c : c + 2], axis=0) for c in range(2, places, 2)]
    seg_row = pick(segments, row, 0).reshape(places, span)
    for bit in range(bits_of("seq")):
        shaped = seg_row.reshape(places >> (bit + 1), 2, 1 << bit, span)
        seg_row = jnp.where(place_bit("seq", bit) == 1, shaped[:, ::-1], shaped).reshape(places, span)
    seg_keys = seg_row.reshape(places * span)
    same = seg_keys[: 2 * span, None] == seg_keys[None, :]
    cot_mine = pick(cotangent, row, 0)
    cot_far = from_far(pick(cotangent, 1 - row, 0), 1)
    cot_float = jnp.concatenate([cot_mine, cot_far], axis=0).astype(f32)
    kept = lax.dynamic_index_in_dim(dropped, lax.axis_index("dp") * rows_here + row, 0, keepdims=False) == 0

    hidden_one, saved_one = layer_forward(low_own.astype(f32), low_own, low_others, same, first)
    low_one = hidden_one.astype(bf16)
    others_one = [from_far(low_one, c) for c in range(2, places, 2)]
    result_two, saved_two = layer_forward(hidden_one, low_one, others_one, same, second)
    result = jnp.where(kept, result_two, hidden_one)

    def send_back(value):
        mine, partner = value[:span], value[span:].astype(bf16)
        arrived = from_far(partner, 1).astype(f32)
        return jnp.where(row == 0, jnp.stack([mine, arrived]), jnp.stack([arrived, mine]))

    outputs = send_back(result)
    grad_two = jnp.where(kept, cot_float, 0.0)
    up_down = list(range(bits_of("seq")))
    down_up = up_down[::-1]
    grad_in_two, small_two, big_two = layer_backward(
        grad_two, saved_two, same, second, (up_down, down_up, up_down)
    )
    grad_hidden_one = jnp.where(kept, grad_in_two, cot_float)
    grad_tokens, small_one, big_one = layer_backward(
        grad_hidden_one, saved_one, same, first, (down_up, up_down, down_up)
    )
    tokens_grad = send_back(grad_tokens)
    small = sum_everywhere(jnp.stack([small_one, small_two]))
    halves = width // 2
    qv_sum = small[:, 0].reshape(2, 2, halves)
    out_bias_sum = small[:, 1]
    gain_sum, shift_sum = small[:, 2:4], small[:, 4:6]
    up_bias_sum = small[:, 6:8].reshape(2, 2 * width)
    down_bias_sum = small[:, 8]

    def attn_parts(total):
        quarter = total.shape[1] // 4
        pieces = [total[:, i * quarter : (i + 1) * quarter].astype(f32) for i in range(4)]
        return jnp.stack(pieces[:3]), pieces[3].T

    qkv_sum, out_sum = jax.tree.map(stack_pair, attn_parts(big_one[0]), attn_parts(big_two[0]))
    up_sum = jnp.stack([big_one[1].astype(f32), big_two[1].astype(f32)])
    down_sum = jnp.stack([big_one[2].astype(f32).T, big_two[2].astype(f32).T])
    return (
        outputs,
        tokens_grad,
        qkv_sum,
        qv_sum,
        out_sum,
        out_bias_sum,
        gain_sum,
        shift_sum,
        up_sum,
        up_bias_sum,
        down_sum,
        down_bias_sum,
    )


def solution(mesh):
    placed = (
        P("dp", "seq", None),
        P("dp", None),
        P(),
        P(None, None, None, "mp"),
        P(None, None, "mp"),
        P(None, "mp", None),
        P(),
        P(),
        P(),
        P(None, None, "mp"),
        P(None, "mp"),
        P(None, "mp", None),
        P(),
        P("dp", "seq", None),
    )
    return jax.shard_map(
        local,
        mesh=mesh,
        in_specs=placed,
        out_specs=(
            P("dp", "seq", None),
            P("dp", "seq", None),
            P(None, None, "dp", "mp"),
            P(None, None, "mp"),
            P(None, "mp", "dp"),
            P(),
            P(),
            P(),
            P(None, "dp", "mp"),
            P(None, "mp"),
            P(None, "mp", "dp"),
            P(),
        ),
        check_vma=False,
    )
```

```python
import functools

import jax
import jax.numpy as jnp
from jax import lax
from jax.experimental import pallas as pl
from jax.experimental.pallas import tpu as pltpu
from jax.sharding import PartitionSpec as P

HEAD = 64
PAIR = 2 * HEAD
SEGMENTS = 4
FAR = 1e30
eps_norm = 1e-05
root_half = 0.7071067811865476
inv_root_tau = 0.3989422804014327
scale_two = 0.125 * 1.4426950408889634
f32 = jnp.float32
bf16 = jnp.bfloat16
smem = pl.BlockSpec(memory_space=pltpu.SMEM)


def dot_nn(left, right):
    return lax.dot_general(left, right, (((1,), (0,)), ((), ())), preferred_element_type=f32)


def dot_nt(left, right):
    return lax.dot_general(left, right, (((1,), (1,)), ((), ())), preferred_element_type=f32)


def dot_tn(left, right):
    return lax.dot_general(left, right, (((0,), (0,)), ((), ())), preferred_element_type=f32)


def swap(value, axis, mask):
    count = lax.axis_size(axis)
    return lax.ppermute(value, axis, [(i, i ^ mask) for i in range(count)])


def place_bit(axis, bit):
    return (lax.axis_index(axis) >> bit) & 1


def bits_of(axis):
    count = lax.axis_size(axis)
    number = count.bit_length() - 1
    assert 1 << number == count
    return number


def pick(value, index, axis):
    return lax.dynamic_index_in_dim(value, index, axis, keepdims=False)


def add_low(left, right):
    return (left.astype(f32) + right.astype(f32)).astype(bf16)


def call(kernel, name, ins, outs, grid=(), scratch=(), flops=0):
    def spec(shape, block, index):
        if block == "smem":
            return smem
        if block is None:
            return pl.BlockSpec(shape, lambda *g: (0,) * len(shape))
        return pl.BlockSpec(block, index)

    moved = sum(a.size * a.dtype.itemsize for a, _, _ in ins)
    moved += sum(s.size * s.dtype.itemsize for s, _, _ in outs)
    return pl.pallas_call(
        kernel,
        grid=grid,
        in_specs=[spec(a.shape, b, i) for a, b, i in ins],
        out_specs=[spec(s.shape, b, i) for s, b, i in outs],
        out_shape=[s for s, _, _ in outs],
        scratch_shapes=list(scratch),
        name=name,
        cost_estimate=pl.CostEstimate(flops=flops, bytes_accessed=moved, transcendentals=0),
        compiler_params=pltpu.CompilerParams(vmem_limit_bytes=40 << 20),
    )(*[a for a, _, _ in ins])


def like(shape, dtype):
    return jax.ShapeDtypeStruct(shape, dtype)


def head_lanes(side):
    lane = lax.broadcasted_iota(jnp.int32, (1, PAIR), 1)
    return lane < HEAD if side == 0 else lane >= HEAD


def attend_kernel(q_ref, k_ref, v_ref, qaug_ref, kaug_ref, context_ref, log_ref, vt_ref):
    @pl.when(pl.program_id(1) == 0)
    def _():
        vt_ref[...] = v_ref[...].T

    query, keys = q_ref[...], k_ref[...]
    outs = []
    for side in range(2):
        inside = head_lanes(side)
        scores = dot_nt(
            jnp.where(inside, keys, kaug_ref[...]), jnp.where(inside, query, qaug_ref[...])
        )
        peak = jnp.max(scores, axis=0, keepdims=True) * scale_two
        raised = jnp.exp2(scores * scale_two - peak)
        total = jnp.sum(raised, axis=0, keepdims=True)
        mixed = dot_nn(vt_ref[side * HEAD : (side + 1) * HEAD, :], raised.astype(bf16))
        outs.append(mixed / total)
        log_ref[0, side : side + 1, :] = peak + jnp.log2(total)
    context_ref[...] = jnp.concatenate(outs, axis=0).T.astype(bf16)


def attend(query, keys, values, qaug, kaug):
    count, width = query.shape
    full = keys.shape[0]
    pairs = width // PAIR
    tile = min(count, 512)
    own = (tile, PAIR), lambda p, i: (i, p)
    every = (full, PAIR), lambda p, i: (0, p)
    return call(
        attend_kernel,
        "attend",
        [
            (query, *own),
            (keys, *every),
            (values, *every),
            (qaug, (tile, PAIR), lambda p, i: (i, 0)),
            (kaug, None, None),
        ],
        [
            (like(query.shape, bf16), *own),
            (like((pairs, 2, count), f32), (1, 2, tile), lambda p, i: (p, 0, i)),
        ],
        grid=(pairs, count // tile),
        scratch=[pltpu.VMEM((PAIR, full), bf16)],
        flops=8 * count * full * width,
    )


def attend_back_kernel(
    q_ref,
    k_ref,
    v_ref,
    qaug_ref,
    kaug_ref,
    log_ref,
    context_ref,
    grad_ref,
    dq_ref,
    dk_ref,
    dv_ref,
    kt_ref,
    dk_sum,
    dv_sum,
):
    step = pl.program_id(1)

    @pl.when(step == 0)
    def _():
        kt_ref[...] = k_ref[...].T
        dk_sum[...] = jnp.zeros_like(dk_sum)
        dv_sum[...] = jnp.zeros_like(dv_sum)

    query, keys, grad = q_ref[...], k_ref[...], grad_ref[...]
    zero = jnp.zeros((), bf16)
    product = (grad.astype(f32) * context_ref[...].astype(f32)).T
    outs = []
    for side in range(2):
        inside = head_lanes(side)
        scores = dot_nt(
            jnp.where(inside, keys, kaug_ref[...]), jnp.where(inside, query, qaug_ref[...])
        )
        chance = jnp.exp2(scores * scale_two - log_ref[0, side : side + 1, :])
        grad_side = jnp.where(inside, grad, zero)
        inner = jnp.sum(product[side * HEAD : (side + 1) * HEAD], axis=0, keepdims=True)
        grad_chance = dot_nt(v_ref[...], grad_side)
        grad_scores = (chance * (grad_chance - inner)).astype(bf16)
        dv_sum[...] += dot_nn(chance.astype(bf16), grad_side)
        dk_sum[...] += dot_nn(grad_scores, jnp.where(inside, query, zero))
        outs.append(dot_nn(kt_ref[side * HEAD : (side + 1) * HEAD, :], grad_scores))
    dq_ref[...] = (jnp.concatenate(outs, axis=0) * 0.125).T.astype(bf16)

    @pl.when(step == pl.num_programs(1) - 1)
    def _():
        dk_ref[...] = (dk_sum[...] * 0.125).astype(bf16)
        dv_ref[...] = dv_sum[...].astype(bf16)


def attend_back(query, keys, values, qaug, kaug, log_total, context, grad_context):
    count, width = query.shape
    full = keys.shape[0]
    pairs = width // PAIR
    tile = min(count, 512)
    own = (tile, PAIR), lambda p, i: (i, p)
    every = (full, PAIR), lambda p, i: (0, p)
    return call(
        attend_back_kernel,
        "attend_back",
        [
            (query, *own),
            (keys, *every),
            (values, *every),
            (qaug, (tile, PAIR), lambda p, i: (i, 0)),
            (kaug, None, None),
            (log_total, (1, 2, tile), lambda p, i: (p, 0, i)),
            (context, *own),
            (grad_context, *own),
        ],
        [
            (like(query.shape, bf16), *own),
            (like(keys.shape, bf16), *every),
            (like(keys.shape, bf16), *every),
        ],
        grid=(pairs, count // tile),
        scratch=[
            pltpu.VMEM((PAIR, full), bf16),
            pltpu.VMEM((full, PAIR), f32),
            pltpu.VMEM((full, PAIR), f32),
        ],
        flops=20 * count * full * width,
    )


def normalize(rows_in, gain, shift):
    center = rows_in - jnp.mean(rows_in, axis=-1, keepdims=True)
    scale = lax.rsqrt(jnp.mean(center * center, axis=-1, keepdims=True) + eps_norm)
    unit = center * scale
    return (unit * gain + shift, unit, scale)


def normalize_back(grad_out, unit, scale, gain):
    grad_unit = grad_out * gain
    inner = (
        grad_unit
        - jnp.mean(grad_unit, axis=-1, keepdims=True)
        - unit * jnp.mean(grad_unit * unit, axis=-1, keepdims=True)
    )
    return inner * scale


def rows(tile, width):
    return (tile, width), lambda i: (i, 0)


def feed_kernel(
    in_ref,
    mine_ref,
    theirs_ref,
    bias_ref,
    gain_ref,
    shift_ref,
    up_ref,
    up_bias_ref,
    down_ref,
    hidden_ref,
    low_ref,
    unit_ref,
    scale_ref,
    active_ref,
    slope_ref,
    part_ref,
):
    summed = mine_ref[...].astype(f32) + theirs_ref[...].astype(f32)
    total = in_ref[...].astype(f32) + (summed + bias_ref[...])
    hidden, unit, scale = normalize(total, gain_ref[...], shift_ref[...])
    low = hidden.astype(bf16)
    hidden_ref[...] = hidden
    low_ref[...] = low
    unit_ref[...] = unit.astype(bf16)
    scale_ref[...] = jnp.broadcast_to(scale, scale_ref.shape)
    pre = dot_nn(low, up_ref[...]) + up_bias_ref[...]
    below = 0.5 * (1.0 + lax.erf(pre * root_half))
    active = (pre * below).astype(bf16)
    active_ref[...] = active
    slope_ref[...] = (below + pre * (jnp.exp(-0.5 * pre * pre) * inv_root_tau)).astype(bf16)
    part_ref[...] = dot_nn(active, down_ref[...]).astype(bf16)


def feed(inputs, mine, theirs, bias, gain, shift, up, up_bias, down):
    count, width = inputs.shape
    units = up.shape[1]
    tile = min(count, 256)
    wide, narrow = rows(tile, units), rows(tile, width)
    return call(
        feed_kernel,
        "feed",
        [(inputs, *narrow), (mine, *narrow), (theirs, *narrow)]
        + [(a, None, None) for a in (bias, gain, shift, up, up_bias, down)],
        [
            (like((count, width), f32), *narrow),
            (like((count, width), bf16), *narrow),
            (like((count, width), bf16), *narrow),
            (like((count, 128), f32), *rows(tile, 128)),
            (like((count, units), bf16), *wide),
            (like((count, units), bf16), *wide),
            (like((count, width), bf16), *narrow),
        ],
        grid=(count // tile,),
        flops=4 * count * width * units,
    )


def close_kernel(
    in_ref, mine_ref, theirs_ref, bias_ref, gain_ref, shift_ref, out_ref, low_ref, unit_ref, scale_ref
):
    summed = mine_ref[...].astype(f32) + theirs_ref[...].astype(f32)
    total = in_ref[...] + (summed + bias_ref[...])
    result, unit, scale = normalize(total, gain_ref[...], shift_ref[...])
    out_ref[...] = result
    low_ref[...] = result.astype(bf16)
    unit_ref[...] = unit.astype(bf16)
    scale_ref[...] = jnp.broadcast_to(scale, scale_ref.shape)


def close(inputs, mine, theirs, bias, gain, shift):
    count, width = inputs.shape
    tile = min(count, 256)
    narrow = rows(tile, width)
    return call(
        close_kernel,
        "close",
        [(inputs, *narrow), (mine, *narrow), (theirs, *narrow)]
        + [(a, None, None) for a in (bias, gain, shift)],
        [
            (like((count, width), f32), *narrow),
            (like((count, width), bf16), *narrow),
            (like((count, width), bf16), *narrow),
            (like((count, 128), f32), *rows(tile, 128)),
        ],
        grid=(count // tile,),
        flops=10 * count * width,
    )


def feed_back_kernel(has_base, flag_ref, *refs):
    if has_base:
        base_ref, mine_ref, theirs_ref, refs = refs[0], refs[1], refs[2], refs[3:]
    (
        cot_ref,
        unit_ref,
        scale_ref,
        gain_ref,
        down_ref,
        slope_ref,
        up_ref,
        mixed_ref,
        low_mixed_ref,
        low_pre_ref,
        part_ref,
        small_ref,
    ) = refs
    step = pl.program_id(0)
    kept = flag_ref[0] > 0
    cot = cot_ref[...].astype(f32)
    if has_base:
        here = flag_ref[1] == step
        back = jnp.where(here, mine_ref[...], theirs_ref[...]).astype(f32)
        grad_out = jnp.where(kept, base_ref[...] + back, cot)
    else:
        grad_out = jnp.where(kept, cot, 0.0)
    unit = unit_ref[...].astype(f32)
    grad_mixed = normalize_back(grad_out, unit, scale_ref[:, :1], gain_ref[...])
    mixed_ref[...] = grad_mixed
    low_mixed = grad_mixed.astype(bf16)
    low_mixed_ref[...] = low_mixed
    grad_active = dot_nt(low_mixed, down_ref[...])
    low_pre = (grad_active * slope_ref[...].astype(f32)).astype(bf16)
    low_pre_ref[...] = low_pre
    part_ref[...] = dot_nt(low_pre, up_ref[...]).astype(bf16)

    @pl.when(step == 0)
    def _():
        small_ref[...] = jnp.zeros_like(small_ref)

    width = grad_out.shape[1]

    def total(value):
        return jnp.sum(value, axis=0, keepdims=True)

    pre_sum = total(low_pre.astype(f32))
    small_ref[0:1, :] += total(grad_out * unit)
    small_ref[1:2, :] += total(grad_out)
    small_ref[2:3, :] += total(grad_mixed)
    small_ref[3:4, :] += pre_sum[:, :width]
    small_ref[4:5, :] += pre_sum[:, width:]


def feed_back(flags, base, cot, unit, scale, gain, down, slope, up):
    count, width = cot.shape
    units = up.shape[1]
    tile = count // 2
    wide, narrow = rows(tile, units), rows(tile, width)
    ins = [(flags, "smem", None)]
    if base is not None:
        ins += [(base[0], *narrow), (base[1], None, None), (base[2], None, None)]
    ins += [
        (cot, *narrow),
        (unit, *narrow),
        (scale, *rows(tile, 128)),
        (gain, None, None),
        (down, None, None),
        (slope, *wide),
        (up, None, None),
    ]
    return call(
        functools.partial(feed_back_kernel, base is not None),
        "feed_back",
        ins,
        [
            (like((count, width), f32), *narrow),
            (like((count, width), bf16), *narrow),
            (like((count, units), bf16), *wide),
            (like((count, width), bf16), *narrow),
            (like((8, width), f32), None, None),
        ],
        grid=(2,),
        flops=4 * count * width * units,
    )


def middle_back_kernel(
    mixed_ref,
    mine_ref,
    theirs_ref,
    unit_ref,
    scale_ref,
    gain_ref,
    out_ref,
    attended_ref,
    low_ref,
    context_ref,
    small_ref,
):
    summed = mine_ref[...].astype(f32) + theirs_ref[...].astype(f32)
    grad_hidden = mixed_ref[...] + summed
    unit = unit_ref[...].astype(f32)
    grad = normalize_back(grad_hidden, unit, scale_ref[:, :1], gain_ref[...])
    attended_ref[...] = grad
    low = grad.astype(bf16)
    low_ref[...] = low
    context_ref[...] = dot_nt(low, out_ref[...]).astype(bf16)

    @pl.when(pl.program_id(0) == 0)
    def _():
        small_ref[...] = jnp.zeros_like(small_ref)

    small_ref[0:1, :] += jnp.sum(grad_hidden * unit, axis=0, keepdims=True)
    small_ref[1:2, :] += jnp.sum(grad_hidden, axis=0, keepdims=True)
    small_ref[2:3, :] += jnp.sum(grad, axis=0, keepdims=True)


def middle_back(mixed, mine, theirs, unit, scale, gain, out_weight):
    count, width = mixed.shape
    local_width = out_weight.shape[0]
    tile = min(count, 256)
    narrow = rows(tile, width)
    return call(
        middle_back_kernel,
        "middle_back",
        [
            (mixed, *narrow),
            (mine, *narrow),
            (theirs, *narrow),
            (unit, *narrow),
            (scale, *rows(tile, 128)),
            (gain, None, None),
            (out_weight, None, None),
        ],
        [
            (like((count, width), f32), *narrow),
            (like((count, width), bf16), *narrow),
            (like((count, local_width), bf16), *rows(tile, local_width)),
            (like((8, width), f32), None, None),
        ],
        grid=(count // tile,),
        flops=2 * count * width * local_width,
    )


def put_halves(flag, first, second, send_ref, keep_ref):
    first, second = first.astype(bf16), second.astype(bf16)
    send_ref[...] = jnp.where(flag > 0, first, second)
    keep_ref[...] = jnp.where(flag > 0, second, first)


def weight_kernel(flag_ref, left_ref, right_ref, send_ref, keep_ref):
    half = right_ref.shape[1] // 2
    left = left_ref[...]
    put_halves(
        flag_ref[0],
        dot_tn(left, right_ref[:, :half]),
        dot_tn(left, right_ref[:, half:]),
        send_ref,
        keep_ref,
    )


def weight_grad(flag, left, right):
    shape = (left.shape[1], right.shape[1] // 2)
    return call(
        weight_kernel,
        "weight_grad",
        [(flag, "smem", None), (left, None, None), (right, None, None)],
        [(like(shape, bf16), None, None)] * 2,
        flops=4 * left.shape[0] * shape[0] * shape[1],
    )


def weight_attn_kernel(
    flag_ref, low_ref, dq_ref, dk_ref, dv_ref, att_ref, ctx_ref, send_ref, keep_ref, small_ref
):
    low = low_ref[...]
    own = low[: dq_ref.shape[0]]
    first = [dot_tn(own, dq_ref[...]), dot_tn(low, dk_ref[...])]
    second = [dot_tn(low, dv_ref[...]), dot_tn(att_ref[...], ctx_ref[...])]
    put_halves(
        flag_ref[0],
        jnp.concatenate(first, axis=1),
        jnp.concatenate(second, axis=1),
        send_ref,
        keep_ref,
    )
    width = dq_ref.shape[1]
    small_ref[...] = jnp.zeros_like(small_ref)
    small_ref[0:1, :width] = jnp.sum(dq_ref[...].astype(f32), axis=0, keepdims=True)
    small_ref[0:1, width:] = jnp.sum(dv_ref[...].astype(f32), axis=0, keepdims=True)


def weight_attn(flag, low_all, grad_query, grad_key, grad_value, low_attended, context):
    width = low_all.shape[1]
    local_width = grad_query.shape[1]
    shape = (width, 2 * local_width)
    return call(
        weight_attn_kernel,
        "weight_attn",
        [(flag, "smem", None)]
        + [
            (a, None, None)
            for a in (low_all, grad_query, grad_key, grad_value, low_attended, context)
        ],
        [(like(shape, bf16), None, None)] * 2 + [(like((8, width), f32), None, None)],
        flops=4 * low_all.shape[0] * shape[0] * shape[1],
    )


def share_halves(half):
    other = swap(half, "mp", 1)
    first = lax.axis_index("mp") == 0
    return jnp.where(first, jnp.stack([half, other]), jnp.stack([other, half])).reshape(
        (2 * half.shape[0],) + half.shape[1:]
    )


def from_far(value, mask):
    count = value.shape[0] // 2
    mine = pick(value.reshape((2, count) + value.shape[1:]), lax.axis_index("mp"), 0)
    return share_halves(swap(mine, "seq", mask))


def send_half(halves, order):
    return halves[1], swap(halves[0], "seq", 1 << order[0])


def reduce_rest(keep, arrived, order):
    shares = lax.axis_size("dp")
    width = keep.shape[0] // shares
    keep = keep.reshape(shares, width, keep.shape[1])
    arrived = arrived.reshape(keep.shape)

    def part(value, side):
        return pick(value.reshape(value.shape[0] // 2, 2, width, value.shape[2]), side, 1)

    for bit in range(bits_of("dp")):
        mine = place_bit("dp", bit)
        send = add_low(part(keep, 1 - mine), part(arrived, 1 - mine))
        keep = add_low(part(keep, mine), part(arrived, mine))
        arrived = swap(send, "dp", 1 << bit)
    total = add_low(keep, arrived)[0]
    for bit in order[1:]:
        total = add_low(total, swap(total, "seq", 1 << bit))
    other = swap(total, "seq", 1 << order[0])
    first = place_bit("seq", order[0]) == 0
    return jnp.where(first, total, other), jnp.where(first, other, total)


def sum_everywhere(value):
    for axis in ("seq", "dp"):
        for bit in range(bits_of(axis)):
            value = value + swap(value, axis, 1 << bit)
    return value


def layer_forward(inputs, low_own, low_others, augs, params):
    (
        weight_qkv,
        bias_qv,
        weight_out,
        bias_out,
        gain,
        shift,
        weight_up,
        bias_up,
        weight_down,
        bias_down,
    ) = params
    low_all = jnp.concatenate([low_own] + low_others, axis=0)
    query = (dot_nn(low_own, weight_qkv[0]) + bias_qv[0]).astype(bf16)
    keys = dot_nn(low_all, weight_qkv[1]).astype(bf16)
    values = (dot_nn(low_all, weight_qkv[2]) + bias_qv[1]).astype(bf16)
    context, log_total = attend(query, keys, values, *augs)
    part = dot_nn(context, weight_out).astype(bf16)
    hidden, low_hidden, unit_one, scale_one, active, slope, part = feed(
        inputs,
        part,
        swap(part, "mp", 1),
        bias_out,
        gain[0],
        shift[0],
        weight_up,
        bias_up,
        weight_down,
    )
    result, low_result, unit_two, scale_two = close(
        hidden, part, swap(part, "mp", 1), bias_down, gain[1], shift[1]
    )
    saved = (
        low_all,
        query,
        keys,
        values,
        log_total,
        context,
        unit_one,
        scale_one,
        low_hidden,
        active,
        slope,
        unit_two,
        scale_two,
    )
    return (result, low_result, saved)


def layer_backward(flags, base, cot, saved, augs, params, orders):
    weight_qkv, _, weight_out, _, gain, _, weight_up, _, weight_down, _ = params
    (
        low_all,
        query,
        keys,
        values,
        log_total,
        context,
        unit_one,
        scale_one,
        low_hidden,
        active,
        slope,
        unit_two,
        scale_two,
    ) = saved
    span = query.shape[0]
    grad_mixed, low_mixed, low_pre, part, small_feed = feed_back(
        flags, base, cot, unit_two, scale_two, gain[1], weight_down, slope, weight_up
    )

    def keeps(order):
        return place_bit("seq", order[0]).reshape(1)

    down = send_half(weight_grad(keeps(orders[0]), low_mixed, active), orders[0])
    up = send_half(weight_grad(keeps(orders[1]), low_hidden, low_pre), orders[1])
    grad_attended, low_attended, grad_context, small_middle = middle_back(
        grad_mixed, part, swap(part, "mp", 1), unit_one, scale_one, gain[0], weight_out
    )
    grad_query, grad_key, grad_value = attend_back(
        query, keys, values, *augs, log_total, context, grad_context
    )
    place = lax.axis_index("mp")
    back_kv = dot_nt(grad_key, weight_qkv[1]) + dot_nt(grad_value, weight_qkv[2])
    parts = back_kv.shape[0] // span
    back_kv = back_kv.reshape(parts, 2, span // 2, back_kv.shape[1])
    back_own = back_kv[0] + dot_nt(grad_query, weight_qkv[0]).reshape(back_kv.shape[1:])

    def half_sum(value):
        send = pick(value, 1 - place, 0).astype(bf16)
        return pick(value, place, 0).astype(bf16).astype(f32) + swap(send, "mp", 1).astype(f32)

    total_half = half_sum(back_own)
    for j in range(1, parts):
        total_half = total_half + swap(half_sum(back_kv[j]).astype(bf16), "seq", 2 * j).astype(f32)
    total_half = total_half.astype(bf16)
    send, keep, small_attn = weight_attn(
        keeps(orders[2]), low_all, grad_query, grad_key, grad_value, low_attended, context
    )
    attn = send_half((send, keep), orders[2])
    small = jnp.stack(
        [
            small_attn[0],
            small_middle[2],
            small_middle[0],
            small_feed[0],
            small_middle[1],
            small_feed[1],
            small_feed[3],
            small_feed[4],
            small_feed[2],
        ]
    )
    back = (grad_attended, total_half, swap(total_half, "mp", 1))
    sums = [reduce_rest(*bundle, order) for bundle, order in zip((down, up, attn), orders)]
    return (back, small, sums)


def layer_part(index, params):
    parts = [array[index] for array in params]
    for i in (3, 7, 9):
        parts[i] = parts[i].reshape(1, -1)
    for i in (4, 5):
        parts[i] = parts[i][:, None, :]
    return tuple(parts)


def stack_pair(first_part, second_part):
    return jnp.stack([first_part, second_part])


def local(
    tokens,
    segments,
    dropped,
    qkv_weight,
    qv_bias,
    out_weight,
    out_bias,
    norm_gain,
    norm_shift,
    up_weight,
    up_bias,
    down_weight,
    down_bias,
    cotangent,
):
    params = (
        qkv_weight,
        qv_bias,
        out_weight,
        out_bias,
        norm_gain,
        norm_shift,
        up_weight,
        up_bias,
        down_weight,
        down_bias,
    )
    first = layer_part(0, params)
    second = layer_part(1, params)
    rows_here, span, width = tokens.shape
    assert rows_here == 2
    places = lax.axis_size("seq")
    place = lax.axis_index("seq")
    row = place & 1
    tokens_mine = pick(tokens, row, 0)
    tokens_partner = pick(tokens, 1 - row, 0)
    chunks = [tokens_mine]
    for c in range(1, places):
        chunks.append(from_far(tokens_mine if c % 2 == 0 else tokens_partner, c))
    low_own = jnp.concatenate(chunks[:2], axis=0)
    low_others = [jnp.concatenate(chunks[c : c + 2], axis=0) for c in range(2, places, 2)]
    seg_row = pick(segments, row, 0).reshape(places, span)
    for bit in range(bits_of("seq")):
        shaped = seg_row.reshape(places >> (bit + 1), 2, 1 << bit, span)
        seg_row = jnp.where(place_bit("seq", bit) == 1, shaped[:, ::-1], shaped).reshape(places, span)
    seg_keys = seg_row.reshape(places * span, 1)
    lane = lax.broadcasted_iota(jnp.int32, (1, PAIR), 1) % HEAD
    used = lane < SEGMENTS
    kaug = jnp.where(used & (seg_keys != lane), 1.0, 0.0).astype(bf16)
    qaug = jnp.where(used & (seg_keys[: 2 * span] == lane), -FAR, 0.0).astype(bf16)
    augs = (qaug, kaug)
    cot_mine = pick(cotangent, row, 0)
    cot_far = from_far(pick(cotangent, 1 - row, 0), 1)
    cot = jnp.concatenate([cot_mine, cot_far], axis=0)
    kept = 1 - pick(dropped, lax.axis_index("dp") * rows_here + row, 0)
    flags = jnp.stack([kept, lax.axis_index("mp")])

    hidden_one, low_one, saved_one = layer_forward(low_own, low_own, low_others, augs, first)
    others_one = [from_far(low_one, c) for c in range(2, places, 2)]
    result_two, _, saved_two = layer_forward(hidden_one, low_one, others_one, augs, second)
    result = jnp.where(kept > 0, result_two, hidden_one)

    def send_back(value):
        mine, partner = value[:span], value[span:].astype(bf16)
        arrived = from_far(partner, 1).astype(f32)
        return jnp.where(row == 0, jnp.stack([mine, arrived]), jnp.stack([arrived, mine]))

    outputs = send_back(result)
    up_down = list(range(bits_of("seq")))
    down_up = up_down[::-1]
    back_two, small_two, big_two = layer_backward(
        flags, None, cot, saved_two, augs, second, (up_down, down_up, up_down)
    )
    back_one, small_one, big_one = layer_backward(
        flags, back_two, cot, saved_one, augs, first, (down_up, up_down, down_up)
    )
    base, own_half, other_half = back_one
    first_core = lax.axis_index("mp") == 0
    grad_tokens = base + jnp.where(
        first_core,
        jnp.concatenate([own_half, other_half]),
        jnp.concatenate([other_half, own_half]),
    ).astype(f32)
    tokens_grad = send_back(grad_tokens)
    small = sum_everywhere(jnp.stack([small_one, small_two]))
    halves = width // 2
    qv_sum = small[:, 0].reshape(2, 2, halves)
    out_bias_sum = small[:, 1]
    gain_sum, shift_sum = small[:, 2:4], small[:, 4:6]
    up_bias_sum = small[:, 6:8].reshape(2, 2 * width)
    down_bias_sum = small[:, 8]

    def down_part(pieces):
        return jnp.concatenate([piece.astype(f32).T for piece in pieces], axis=0)

    def up_part(pieces):
        return jnp.concatenate(pieces, axis=1).astype(f32)

    def attn_parts(pieces):
        half = pieces[0].shape[1] // 2
        query, key = pieces[0][:, :half], pieces[0][:, half:]
        value, out = pieces[1][:, :half], pieces[1][:, half:]
        return jnp.stack([query, key, value]).astype(f32), out.astype(f32).T

    down_sum = stack_pair(down_part(big_one[0]), down_part(big_two[0]))
    up_sum = stack_pair(up_part(big_one[1]), up_part(big_two[1]))
    qkv_sum, out_sum = jax.tree.map(stack_pair, attn_parts(big_one[2]), attn_parts(big_two[2]))
    return (
        outputs,
        tokens_grad,
        qkv_sum,
        qv_sum,
        out_sum,
        out_bias_sum,
        gain_sum,
        shift_sum,
        up_sum,
        up_bias_sum,
        down_sum,
        down_bias_sum,
    )


def solution(mesh):
    placed = (
        P("dp", "seq", None),
        P("dp", None),
        P(),
        P(None, None, None, "mp"),
        P(None, None, "mp"),
        P(None, "mp", None),
        P(),
        P(),
        P(),
        P(None, None, "mp"),
        P(None, "mp"),
        P(None, "mp", None),
        P(),
        P("dp", "seq", None),
    )
    return jax.shard_map(
        local,
        mesh=mesh,
        in_specs=placed,
        out_specs=(
            P("dp", "seq", None),
            P("dp", "seq", None),
            P(None, None, "dp", "mp"),
            P(None, None, "mp"),
            P(None, "mp", "dp"),
            P(),
            P(),
            P(),
            P(None, "dp", "mp"),
            P(None, "mp"),
            P(None, "mp", "dp"),
            P(),
        ),
        check_vma=False,
    )
```

```python
import functools

import jax
import jax.numpy as jnp
from jax import lax
from jax.experimental import pallas as pl
from jax.experimental.pallas import tpu as pltpu
from jax.sharding import PartitionSpec as P

HEAD = 64
PAIR = 2 * HEAD
SEGMENTS = 4
FAR = 1e30
eps_norm = 1e-05
root_half = 0.7071067811865476
inv_root_tau = 0.3989422804014327
scale_two = 0.125 * 1.4426950408889634
f32 = jnp.float32
bf16 = jnp.bfloat16
ALPHA = 10 * 1.15e9
LIMITS = {'back': 12, 'sums': 8, 'adds': 8, 'share': 12, 'project': 4, 'attend': 10, 'feed': 14, 'close': 6, 'feed_back': 14, 'weight_grad': 10, 'middle_back': 8, 'attend_back': 14}
BUSY = dict(back=1.5, sums=1.0, adds=1.0, share=2.0, project=1.5, attend=7.0, feed=6.0, close=1.5, feed_back=6.0, weight_grad=1.4, middle_back=2.5, attend_back=9.5)
anywhere = pl.BlockSpec(memory_space=pl.ANY)
smem = pl.BlockSpec(memory_space=pltpu.SMEM)


def dot_nn(left, right):
    return lax.dot_general(left, right, (((1,), (0,)), ((), ())), preferred_element_type=f32)


def dot_nt(left, right):
    return lax.dot_general(left, right, (((1,), (1,)), ((), ())), preferred_element_type=f32)


def dot_tn(left, right):
    return lax.dot_general(left, right, (((0,), (0,)), ((), ())), preferred_element_type=f32)


def swap(value, axis, mask):
    count = lax.axis_size(axis)
    return lax.ppermute(value, axis, [(i, i ^ mask) for i in range(count)])


def place_bit(axis, bit):
    return (lax.axis_index(axis) >> bit) & 1


def bits_of(axis):
    count = lax.axis_size(axis)
    number = count.bit_length() - 1
    assert 1 << number == count
    return number


def pick(value, index, axis):
    return lax.dynamic_index_in_dim(value, index, axis, keepdims=False)


def add_low(left, right):
    return (left.astype(f32) + right.astype(f32)).astype(bf16)


def call(kernel, name, ins, outs, grid=(), scratch=(), after=()):
    def placed(shape):
        return pltpu.HBM(shape.shape, shape.dtype) if isinstance(shape, Saved) else shape

    def spec(shape, block, index):
        if block == "smem":
            return smem
        if block is None:
            return pl.BlockSpec(shape, lambda *g: (0,) * len(shape))
        return pl.BlockSpec(block, index)

    count = len(ins)

    def body(*refs):
        kernel(*refs[:count], *refs[count + len(after) :])

    return pl.pallas_call(
        body,
        grid=grid,
        in_specs=[spec(a.shape, b, i) for a, b, i in ins] + [anywhere] * len(after),
        out_specs=[spec(s.shape, b, i) for s, b, i in outs],
        out_shape=[placed(s) for s, _, _ in outs],
        scratch_shapes=list(scratch),
        name=name,
        cost_estimate=pl.CostEstimate(flops=int(ALPHA * BUSY[name]), bytes_accessed=0, transcendentals=0),
        compiler_params=pltpu.CompilerParams(vmem_limit_bytes=LIMITS[name] << 20),
    )(*[a for a, _, _ in ins], *after)


def like(shape, dtype):
    return jax.ShapeDtypeStruct(shape, dtype)


class Saved:
    def __init__(self, shape, dtype):
        self.shape, self.dtype = shape, dtype


def head_lanes(side):
    lane = lax.broadcasted_iota(jnp.int32, (1, PAIR), 1)
    return lane < HEAD if side == 0 else lane >= HEAD


def scores_of(inside, parts, query, qaug):
    probe = jnp.where(inside, query, qaug)
    return jnp.concatenate(
        [dot_nt(jnp.where(inside, k[...], aug[...]), probe) for k, aug in parts], axis=0
    )


def attend_kernel(
    q_ref, k_ref, k2_ref, v_ref, v2_ref, qaug_ref, kaug_ref, kaug2_ref, context_ref, log_ref, vt_ref
):
    own = v_ref.shape[0]

    @pl.when(pl.program_id(1) == 0)
    def _():
        vt_ref[:, :own] = v_ref[...].T
        vt_ref[:, own:] = v2_ref[...].T

    parts = ((k_ref, kaug_ref), (k2_ref, kaug2_ref))
    query = q_ref[...]
    outs = []
    for side in range(2):
        scores = scores_of(head_lanes(side), parts, query, qaug_ref[...])
        peak = jnp.max(scores, axis=0, keepdims=True) * scale_two
        raised = jnp.exp2(scores * scale_two - peak)
        total = jnp.sum(raised, axis=0, keepdims=True)
        mixed = dot_nn(vt_ref[side * HEAD : (side + 1) * HEAD, :], raised.astype(bf16))
        outs.append(mixed / total)
        log_ref[0, side : side + 1, :] = peak + jnp.log2(total)
    context_ref[...] = jnp.concatenate(outs, axis=0).T.astype(bf16)


def attention_specs(count, counts):
    tile = min(count, 512)
    own = (tile, PAIR), lambda p, i: (i, p)
    first, rest = [((n, PAIR), lambda p, i: (0, p)) for n in counts]
    logs = (1, 2, tile), lambda p, i: (p, 0, i)
    aug = (tile, PAIR), lambda p, i: (i, 0)
    return tile, own, first, rest, logs, aug


def attend(query, keys, values, augs):
    count, width = query.shape
    pairs = width // PAIR
    tile, own, first, rest, logs, aug = attention_specs(count, [k.shape[0] for k in keys])
    return call(
        attend_kernel,
        "attend",
        [
            (query, *own),
            (keys[0], *first),
            (keys[1], *rest),
            (values[0], *first),
            (values[1], *rest),
            (augs[0], *aug),
            (augs[1], None, None),
            (augs[2], None, None),
        ],
        [(like(query.shape, bf16), *own), (Saved((pairs, 2, count), f32), *logs)],
        grid=(pairs, count // tile),
        scratch=[pltpu.VMEM((PAIR, sum(k.shape[0] for k in keys)), bf16)],
    )


def attend_back_kernel(
    q_ref,
    k_ref,
    k2_ref,
    v_ref,
    v2_ref,
    qaug_ref,
    kaug_ref,
    kaug2_ref,
    log_ref,
    context_ref,
    grad_ref,
    dq_ref,
    dk_ref,
    dk2_ref,
    dv_ref,
    dv2_ref,
    kt_ref,
    dk_sum,
    dv_sum,
):
    step = pl.program_id(1)
    own = k_ref.shape[0]

    @pl.when(step == 0)
    def _():
        kt_ref[:, :own] = k_ref[...].T
        kt_ref[:, own:] = k2_ref[...].T
        dk_sum[...] = jnp.zeros_like(dk_sum)
        dv_sum[...] = jnp.zeros_like(dv_sum)

    parts = ((k_ref, kaug_ref), (k2_ref, kaug2_ref))
    query, grad = q_ref[...], grad_ref[...]
    zero = jnp.zeros((), bf16)
    product = (grad.astype(f32) * context_ref[...].astype(f32)).T
    outs = []
    for side in range(2):
        inside = head_lanes(side)
        scores = scores_of(inside, parts, query, qaug_ref[...])
        chance = jnp.exp2(scores * scale_two - log_ref[0, side : side + 1, :])
        grad_side = jnp.where(inside, grad, zero)
        inner = jnp.sum(product[side * HEAD : (side + 1) * HEAD], axis=0, keepdims=True)
        grad_chance = jnp.concatenate([dot_nt(v[...], grad_side) for v in (v_ref, v2_ref)], axis=0)
        grad_scores = (chance * (grad_chance - inner)).astype(bf16)
        dv_sum[...] += dot_nn(chance.astype(bf16), grad_side)
        dk_sum[...] += dot_nn(grad_scores, jnp.where(inside, query, zero))
        outs.append(dot_nn(kt_ref[side * HEAD : (side + 1) * HEAD, :], grad_scores))
    dq_ref[...] = (jnp.concatenate(outs, axis=0) * 0.125).T.astype(bf16)

    @pl.when(step == pl.num_programs(1) - 1)
    def _():
        dk_ref[...] = (dk_sum[:own] * 0.125).astype(bf16)
        dk2_ref[...] = (dk_sum[own:] * 0.125).astype(bf16)
        dv_ref[...] = dv_sum[:own].astype(bf16)
        dv2_ref[...] = dv_sum[own:].astype(bf16)


def attend_back(query, keys, values, augs, log_total, context, grad_context, after=()):
    count, width = query.shape
    full = sum(k.shape[0] for k in keys)
    pairs = width // PAIR
    tile, own, first, rest, logs, aug = attention_specs(count, [k.shape[0] for k in keys])
    return call(
        attend_back_kernel,
        "attend_back",
        [
            (query, *own),
            (keys[0], *first),
            (keys[1], *rest),
            (values[0], *first),
            (values[1], *rest),
            (augs[0], *aug),
            (augs[1], None, None),
            (augs[2], None, None),
            (log_total, *logs),
            (context, *own),
            (grad_context, *own),
        ],
        [
            (like(query.shape, bf16), *own),
            (like(keys[0].shape, bf16), *first),
            (like(keys[1].shape, bf16), *rest),
            (like(keys[0].shape, bf16), *first),
            (like(keys[1].shape, bf16), *rest),
        ],
        grid=(pairs, count // tile),
        scratch=[
            pltpu.VMEM((PAIR, full), bf16),
            pltpu.VMEM((full, PAIR), f32),
            pltpu.VMEM((full, PAIR), f32),
        ],
        after=after,
    )


def project_kernel(with_query, in_ref, weight_ref, bias_ref, *outs):
    low = in_ref[...]
    if with_query:
        outs[0][...] = (dot_nn(low, weight_ref[0]) + bias_ref[0]).astype(bf16)
        outs = outs[1:]
    outs[0][...] = dot_nn(low, weight_ref[1]).astype(bf16)
    outs[1][...] = (dot_nn(low, weight_ref[2]) + bias_ref[1]).astype(bf16)


def project(low, weight, bias, with_query):
    count, width = low.shape
    local_width = weight.shape[2]
    tile = min(count, 256)
    if count % tile:
        tile = count
    out = like((count, local_width), bf16), *rows(tile, local_width)
    return call(
        functools.partial(project_kernel, with_query),
        "project",
        [(low, *rows(tile, width)), (weight, None, None), (bias, None, None)],
        [out] * (3 if with_query else 2),
        grid=(count // tile,),
    )


def normalize(rows_in, gain, shift):
    center = rows_in - jnp.mean(rows_in, axis=-1, keepdims=True)
    scale = lax.rsqrt(jnp.mean(center * center, axis=-1, keepdims=True) + eps_norm)
    unit = center * scale
    return (unit * gain + shift, unit, scale)


def normalize_back(grad_out, unit, scale, gain):
    grad_unit = grad_out * gain
    inner = (
        grad_unit
        - jnp.mean(grad_unit, axis=-1, keepdims=True)
        - unit * jnp.mean(grad_unit * unit, axis=-1, keepdims=True)
    )
    return inner * scale


def rows(tile, width):
    return (tile, width), lambda i: (i, 0)


def feed_kernel(
    in_ref,
    mine_ref,
    theirs_ref,
    bias_ref,
    gain_ref,
    shift_ref,
    up_ref,
    up_bias_ref,
    down_ref,
    hidden_ref,
    low_ref,
    unit_ref,
    scale_ref,
    active_ref,
    slope_ref,
    part_ref,
):
    summed = mine_ref[...].astype(f32) + theirs_ref[...].astype(f32)
    total = in_ref[...].astype(f32) + (summed + bias_ref[...])
    hidden, unit, scale = normalize(total, gain_ref[...], shift_ref[...])
    low = hidden.astype(bf16)
    hidden_ref[...] = hidden
    low_ref[...] = low
    unit_ref[...] = unit.astype(bf16)
    scale_ref[...] = jnp.broadcast_to(scale, scale_ref.shape)
    pre = dot_nn(low, up_ref[...]) + up_bias_ref[...]
    below = 0.5 * (1.0 + lax.erf(pre * root_half))
    active = (pre * below).astype(bf16)
    active_ref[...] = active
    slope_ref[...] = (below + pre * (jnp.exp(-0.5 * pre * pre) * inv_root_tau)).astype(bf16)
    part_ref[...] = dot_nn(active, down_ref[...]).astype(bf16)


def feed(inputs, mine, theirs, bias, gain, shift, up, up_bias, down):
    count, width = inputs.shape
    units = up.shape[1]
    tile = min(count, 256)
    wide, narrow = rows(tile, units), rows(tile, width)
    return call(
        feed_kernel,
        "feed",
        [(inputs, *narrow), (mine, *narrow), (theirs, *narrow)]
        + [(a, None, None) for a in (bias, gain, shift, up, up_bias, down)],
        [
            (like((count, width), f32), *narrow),
            (Saved((count, width), bf16), *narrow),
            (Saved((count, width), bf16), *narrow),
            (Saved((count, 128), f32), *rows(tile, 128)),
            (Saved((count, units), bf16), *wide),
            (Saved((count, units), bf16), *wide),
            (like((count, width), bf16), *narrow),
        ],
        grid=(count // tile,),
    )


def close_kernel(
    in_ref, mine_ref, theirs_ref, bias_ref, gain_ref, shift_ref, out_ref, low_ref, unit_ref, scale_ref
):
    summed = mine_ref[...].astype(f32) + theirs_ref[...].astype(f32)
    total = in_ref[...] + (summed + bias_ref[...])
    result, unit, scale = normalize(total, gain_ref[...], shift_ref[...])
    out_ref[...] = result
    low_ref[...] = result.astype(bf16)
    unit_ref[...] = unit.astype(bf16)
    scale_ref[...] = jnp.broadcast_to(scale, scale_ref.shape)


def close(inputs, mine, theirs, bias, gain, shift):
    count, width = inputs.shape
    tile = min(count, 256)
    narrow = rows(tile, width)
    return call(
        close_kernel,
        "close",
        [(inputs, *narrow), (mine, *narrow), (theirs, *narrow)]
        + [(a, None, None) for a in (bias, gain, shift)],
        [
            (like((count, width), f32), *narrow),
            (like((count, width), bf16), *narrow),
            (like((count, width), bf16), *narrow),
            (like((count, 128), f32), *rows(tile, 128)),
        ],
        grid=(count // tile,),
    )


def feed_back_kernel(has_base, flag_ref, *refs):
    if has_base:
        base_ref, mine_ref, theirs_ref, refs = refs[0], refs[1], refs[2], refs[3:]
    (
        cot_ref,
        unit_ref,
        scale_ref,
        gain_ref,
        down_ref,
        slope_ref,
        up_ref,
        mixed_ref,
        low_mixed_ref,
        low_pre_ref,
        part_ref,
        small_ref,
    ) = refs
    step = pl.program_id(0)
    kept = flag_ref[0] > 0
    cot = cot_ref[...].astype(f32)
    if has_base:
        here = flag_ref[1] == step
        back = jnp.where(here, mine_ref[...], theirs_ref[...]).astype(f32)
        grad_out = jnp.where(kept, base_ref[...] + back, cot)
    else:
        grad_out = jnp.where(kept, cot, 0.0)
    unit = unit_ref[...].astype(f32)
    grad_mixed = normalize_back(grad_out, unit, scale_ref[:, :1], gain_ref[...])
    mixed_ref[...] = grad_mixed
    low_mixed = grad_mixed.astype(bf16)
    low_mixed_ref[...] = low_mixed
    grad_active = dot_nt(low_mixed, down_ref[...])
    low_pre = (grad_active * slope_ref[...].astype(f32)).astype(bf16)
    low_pre_ref[...] = low_pre
    part_ref[...] = dot_nt(low_pre, up_ref[...]).astype(bf16)

    @pl.when(step == 0)
    def _():
        small_ref[...] = jnp.zeros_like(small_ref)

    width = grad_out.shape[1]

    def total(value):
        return jnp.sum(value, axis=0, keepdims=True)

    pre_sum = total(low_pre.astype(f32))
    small_ref[0:1, :] += total(grad_out * unit)
    small_ref[1:2, :] += total(grad_out)
    small_ref[2:3, :] += total(grad_mixed)
    small_ref[3:4, :] += pre_sum[:, :width]
    small_ref[4:5, :] += pre_sum[:, width:]


def feed_back(flags, base, cot, unit, scale, gain, down, slope, up, after=()):
    count, width = cot.shape
    units = up.shape[1]
    tile = count // 2
    wide, narrow = rows(tile, units), rows(tile, width)
    ins = [(flags, "smem", None)]
    if base is not None:
        ins += [(base[0], *narrow), (base[1], None, None), (base[2], None, None)]
    ins += [
        (cot, *narrow),
        (unit, *narrow),
        (scale, *rows(tile, 128)),
        (gain, None, None),
        (down, None, None),
        (slope, *wide),
        (up, None, None),
    ]
    return call(
        functools.partial(feed_back_kernel, base is not None),
        "feed_back",
        ins,
        [
            (like((count, width), f32), *narrow),
            (like((count, width), bf16), *narrow),
            (like((count, units), bf16), *wide),
            (like((count, width), bf16), *narrow),
            (like((8, width), f32), None, None),
        ],
        grid=(2,),
        after=after,
    )


def middle_back_kernel(
    mixed_ref,
    mine_ref,
    theirs_ref,
    unit_ref,
    scale_ref,
    gain_ref,
    out_ref,
    attended_ref,
    low_ref,
    context_ref,
    small_ref,
):
    summed = mine_ref[...].astype(f32) + theirs_ref[...].astype(f32)
    grad_hidden = mixed_ref[...] + summed
    unit = unit_ref[...].astype(f32)
    grad = normalize_back(grad_hidden, unit, scale_ref[:, :1], gain_ref[...])
    attended_ref[...] = grad
    low = grad.astype(bf16)
    low_ref[...] = low
    context_ref[...] = dot_nt(low, out_ref[...]).astype(bf16)

    @pl.when(pl.program_id(0) == 0)
    def _():
        small_ref[...] = jnp.zeros_like(small_ref)

    small_ref[0:1, :] += jnp.sum(grad_hidden * unit, axis=0, keepdims=True)
    small_ref[1:2, :] += jnp.sum(grad_hidden, axis=0, keepdims=True)
    small_ref[2:3, :] += jnp.sum(grad, axis=0, keepdims=True)


def middle_back(mixed, mine, theirs, unit, scale, gain, out_weight, after=()):
    count, width = mixed.shape
    local_width = out_weight.shape[0]
    tile = min(count, 256)
    narrow = rows(tile, width)
    return call(
        middle_back_kernel,
        "middle_back",
        [
            (mixed, *narrow),
            (mine, *narrow),
            (theirs, *narrow),
            (unit, *narrow),
            (scale, *rows(tile, 128)),
            (gain, None, None),
            (out_weight, None, None),
        ],
        [
            (like((count, width), f32), *narrow),
            (like((count, width), bf16), *narrow),
            (like((count, local_width), bf16), *rows(tile, local_width)),
            (like((8, width), f32), None, None),
        ],
        grid=(count // tile,),
        after=after,
    )


def put_halves(flag, value, column, send_ref, keep_ref):
    shares, half = send_ref.shape[:2]
    columns = slice(column, column + value.shape[1])
    value = value.astype(bf16)
    for share in range(shares):
        low = value[2 * share * half : (2 * share + 1) * half]
        high = value[(2 * share + 1) * half : (2 * share + 2) * half]
        send_ref[share, :, columns] = jnp.where(flag > 0, low, high)
        keep_ref[share, :, columns] = jnp.where(flag > 0, high, low)


def weight_kernel(pairs, flag_ref, *refs):
    lefts_rights, (send_ref, keep_ref) = refs[:-2], refs[-2:]
    column = 0
    for terms in pairs:
        value = 0.0
        for left, right in terms:
            value = value + dot_tn(lefts_rights[left][...], lefts_rights[right][...])
        put_halves(flag_ref[0], value, column, send_ref, keep_ref)
        column += value.shape[1]


def weight_grad(flag, arrays, pairs, after=()):
    shares = lax.axis_size("dp")
    width = arrays[pairs[0][0][0]].shape[1]
    columns = sum(arrays[terms[0][1]].shape[1] for terms in pairs)
    shape = (shares, width // (2 * shares), columns)
    return call(
        functools.partial(weight_kernel, pairs),
        "weight_grad",
        [(flag, "smem", None)] + [(a, None, None) for a in arrays],
        [(like(shape, bf16), None, None)] * 2,
        after=after,
    )


def back_kernel(flag_ref, *refs):
    terms, (mine_ref, theirs_ref) = refs[:-2], refs[-2:]
    parts, half = mine_ref.shape[:2]
    grads = terms[: len(terms) // 2]
    weights = terms[len(terms) // 2 :]
    for part in range(parts):
        halves = []
        for side in range(2):
            start = (2 * part + side) * half
            value = 0.0
            for grad, weight in zip(grads, weights):
                value = value + dot_nt(grad[start : start + half], weight[0])
            halves.append(value.astype(bf16))
        mine_ref[part] = jnp.where(flag_ref[1] > 0, halves[1], halves[0])
        theirs_ref[part] = jnp.where(flag_ref[1] > 0, halves[0], halves[1])


def back_grad(flags, grads, weight, which, span, after=()):
    count, local_width = grads[0].shape
    width = weight.shape[1]
    out = like((count // span, span // 2, width), bf16), None, None
    return call(
        back_kernel,
        "back",
        [(flags, "smem", None)]
        + [(g, g.shape, lambda i: (0, 0)) for g in grads]
        + [(weight, (1, width, local_width), lambda i, w=w: (w, 0, 0)) for w in which],
        [out, out],
        grid=(1,),
        after=after,
    )


def sums_kernel(count, *refs):
    keeps, arrived, outs = refs[:count], refs[count : 2 * count], refs[2 * count :]
    for k in range(2):
        column = 0
        for keep, other in zip(keeps, arrived):
            columns = slice(column, column + keep.shape[-1])
            outs[k][:, columns] = add_low(keep[k, 0], other[k, 0])
            column += keep.shape[-1]


def sums(keeps, arrived, after=()):
    rows_, columns = keeps[0].shape[2], sum(k.shape[3] for k in keeps)
    out = like((rows_, columns), bf16), None, None
    return call(
        functools.partial(sums_kernel, len(keeps)),
        "sums",
        [(a, None, None) for a in (*keeps, *arrived)],
        [out, out],
        after=after,
    )


def adds_kernel(a_ref, b_ref, c_ref, d_ref, first_ref, second_ref):
    first_ref[...] = add_low(a_ref[...], b_ref[...])
    second_ref[...] = add_low(c_ref[...], d_ref[...])


def adds(first, second, after=()):
    out = like(first[0].shape, bf16), None, None
    return call(
        adds_kernel,
        "adds",
        [(a, None, None) for a in (*first, *second)],
        [out, out],
        after=after,
    )


class Order:
    def __init__(self):
        self.last = ()

    def mark(self, *values):
        self.last = values


def both_halves(mine, axis=0):
    other = swap(mine, "mp", 1)
    first = lax.axis_index("mp") == 0
    whole = jnp.where(
        first, jnp.stack([mine, other], axis=axis), jnp.stack([other, mine], axis=axis)
    )
    return whole.reshape(mine.shape[:axis] + (-1,) + mine.shape[axis + 1 :])


def my_half(value):
    count = value.shape[0] // 2
    return pick(value.reshape((2, count) + value.shape[1:]), lax.axis_index("mp"), 0)


def share_kernel(stacked, flag_ref, *refs):
    keeps, arrived, send_ref, keep_ref = refs[: len(refs) // 2 - 1], refs[len(refs) // 2 - 1 : -2], *refs[-2:]

    def part(group, bundle, side):
        return group[0][bundle, side] if stacked else group[bundle][side]

    for bundle in range(2):
        low, high = [
            add_low(part(keeps, bundle, side), part(arrived, bundle, side)) for side in range(2)
        ]
        send_ref[bundle, 0] = jnp.where(flag_ref[0] > 0, low, high)
        keep_ref[bundle, 0] = jnp.where(flag_ref[0] > 0, high, low)


def share_step(flag, keeps, arrived, after=()):
    stacked = len(keeps) == 1
    shares, half, columns = keeps[0].shape[-3:]
    block = (2, half, columns), lambda i: (i, 0, 0)
    if stacked:
        block = (2, 2, half, columns), lambda i: (0, i, 0, 0)
    out = like((2, shares // 2, half, columns), bf16), (2, 1, half, columns), lambda i: (0, i, 0, 0)
    return call(
        functools.partial(share_kernel, stacked),
        "share",
        [(flag, "smem", None)] + [(a, *block) for a in (*keeps, *arrived)],
        [out, out],
        grid=(shares // 2,),
        after=after,
    )


def last_bit():
    return bits_of("seq") - 1


class Pair:
    def __init__(self):
        self.keeps, self.arrived, self.bit = [], [], 0

    def start(self, line, arrays, pairs):
        bit = 0 if self.keeps else last_bit()
        flag = place_bit("seq", bit).reshape(1)
        send, keep = weight_grad(flag, arrays, pairs, line.last)
        line.mark(send)
        self.keeps.append(keep)
        self.arrived.append(swap(send, "seq", 1 << bit))

    def share(self, line):
        flag = place_bit("dp", self.bit).reshape(1)
        send, keep = share_step(flag, self.keeps, self.arrived, line.last)
        line.mark(send)
        self.keeps, self.arrived = [keep], [swap(send, "dp", 1 << self.bit)]
        self.bit += 1

    def shares(self, line):
        while self.bit < bits_of("dp"):
            self.share(line)


class Tail:
    def __init__(self, line, pairs):
        keeps, arrived = [p.keeps[0] for p in pairs], [p.arrived[0] for p in pairs]
        self.totals = sums(keeps, arrived, line.last)
        bits = list(range(bits_of("seq")))
        self.across = (bits[:-1], bits[1:])
        for place in range(len(bits) - 2):
            self.totals = [
                add_low(t, swap(t, "seq", 1 << across[place]))
                for t, across in zip(self.totals, self.across)
            ]
        line.mark(*self.totals)
        self.arrived = [
            swap(t, "seq", 1 << across[-1]) for t, across in zip(self.totals, self.across)
        ]

    def gather(self, line):
        first, second = zip(self.totals, self.arrived)
        self.totals = adds(first, second, line.last)
        line.mark(*self.totals)
        self.arrived = [swap(t, "seq", 1 << b) for t, b in zip(self.totals, (last_bit(), 0))]

    def finish(self):
        whole = []
        for total, other, bit in zip(self.totals, self.arrived, (last_bit(), 0)):
            first = place_bit("seq", bit) == 0
            whole.append(
                jnp.where(
                    first, jnp.concatenate([total, other]), jnp.concatenate([other, total])
                ).astype(f32)
            )
        return whole


class Layer:
    def __init__(self, params, augs):
        (
            self.weight_qkv,
            self.bias_qv,
            self.weight_out,
            self.bias_out,
            self.gain,
            self.shift,
            self.weight_up,
            self.bias_up,
            self.weight_down,
            self.bias_down,
        ) = params
        self.augs = augs

    def open(self, low_own):
        self.low_own = low_own
        self.query, self.key_own, self.value_own = project(
            low_own, self.weight_qkv, self.bias_qv, True
        )

    def forward(self, inputs, low_rest):
        self.low_rest = low_rest
        key_rest, value_rest = project(low_rest, self.weight_qkv, self.bias_qv, False)
        self.keys = (self.key_own, key_rest)
        self.values = (self.value_own, value_rest)
        self.context, self.log_total = attend(self.query, self.keys, self.values, self.augs)
        part = dot_nn(self.context, self.weight_out).astype(bf16)
        hidden, self.low_hidden, self.unit_one, self.scale_one, self.active, self.slope, part = feed(
            inputs,
            part,
            swap(part, "mp", 1),
            self.bias_out,
            self.gain[0],
            self.shift[0],
            self.weight_up,
            self.bias_up,
            self.weight_down,
        )
        result, low_result, self.unit_two, self.scale_two = close(
            hidden, part, swap(part, "mp", 1), self.bias_down, self.gain[1], self.shift[1]
        )
        return result, low_result

    def feed_back(self, line, flags, base, cot):
        self.grad_mixed, self.low_mixed, self.low_pre, self.part, self.small_feed = feed_back(
            flags,
            base,
            cot,
            self.unit_two,
            self.scale_two,
            self.gain[1],
            self.weight_down,
            self.slope,
            self.weight_up,
            line.last,
        )
        line.mark(self.small_feed)

    def down_grad(self, line, pair):
        pair.start(line, (self.low_mixed, self.active), (((0, 1),),))

    def up_grad(self, line, pair):
        pair.start(line, (self.low_hidden, self.low_pre), (((0, 1),),))

    def middle_back(self, line):
        self.grad_attended, self.low_attended, self.grad_context, self.small_middle = middle_back(
            self.grad_mixed,
            self.part,
            swap(self.part, "mp", 1),
            self.unit_one,
            self.scale_one,
            self.gain[0],
            self.weight_out,
            line.last,
        )
        line.mark(self.small_middle)

    def attend_back(self, line):
        self.dq, *grads = attend_back(
            self.query,
            self.keys,
            self.values,
            self.augs,
            self.log_total,
            self.context,
            self.grad_context,
            line.last,
        )
        self.dk, self.dv = grads[:2], grads[2:]
        line.mark(self.dq)

    def input_grad_parts(self, line, flags):
        span = self.query.shape[0]
        mine, theirs = back_grad(
            flags, (self.dk[1], self.dv[1]), self.weight_qkv, (1, 2), span, line.last
        )
        arrived = swap(theirs, "mp", 1)
        self.own, theirs = back_grad(
            flags, (self.dq, self.dk[0], self.dv[0]), self.weight_qkv, (0, 1, 2), span, (theirs,)
        )
        rest = add_low(mine, arrived)
        self.far = [swap(rest[j], "seq", 2 * (j + 1)) for j in range(rest.shape[0])]
        self.near = swap(theirs, "mp", 1)
        line.mark(rest, theirs)

    def input_grad(self):
        half = self.own[0].astype(f32) + self.near[0].astype(f32)
        half = (half + sum(f.astype(f32) for f in self.far)).astype(bf16)
        return (self.grad_attended, half, swap(half, "mp", 1))

    qk_pairs = (((0, 2),), ((0, 3), (1, 4)))
    vo_pairs = (((0, 3), (1, 4)), ((2, 5),))

    def value_out_grad(self, line, pair):
        arrays = (self.low_own, self.low_rest, self.low_attended, *self.dv, self.context)
        pair.start(line, arrays, self.vo_pairs)

    def query_key_grad(self, line, pair):
        arrays = (self.low_own, self.low_rest, self.dq, *self.dk)
        pair.start(line, arrays, self.qk_pairs)

    def small(self):
        query_sum = jnp.sum(self.dq.astype(f32), axis=0)
        value_sum = sum(jnp.sum(v.astype(f32), axis=0) for v in self.dv)
        feed, middle = self.small_feed, self.small_middle
        return jnp.stack(
            [
                jnp.concatenate([query_sum, value_sum]),
                middle[2],
                middle[0],
                feed[0],
                middle[1],
                feed[1],
                feed[3],
                feed[4],
                feed[2],
            ]
        )


def layer_part(index, params):
    parts = [array[index] for array in params]
    for i in (3, 7, 9):
        parts[i] = parts[i].reshape(1, -1)
    for i in (4, 5):
        parts[i] = parts[i][:, None, :]
    return tuple(parts)


def stack_pair(first_part, second_part):
    return jnp.stack([first_part, second_part])


def local(
    tokens,
    segments,
    dropped,
    qkv_weight,
    qv_bias,
    out_weight,
    out_bias,
    norm_gain,
    norm_shift,
    up_weight,
    up_bias,
    down_weight,
    down_bias,
    cotangent,
):
    params = (
        qkv_weight,
        qv_bias,
        out_weight,
        out_bias,
        norm_gain,
        norm_shift,
        up_weight,
        up_bias,
        down_weight,
        down_bias,
    )
    first = layer_part(0, params)
    second = layer_part(1, params)
    rows_here, span, width = tokens.shape
    assert rows_here == 2
    places = lax.axis_size("seq")
    place = lax.axis_index("seq")
    row = place & 1
    halves_of = tokens.reshape(rows_here, 2, span // 2, width)
    halves_of = pick(halves_of, lax.axis_index("mp"), 1)
    half_mine, half_partner = pick(halves_of, row, 0), pick(halves_of, 1 - row, 0)
    arrived = [swap((half_mine, half_partner)[c % 2], "seq", c) for c in range(1, places)]
    rest = both_halves(jnp.stack(arrived), axis=1)
    low_own = jnp.concatenate([pick(tokens, row, 0), rest[0]])
    low_rest = rest[1:].reshape(-1, width)
    seg_row = pick(segments, row, 0).reshape(places, span)
    for bit in range(bits_of("seq")):
        shaped = seg_row.reshape(places >> (bit + 1), 2, 1 << bit, span)
        seg_row = jnp.where(place_bit("seq", bit) == 1, shaped[:, ::-1], shaped).reshape(places, span)
    seg_keys = seg_row.reshape(places * span, 1)
    lane = lax.broadcasted_iota(jnp.int32, (1, PAIR), 1) % HEAD
    used = lane < SEGMENTS
    kaug = jnp.where(used & (seg_keys != lane), 1.0, 0.0).astype(bf16)
    qaug = jnp.where(used & (seg_keys[: 2 * span] == lane), -FAR, 0.0).astype(bf16)
    augs = (qaug, kaug[: 2 * span], kaug[2 * span :])
    cot_far = swap(my_half(pick(cotangent, 1 - row, 0)), "seq", 1)
    kept = 1 - pick(dropped, lax.axis_index("dp") * rows_here + row, 0)
    flags = jnp.stack([kept, lax.axis_index("mp")])

    one, two = Layer(first, augs), Layer(second, augs)
    one.open(low_own)
    hidden_one, low_one = one.forward(low_own, low_rest)
    low_half = my_half(low_one)
    arrived = [swap(low_half, "seq", c) for c in range(2, places, 2)]
    two.open(low_one)
    cot = jnp.concatenate([pick(cotangent, row, 0), both_halves(cot_far)])
    rest = both_halves(jnp.stack(arrived), axis=1)
    result_two, _ = two.forward(hidden_one, rest.reshape(-1, width))
    result = jnp.where(kept > 0, result_two, hidden_one)

    class Return:
        def __init__(self, value):
            self.mine = value[:span]
            self.arrived = swap(my_half(value[span:].astype(bf16)), "seq", 1)

        def whole(self):
            far = both_halves(self.arrived).astype(f32)
            return jnp.where(row == 0, jnp.stack([self.mine, far]), jnp.stack([far, self.mine]))

    line = Order()
    outputs = Return(result)
    two.feed_back(line, flags, None, cot)
    feed_two, attn_two, feed_one, attn_one = Pair(), Pair(), Pair(), Pair()
    two.down_grad(line, feed_two)
    two.up_grad(line, feed_two)
    line.mark(*line.last, outputs.arrived)
    two.middle_back(line)
    two.attend_back(line)
    two.input_grad_parts(line, flags)
    two.value_out_grad(line, attn_two)
    two.query_key_grad(line, attn_two)
    feed_two.share(line)
    base = two.input_grad()
    one.feed_back(line, flags, base, cot)
    one.down_grad(line, feed_one)
    one.up_grad(line, feed_one)
    one.middle_back(line)
    attn_two.share(line)
    one.attend_back(line)
    one.value_out_grad(line, attn_one)
    one.query_key_grad(line, attn_one)
    feed_two.shares(line)
    one.input_grad_parts(line, flags)
    attn_two.shares(line)
    feed_one.share(line)
    base, own_half, other_half = one.input_grad()
    line.mark(*line.last, own_half)
    first_core = lax.axis_index("mp") == 0
    grad_tokens = base + jnp.where(
        first_core,
        jnp.concatenate([own_half, other_half]),
        jnp.concatenate([other_half, own_half]),
    ).astype(f32)
    small = jnp.stack([one.small(), two.small()])
    attn_one.share(line)
    tail_two = Tail(line, (feed_two, attn_two))
    small = small + swap(small, "seq", 1)
    tokens_grad = Return(grad_tokens)
    for bit in range(1, bits_of("seq")):
        small = small + swap(small, "seq", 1 << bit)
    line.mark(*line.last, small)
    tail_two.gather(line)
    small = small + swap(small, "dp", 1)
    line.mark(*line.last, small, tokens_grad.arrived)
    feed_one.shares(line)
    attn_one.shares(line)
    for bit in range(1, bits_of("dp")):
        small = small + swap(small, "dp", 1 << bit)
    whole_two = tail_two.finish()
    line.mark(*line.last, small, *tail_two.arrived)
    tail_one = Tail(line, (feed_one, attn_one))
    outputs, tokens_grad = outputs.whole(), tokens_grad.whole()
    tail_one.gather(line)
    whole_one = tail_one.finish()
    halves = width // 2
    qv_sum = small[:, 0].reshape(2, 2, halves)
    out_bias_sum = small[:, 1]
    gain_sum, shift_sum = small[:, 2:4], small[:, 4:6]
    up_bias_sum = small[:, 6:8].reshape(2, 2 * width)
    down_bias_sum = small[:, 8]

    local_width = qkv_weight.shape[3]
    units = up_weight.shape[2]

    def parts(whole):
        down, up = whole
        value, out = down[:, units : units + local_width], down[:, units + local_width :]
        query, key = up[:, units : units + local_width], up[:, units + local_width :]
        return jnp.stack([query, key, value]), out.T, up[:, :units], down[:, :units].T

    qkv_sum, out_sum, up_sum, down_sum = map(stack_pair, parts(whole_one), parts(whole_two))
    return (
        outputs,
        tokens_grad,
        qkv_sum,
        qv_sum,
        out_sum,
        out_bias_sum,
        gain_sum,
        shift_sum,
        up_sum,
        up_bias_sum,
        down_sum,
        down_bias_sum,
    )


def solution(mesh):
    placed = (
        P("dp", "seq", None),
        P("dp", None),
        P(),
        P(None, None, None, "mp"),
        P(None, None, "mp"),
        P(None, "mp", None),
        P(),
        P(),
        P(),
        P(None, None, "mp"),
        P(None, "mp"),
        P(None, "mp", None),
        P(),
        P("dp", "seq", None),
    )
    return jax.shard_map(
        local,
        mesh=mesh,
        in_specs=placed,
        out_specs=(
            P("dp", "seq", None),
            P("dp", "seq", None),
            P(None, None, "dp", "mp"),
            P(None, None, "mp"),
            P(None, "mp", "dp"),
            P(),
            P(),
            P(),
            P(None, "dp", "mp"),
            P(None, "mp"),
            P(None, "mp", "dp"),
            P(),
        ),
        check_vma=False,
    )
```

```python
import functools

import jax
import jax.numpy as jnp
from jax import lax
from jax.experimental import pallas as pl
from jax.experimental.pallas import tpu as pltpu
from jax.sharding import PartitionSpec as P

HEAD = 64
PAIR = 2 * HEAD
SEGMENTS = 4
FAR = 1e30
eps_norm = 1e-05
root_half = 0.7071067811865476
inv_root_tau = 0.3989422804014327
scale_two = 0.125 * 1.4426950408889634
f32 = jnp.float32
bf16 = jnp.bfloat16
PACE = [1.15e9]
MAIN = 3 * 1.15e9
LATE = 3 * 1.15e9
LIMITS = {'pack': 12, 'back': 12, 'sums': 8, 'adds': 8, 'share': 12, 'project': 4, 'attend': 10, 'feed': 14, 'close': 6, 'feed_back': 14, 'weight_grad': 10, 'middle_back': 8, 'attend_back': 14}
BUSY = dict(pack=1.5, back=1.5, sums=1.0, adds=1.0, share=2.0, project=1.5, attend=7.0, feed=6.0, close=1.5, feed_back=6.0, weight_grad=1.4, middle_back=2.5, attend_back=9.5)
anywhere = pl.BlockSpec(memory_space=pl.ANY)
smem = pl.BlockSpec(memory_space=pltpu.SMEM)


def dot_nn(left, right):
    return lax.dot_general(left, right, (((1,), (0,)), ((), ())), preferred_element_type=f32)


def dot_nt(left, right):
    return lax.dot_general(left, right, (((1,), (1,)), ((), ())), preferred_element_type=f32)


def dot_tn(left, right):
    return lax.dot_general(left, right, (((0,), (0,)), ((), ())), preferred_element_type=f32)


def swap(value, axis, mask):
    count = lax.axis_size(axis)
    return lax.ppermute(value, axis, [(i, i ^ mask) for i in range(count)])


def place_bit(axis, bit):
    return (lax.axis_index(axis) >> bit) & 1


def bits_of(axis):
    count = lax.axis_size(axis)
    number = count.bit_length() - 1
    assert 1 << number == count
    return number


def pick(value, index, axis):
    return lax.dynamic_index_in_dim(value, index, axis, keepdims=False)


def add_low(left, right):
    return (left.astype(f32) + right.astype(f32)).astype(bf16)


def call(kernel, name, ins, outs, grid=(), scratch=(), after=()):
    def placed(shape):
        return pltpu.HBM(shape.shape, shape.dtype) if isinstance(shape, Saved) else shape

    def spec(shape, block, index):
        if block == "smem":
            return smem
        if block is None:
            return pl.BlockSpec(shape, lambda *g: (0,) * len(shape))
        return pl.BlockSpec(block, index)

    count = len(ins)

    def body(*refs):
        kernel(*refs[:count], *refs[count + len(after) :])

    return pl.pallas_call(
        body,
        grid=grid,
        in_specs=[spec(a.shape, b, i) for a, b, i in ins] + [anywhere] * len(after),
        out_specs=[spec(s.shape, b, i) for s, b, i in outs],
        out_shape=[placed(s) for s, _, _ in outs],
        scratch_shapes=list(scratch),
        name=name,
        cost_estimate=pl.CostEstimate(flops=int(PACE[0] * BUSY[name]), bytes_accessed=0, transcendentals=0),
        compiler_params=pltpu.CompilerParams(vmem_limit_bytes=LIMITS[name] << 20),
    )(*[a for a, _, _ in ins], *after)


def like(shape, dtype):
    return jax.ShapeDtypeStruct(shape, dtype)


class Saved:
    def __init__(self, shape, dtype):
        self.shape, self.dtype = shape, dtype


def head_lanes(side):
    lane = lax.broadcasted_iota(jnp.int32, (1, PAIR), 1)
    return lane < HEAD if side == 0 else lane >= HEAD


def scores_of(inside, parts, query, qaug):
    probe = jnp.where(inside, query, qaug)
    return jnp.concatenate(
        [dot_nt(jnp.where(inside, k[...], aug[...]), probe) for k, aug in parts], axis=0
    )


def attend_kernel(
    q_ref, k_ref, k2_ref, v_ref, v2_ref, qaug_ref, kaug_ref, kaug2_ref, context_ref, log_ref, vt_ref
):
    own = v_ref.shape[0]

    @pl.when(pl.program_id(1) == 0)
    def _():
        vt_ref[:, :own] = v_ref[...].T
        vt_ref[:, own:] = v2_ref[...].T

    parts = ((k_ref, kaug_ref), (k2_ref, kaug2_ref))
    query = q_ref[...]
    outs = []
    for side in range(2):
        scores = scores_of(head_lanes(side), parts, query, qaug_ref[...])
        peak = jnp.max(scores, axis=0, keepdims=True) * scale_two
        raised = jnp.exp2(scores * scale_two - peak)
        total = jnp.sum(raised, axis=0, keepdims=True)
        mixed = dot_nn(vt_ref[side * HEAD : (side + 1) * HEAD, :], raised.astype(bf16))
        outs.append(mixed / total)
        log_ref[0, side : side + 1, :] = peak + jnp.log2(total)
    context_ref[...] = jnp.concatenate(outs, axis=0).T.astype(bf16)


def attention_specs(count, counts):
    tile = min(count, 512)
    own = (tile, PAIR), lambda p, i: (i, p)
    first, rest = [((n, PAIR), lambda p, i: (0, p)) for n in counts]
    logs = (1, 2, tile), lambda p, i: (p, 0, i)
    aug = (tile, PAIR), lambda p, i: (i, 0)
    return tile, own, first, rest, logs, aug


def attend(query, keys, values, augs):
    count, width = query.shape
    pairs = width // PAIR
    tile, own, first, rest, logs, aug = attention_specs(count, [k.shape[0] for k in keys])
    return call(
        attend_kernel,
        "attend",
        [
            (query, *own),
            (keys[0], *first),
            (keys[1], *rest),
            (values[0], *first),
            (values[1], *rest),
            (augs[0], *aug),
            (augs[1], None, None),
            (augs[2], None, None),
        ],
        [(like(query.shape, bf16), *own), (Saved((pairs, 2, count), f32), *logs)],
        grid=(pairs, count // tile),
        scratch=[pltpu.VMEM((PAIR, sum(k.shape[0] for k in keys)), bf16)],
    )


def attend_back_kernel(
    q_ref,
    k_ref,
    k2_ref,
    v_ref,
    v2_ref,
    qaug_ref,
    kaug_ref,
    kaug2_ref,
    log_ref,
    context_ref,
    grad_ref,
    dq_ref,
    dk_ref,
    dk2_ref,
    dv_ref,
    dv2_ref,
    kt_ref,
    dk_sum,
    dv_sum,
):
    step = pl.program_id(1)
    own = k_ref.shape[0]

    @pl.when(step == 0)
    def _():
        kt_ref[:, :own] = k_ref[...].T
        kt_ref[:, own:] = k2_ref[...].T
        dk_sum[...] = jnp.zeros_like(dk_sum)
        dv_sum[...] = jnp.zeros_like(dv_sum)

    parts = ((k_ref, kaug_ref), (k2_ref, kaug2_ref))
    query, grad = q_ref[...], grad_ref[...]
    zero = jnp.zeros((), bf16)
    product = (grad.astype(f32) * context_ref[...].astype(f32)).T
    outs = []
    for side in range(2):
        inside = head_lanes(side)
        scores = scores_of(inside, parts, query, qaug_ref[...])
        chance = jnp.exp2(scores * scale_two - log_ref[0, side : side + 1, :])
        grad_side = jnp.where(inside, grad, zero)
        inner = jnp.sum(product[side * HEAD : (side + 1) * HEAD], axis=0, keepdims=True)
        grad_chance = jnp.concatenate([dot_nt(v[...], grad_side) for v in (v_ref, v2_ref)], axis=0)
        grad_scores = (chance * (grad_chance - inner)).astype(bf16)
        dv_sum[...] += dot_nn(chance.astype(bf16), grad_side)
        dk_sum[...] += dot_nn(grad_scores, jnp.where(inside, query, zero))
        outs.append(dot_nn(kt_ref[side * HEAD : (side + 1) * HEAD, :], grad_scores))
    dq_ref[...] = (jnp.concatenate(outs, axis=0) * 0.125).T.astype(bf16)

    @pl.when(step == pl.num_programs(1) - 1)
    def _():
        dk_ref[...] = (dk_sum[:own] * 0.125).astype(bf16)
        dk2_ref[...] = (dk_sum[own:] * 0.125).astype(bf16)
        dv_ref[...] = dv_sum[:own].astype(bf16)
        dv2_ref[...] = dv_sum[own:].astype(bf16)


def attend_back(query, keys, values, augs, log_total, context, grad_context, after=()):
    count, width = query.shape
    full = sum(k.shape[0] for k in keys)
    pairs = width // PAIR
    tile, own, first, rest, logs, aug = attention_specs(count, [k.shape[0] for k in keys])
    return call(
        attend_back_kernel,
        "attend_back",
        [
            (query, *own),
            (keys[0], *first),
            (keys[1], *rest),
            (values[0], *first),
            (values[1], *rest),
            (augs[0], *aug),
            (augs[1], None, None),
            (augs[2], None, None),
            (log_total, *logs),
            (context, *own),
            (grad_context, *own),
        ],
        [
            (like(query.shape, bf16), *own),
            (like(keys[0].shape, bf16), *first),
            (like(keys[1].shape, bf16), *rest),
            (like(keys[0].shape, bf16), *first),
            (like(keys[1].shape, bf16), *rest),
        ],
        grid=(pairs, count // tile),
        scratch=[
            pltpu.VMEM((PAIR, full), bf16),
            pltpu.VMEM((full, PAIR), f32),
            pltpu.VMEM((full, PAIR), f32),
        ],
        after=after,
    )


def project_kernel(with_query, in_ref, weight_ref, bias_ref, *outs):
    low = in_ref[...]
    if with_query:
        outs[0][...] = (dot_nn(low, weight_ref[0]) + bias_ref[0]).astype(bf16)
        outs = outs[1:]
    outs[0][...] = dot_nn(low, weight_ref[1]).astype(bf16)
    outs[1][...] = (dot_nn(low, weight_ref[2]) + bias_ref[1]).astype(bf16)


def project(low, weight, bias, with_query):
    count, width = low.shape
    local_width = weight.shape[2]
    tile = min(count, 256)
    if count % tile:
        tile = count
    out = like((count, local_width), bf16), *rows(tile, local_width)
    return call(
        functools.partial(project_kernel, with_query),
        "project",
        [(low, *rows(tile, width)), (weight, None, None), (bias, None, None)],
        [out] * (3 if with_query else 2),
        grid=(count // tile,),
    )


def normalize(rows_in, gain, shift):
    center = rows_in - jnp.mean(rows_in, axis=-1, keepdims=True)
    scale = lax.rsqrt(jnp.mean(center * center, axis=-1, keepdims=True) + eps_norm)
    unit = center * scale
    return (unit * gain + shift, unit, scale)


def normalize_back(grad_out, unit, scale, gain):
    grad_unit = grad_out * gain
    inner = (
        grad_unit
        - jnp.mean(grad_unit, axis=-1, keepdims=True)
        - unit * jnp.mean(grad_unit * unit, axis=-1, keepdims=True)
    )
    return inner * scale


def rows(tile, width):
    return (tile, width), lambda i: (i, 0)


def feed_kernel(
    in_ref,
    mine_ref,
    theirs_ref,
    bias_ref,
    gain_ref,
    shift_ref,
    up_ref,
    up_bias_ref,
    down_ref,
    hidden_ref,
    low_ref,
    unit_ref,
    scale_ref,
    active_ref,
    slope_ref,
    part_ref,
):
    summed = mine_ref[...].astype(f32) + theirs_ref[...].astype(f32)
    total = in_ref[...].astype(f32) + (summed + bias_ref[...])
    hidden, unit, scale = normalize(total, gain_ref[...], shift_ref[...])
    low = hidden.astype(bf16)
    hidden_ref[...] = hidden
    low_ref[...] = low
    unit_ref[...] = unit.astype(bf16)
    scale_ref[...] = jnp.broadcast_to(scale, scale_ref.shape)
    pre = dot_nn(low, up_ref[...]) + up_bias_ref[...]
    below = 0.5 * (1.0 + lax.erf(pre * root_half))
    active = (pre * below).astype(bf16)
    active_ref[...] = active
    slope_ref[...] = (below + pre * (jnp.exp(-0.5 * pre * pre) * inv_root_tau)).astype(bf16)
    part_ref[...] = dot_nn(active, down_ref[...]).astype(bf16)


def feed(inputs, mine, theirs, bias, gain, shift, up, up_bias, down):
    count, width = inputs.shape
    units = up.shape[1]
    tile = min(count, 256)
    wide, narrow = rows(tile, units), rows(tile, width)
    return call(
        feed_kernel,
        "feed",
        [(inputs, *narrow), (mine, *narrow), (theirs, *narrow)]
        + [(a, None, None) for a in (bias, gain, shift, up, up_bias, down)],
        [
            (like((count, width), f32), *narrow),
            (Saved((count, width), bf16), *narrow),
            (Saved((count, width), bf16), *narrow),
            (Saved((count, 128), f32), *rows(tile, 128)),
            (Saved((count, units), bf16), *wide),
            (Saved((count, units), bf16), *wide),
            (like((count, width), bf16), *narrow),
        ],
        grid=(count // tile,),
    )


def close_kernel(
    in_ref, mine_ref, theirs_ref, bias_ref, gain_ref, shift_ref, out_ref, low_ref, unit_ref, scale_ref
):
    summed = mine_ref[...].astype(f32) + theirs_ref[...].astype(f32)
    total = in_ref[...] + (summed + bias_ref[...])
    result, unit, scale = normalize(total, gain_ref[...], shift_ref[...])
    out_ref[...] = result
    low_ref[...] = result.astype(bf16)
    unit_ref[...] = unit.astype(bf16)
    scale_ref[...] = jnp.broadcast_to(scale, scale_ref.shape)


def close(inputs, mine, theirs, bias, gain, shift):
    count, width = inputs.shape
    tile = min(count, 256)
    narrow = rows(tile, width)
    return call(
        close_kernel,
        "close",
        [(inputs, *narrow), (mine, *narrow), (theirs, *narrow)]
        + [(a, None, None) for a in (bias, gain, shift)],
        [
            (like((count, width), f32), *narrow),
            (like((count, width), bf16), *narrow),
            (like((count, width), bf16), *narrow),
            (like((count, 128), f32), *rows(tile, 128)),
        ],
        grid=(count // tile,),
    )


def feed_back_kernel(has_base, flag_ref, *refs):
    if has_base:
        base_ref, mine_ref, theirs_ref, refs = refs[0], refs[1], refs[2], refs[3:]
    (
        cot_ref,
        unit_ref,
        scale_ref,
        gain_ref,
        down_ref,
        slope_ref,
        up_ref,
        mixed_ref,
        low_mixed_ref,
        low_pre_ref,
        part_ref,
        small_ref,
    ) = refs
    step = pl.program_id(0)
    kept = flag_ref[0] > 0
    cot = cot_ref[...].astype(f32)
    if has_base:
        here = flag_ref[1] == step
        back = jnp.where(here, mine_ref[...], theirs_ref[...]).astype(f32)
        grad_out = jnp.where(kept, base_ref[...] + back, cot)
    else:
        grad_out = jnp.where(kept, cot, 0.0)
    unit = unit_ref[...].astype(f32)
    grad_mixed = normalize_back(grad_out, unit, scale_ref[:, :1], gain_ref[...])
    mixed_ref[...] = grad_mixed
    low_mixed = grad_mixed.astype(bf16)
    low_mixed_ref[...] = low_mixed
    grad_active = dot_nt(low_mixed, down_ref[...])
    low_pre = (grad_active * slope_ref[...].astype(f32)).astype(bf16)
    low_pre_ref[...] = low_pre
    part_ref[...] = dot_nt(low_pre, up_ref[...]).astype(bf16)

    @pl.when(step == 0)
    def _():
        small_ref[...] = jnp.zeros_like(small_ref)

    width = grad_out.shape[1]

    def total(value):
        return jnp.sum(value, axis=0, keepdims=True)

    pre_sum = total(low_pre.astype(f32))
    small_ref[0:1, :] += total(grad_out * unit)
    small_ref[1:2, :] += total(grad_out)
    small_ref[2:3, :] += total(grad_mixed)
    small_ref[3:4, :] += pre_sum[:, :width]
    small_ref[4:5, :] += pre_sum[:, width:]


def feed_back(flags, base, cot, unit, scale, gain, down, slope, up, after=()):
    count, width = cot.shape
    units = up.shape[1]
    tile = count // 2
    wide, narrow = rows(tile, units), rows(tile, width)
    ins = [(flags, "smem", None)]
    if base is not None:
        ins += [(base[0], *narrow), (base[1], None, None), (base[2], None, None)]
    ins += [
        (cot, *narrow),
        (unit, *narrow),
        (scale, *rows(tile, 128)),
        (gain, None, None),
        (down, None, None),
        (slope, *wide),
        (up, None, None),
    ]
    return call(
        functools.partial(feed_back_kernel, base is not None),
        "feed_back",
        ins,
        [
            (like((count, width), f32), *narrow),
            (like((count, width), bf16), *narrow),
            (like((count, units), bf16), *wide),
            (like((count, width), bf16), *narrow),
            (like((8, width), f32), None, None),
        ],
        grid=(2,),
        after=after,
    )


def middle_back_kernel(
    mixed_ref,
    mine_ref,
    theirs_ref,
    unit_ref,
    scale_ref,
    gain_ref,
    out_ref,
    attended_ref,
    low_ref,
    context_ref,
    small_ref,
):
    summed = mine_ref[...].astype(f32) + theirs_ref[...].astype(f32)
    grad_hidden = mixed_ref[...] + summed
    unit = unit_ref[...].astype(f32)
    grad = normalize_back(grad_hidden, unit, scale_ref[:, :1], gain_ref[...])
    attended_ref[...] = grad
    low = grad.astype(bf16)
    low_ref[...] = low
    context_ref[...] = dot_nt(low, out_ref[...]).astype(bf16)

    @pl.when(pl.program_id(0) == 0)
    def _():
        small_ref[...] = jnp.zeros_like(small_ref)

    small_ref[0:1, :] += jnp.sum(grad_hidden * unit, axis=0, keepdims=True)
    small_ref[1:2, :] += jnp.sum(grad_hidden, axis=0, keepdims=True)
    small_ref[2:3, :] += jnp.sum(grad, axis=0, keepdims=True)


def middle_back(mixed, mine, theirs, unit, scale, gain, out_weight, after=()):
    count, width = mixed.shape
    local_width = out_weight.shape[0]
    tile = min(count, 256)
    narrow = rows(tile, width)
    return call(
        middle_back_kernel,
        "middle_back",
        [
            (mixed, *narrow),
            (mine, *narrow),
            (theirs, *narrow),
            (unit, *narrow),
            (scale, *rows(tile, 128)),
            (gain, None, None),
            (out_weight, None, None),
        ],
        [
            (like((count, width), f32), *narrow),
            (like((count, width), bf16), *narrow),
            (like((count, local_width), bf16), *rows(tile, local_width)),
            (like((8, width), f32), None, None),
        ],
        grid=(count // tile,),
        after=after,
    )


def put_halves(flag, value, column, send_ref, keep_ref):
    shares, half = send_ref.shape[:2]
    columns = slice(column, column + value.shape[1])
    value = value.astype(bf16)
    for share in range(shares):
        low = value[2 * share * half : (2 * share + 1) * half]
        high = value[(2 * share + 1) * half : (2 * share + 2) * half]
        send_ref[share, :, columns] = jnp.where(flag > 0, low, high)
        keep_ref[share, :, columns] = jnp.where(flag > 0, high, low)


def weight_kernel(pairs, flag_ref, *refs):
    lefts_rights, (send_ref, keep_ref) = refs[:-2], refs[-2:]
    column = 0
    for terms in pairs:
        value = 0.0
        for left, right in terms:
            value = value + dot_tn(lefts_rights[left][...], lefts_rights[right][...])
        put_halves(flag_ref[0], value, column, send_ref, keep_ref)
        column += value.shape[1]


def weight_grad(flag, arrays, pairs, after=()):
    shares = lax.axis_size("dp")
    width = arrays[pairs[0][0][0]].shape[1]
    columns = sum(arrays[terms[0][1]].shape[1] for terms in pairs)
    shape = (shares, width // (2 * shares), columns)
    return call(
        functools.partial(weight_kernel, pairs),
        "weight_grad",
        [(flag, "smem", None)] + [(a, None, None) for a in arrays],
        [(like(shape, bf16), None, None)] * 2,
        after=after,
    )


def back_kernel(flag_ref, *refs):
    terms, (mine_ref, theirs_ref) = refs[:-2], refs[-2:]
    parts, half = mine_ref.shape[:2]
    grads = terms[: len(terms) // 2]
    weights = terms[len(terms) // 2 :]
    for part in range(parts):
        halves = []
        for side in range(2):
            start = (2 * part + side) * half
            value = 0.0
            for grad, weight in zip(grads, weights):
                value = value + dot_nt(grad[start : start + half], weight[0])
            halves.append(value.astype(bf16))
        mine_ref[part] = jnp.where(flag_ref[1] > 0, halves[1], halves[0])
        theirs_ref[part] = jnp.where(flag_ref[1] > 0, halves[0], halves[1])


def back_grad(flags, grads, weight, which, span, after=()):
    count, local_width = grads[0].shape
    width = weight.shape[1]
    out = like((count // span, span // 2, width), bf16), None, None
    return call(
        back_kernel,
        "back",
        [(flags, "smem", None)]
        + [(g, g.shape, lambda i: (0, 0)) for g in grads]
        + [(weight, (1, width, local_width), lambda i, w=w: (w, 0, 0)) for w in which],
        [out, out],
        grid=(1,),
        after=after,
    )


def sums_kernel(count, *refs):
    keeps, arrived, outs = refs[:count], refs[count : 2 * count], refs[2 * count :]
    for k in range(2):
        column = 0
        for keep, other in zip(keeps, arrived):
            columns = slice(column, column + keep.shape[-1])
            outs[k][:, columns] = add_low(keep[k, 0], other[k, 0])
            column += keep.shape[-1]


def sums(keeps, arrived, after=()):
    rows_, columns = keeps[0].shape[2], sum(k.shape[3] for k in keeps)
    out = like((rows_, columns), bf16), None, None
    return call(
        functools.partial(sums_kernel, len(keeps)),
        "sums",
        [(a, None, None) for a in (*keeps, *arrived)],
        [out, out],
        after=after,
    )


def adds_kernel(a_ref, b_ref, c_ref, d_ref, first_ref, second_ref):
    first_ref[...] = add_low(a_ref[...], b_ref[...])
    second_ref[...] = add_low(c_ref[...], d_ref[...])


def adds(first, second, after=()):
    out = like(first[0].shape, bf16), None, None
    return call(
        adds_kernel,
        "adds",
        [(a, None, None) for a in (*first, *second)],
        [out, out],
        after=after,
    )


def pack_kernel(*refs):
    ins, out_ref = refs[:-1], refs[-1]
    each = len(ins) // 2
    out_ref[...] = jnp.zeros_like(out_ref)

    def total(ref):
        return jnp.sum(ref[...].astype(f32), axis=0, keepdims=True)

    for layer in range(2):
        dq, dv, dv2, feed, middle = ins[layer * each : (layer + 1) * each]
        width = dq.shape[1]
        base = 16 * layer
        out_ref[base : base + 1, :width] = total(dq)
        out_ref[base : base + 1, width:] = total(dv) + total(dv2)
        sources = (middle, 2), (middle, 0), (feed, 0), (middle, 1), (feed, 1), (feed, 3), (feed, 4)
        for i, (ref, row) in enumerate(sources + ((feed, 2),)):
            out_ref[base + 1 + i : base + 2 + i, :] = ref[row : row + 1, :]


def pack(first, second, after=()):
    width = first[3].shape[1]
    return call(
        pack_kernel,
        "pack",
        [(a, a.shape, lambda i: (0, 0)) for a in (*first, *second)],
        [(like((32, width), f32), (32, width), lambda i: (0, 0))],
        grid=(1,),
        after=after,
    )[0]


class Order:
    def __init__(self):
        self.last = ()

    def mark(self, *values):
        self.last = values


def both_halves(mine, axis=0):
    other = swap(mine, "mp", 1)
    first = lax.axis_index("mp") == 0
    whole = jnp.where(
        first, jnp.stack([mine, other], axis=axis), jnp.stack([other, mine], axis=axis)
    )
    return whole.reshape(mine.shape[:axis] + (-1,) + mine.shape[axis + 1 :])


def my_half(value):
    count = value.shape[0] // 2
    return pick(value.reshape((2, count) + value.shape[1:]), lax.axis_index("mp"), 0)


def share_kernel(counts, flag_ref, *refs):
    ins, (send_ref, keep_ref) = refs[:-2], refs[-2:]
    half = len(ins) // 2
    place, column = 0, 0
    for count in counts:
        keeps = ins[place : place + count]
        arrived = ins[half + place : half + place + count]
        place += count
        width = keeps[0].shape[-1]
        columns = slice(column, column + width)
        column += width

        def part(group, bundle, side):
            return group[0][bundle, side] if len(group) == 1 else group[bundle][side]

        for bundle in range(2):
            low, high = [
                add_low(part(keeps, bundle, side), part(arrived, bundle, side))
                for side in range(2)
            ]
            send_ref[bundle, 0, :, columns] = jnp.where(flag_ref[0] > 0, low, high)
            keep_ref[bundle, 0, :, columns] = jnp.where(flag_ref[0] > 0, high, low)


def share_step(flag, pairs, after=()):
    shares, half = pairs[0].keeps[0].shape[-3:-1]
    columns = sum(p.keeps[0].shape[-1] for p in pairs)

    def blocked(array):
        shape = array.shape
        if array.ndim == 3:
            return array, (2,) + shape[1:], lambda i: (i, 0, 0)
        return array, (2, 2) + shape[2:], lambda i: (0, i, 0, 0)

    out = like((2, shares // 2, half, columns), bf16), (2, 1, half, columns), lambda i: (0, i, 0, 0)
    return call(
        functools.partial(share_kernel, [len(p.keeps) for p in pairs]),
        "share",
        [(flag, "smem", None)]
        + [blocked(a) for p in pairs for a in p.keeps]
        + [blocked(a) for p in pairs for a in p.arrived],
        [out, out],
        grid=(shares // 2,),
        after=after,
    )


def split_kernel(flag_ref, *refs):
    for bundle in range(2):
        keep, arrived = refs[bundle], refs[2 + bundle]
        send_ref, keep_ref = refs[4 + 2 * bundle : 6 + 2 * bundle]
        half = keep.shape[1] // 2
        low = add_low(keep[:, :half], arrived[:, :half])
        high = add_low(keep[:, half:], arrived[:, half:])
        send_ref[...] = jnp.where(flag_ref[bundle] > 0, low, high)
        keep_ref[...] = jnp.where(flag_ref[bundle] > 0, high, low)


def split_step(flags, keeps, arrived, after=()):
    shares, rows_, columns = keeps[0].shape
    block = (1, rows_, columns), lambda i: (i, 0, 0)
    out = (
        like((shares, rows_ // 2, columns), bf16),
        (1, rows_ // 2, columns),
        lambda i: (i, 0, 0),
    )
    return call(
        split_kernel,
        "share",
        [(flags, "smem", None)] + [(a, *block) for a in (*keeps, *arrived)],
        [out] * 4,
        grid=(shares,),
        after=after,
    )


def join_kernel(flag_ref, a_ref, b_ref, c_ref, d_ref, first_ref, second_ref):
    for k, (mine, other, out) in enumerate(((a_ref, b_ref, first_ref), (c_ref, d_ref, second_ref))):
        half = mine.shape[0]
        out[:half] = jnp.where(flag_ref[k] > 0, other[...], mine[...])
        out[half:] = jnp.where(flag_ref[k] > 0, mine[...], other[...])


def join(flags, first, second, after=()):
    rows_, columns = first[0].shape
    out = like((2 * rows_, columns), bf16), None, None
    return call(
        join_kernel,
        "adds",
        [(flags, "smem", None)] + [(a, None, None) for a in (*first, *second)],
        [out, out],
        after=after,
    )


def last_bit():
    return bits_of("seq") - 1


class Pair:
    def __init__(self):
        self.keeps, self.arrived, self.bit = [], [], 0

    def start(self, line, arrays, pairs):
        bit = 0 if self.keeps else last_bit()
        flag = place_bit("seq", bit).reshape(1)
        send, keep = weight_grad(flag, arrays, pairs, line.last)
        line.mark(send)
        self.keeps.append(keep)
        self.arrived.append(swap(send, "seq", 1 << bit))

    def split(self, line):
        flags = jnp.stack([place_bit("seq", 0), place_bit("seq", last_bit())])
        sent = split_step(flags, self.keeps, self.arrived, line.last)
        self.keeps = [sent[1], sent[3]]
        self.arrived = [
            swap(sent[0], "seq", 1),
            swap(sent[2], "seq", 1 << last_bit()),
        ]
        line.mark(sent[0])


def share(line, *pairs):
    bit = pairs[0].bit
    flag = place_bit("dp", bit).reshape(1)
    send, keep = share_step(flag, pairs, line.last)
    line.mark(send)
    joined = pairs[0]
    joined.keeps, joined.arrived = [keep], [swap(send, "dp", 1 << bit)]
    joined.bit = bit + 1
    return joined


class Tail:
    def __init__(self, line, pair, twice):
        self.totals = sums(pair.keeps, pair.arrived, line.last)
        self.twice = twice
        bits = list(range(bits_of("seq")))
        if twice:
            self.hop(line, (0, last_bit()))
            return
        self.across = (bits[:-1], bits[1:])
        for place in range(len(bits) - 2):
            self.totals = [
                add_low(t, swap(t, "seq", 1 << across[place]))
                for t, across in zip(self.totals, self.across)
            ]
        self.hop(line, [across[-1] for across in self.across])

    def hop(self, line, bits):
        line.mark(*self.totals)
        self.arrived = [swap(t, "seq", 1 << b) for t, b in zip(self.totals, bits)]

    def gather(self, line):
        first, second = zip(self.totals, self.arrived)
        if self.twice:
            flags = jnp.stack([place_bit("seq", 0), place_bit("seq", last_bit())])
            self.totals = join(flags, first, second, line.last)
        else:
            self.totals = adds(first, second, line.last)
        self.hop(line, (last_bit(), 0))

    def finish(self):
        whole = []
        for total, other, bit in zip(self.totals, self.arrived, (last_bit(), 0)):
            first = place_bit("seq", bit) == 0
            whole.append(
                jnp.where(
                    first, jnp.concatenate([total, other]), jnp.concatenate([other, total])
                ).astype(f32)
            )
        return whole


class Layer:
    def __init__(self, params, augs):
        (
            self.weight_qkv,
            self.bias_qv,
            self.weight_out,
            self.bias_out,
            self.gain,
            self.shift,
            self.weight_up,
            self.bias_up,
            self.weight_down,
            self.bias_down,
        ) = params
        self.augs = augs

    def open(self, low_own):
        self.low_own = low_own
        self.query, self.key_own, self.value_own = project(
            low_own, self.weight_qkv, self.bias_qv, True
        )

    def forward(self, inputs, low_rest):
        self.low_rest = low_rest
        key_rest, value_rest = project(low_rest, self.weight_qkv, self.bias_qv, False)
        self.keys = (self.key_own, key_rest)
        self.values = (self.value_own, value_rest)
        self.context, self.log_total = attend(self.query, self.keys, self.values, self.augs)
        part = dot_nn(self.context, self.weight_out).astype(bf16)
        hidden, self.low_hidden, self.unit_one, self.scale_one, self.active, self.slope, part = feed(
            inputs,
            part,
            swap(part, "mp", 1),
            self.bias_out,
            self.gain[0],
            self.shift[0],
            self.weight_up,
            self.bias_up,
            self.weight_down,
        )
        result, low_result, self.unit_two, self.scale_two = close(
            hidden, part, swap(part, "mp", 1), self.bias_down, self.gain[1], self.shift[1]
        )
        return result, low_result

    def feed_back(self, line, flags, base, cot):
        self.grad_mixed, self.low_mixed, self.low_pre, self.part, self.small_feed = feed_back(
            flags,
            base,
            cot,
            self.unit_two,
            self.scale_two,
            self.gain[1],
            self.weight_down,
            self.slope,
            self.weight_up,
            line.last,
        )
        line.mark(self.small_feed)

    def down_grad(self, line, pair):
        pair.start(line, (self.low_mixed, self.active), (((0, 1),),))

    def up_grad(self, line, pair):
        pair.start(line, (self.low_hidden, self.low_pre), (((0, 1),),))

    def middle_back(self, line):
        self.grad_attended, self.low_attended, self.grad_context, self.small_middle = middle_back(
            self.grad_mixed,
            self.part,
            swap(self.part, "mp", 1),
            self.unit_one,
            self.scale_one,
            self.gain[0],
            self.weight_out,
            line.last,
        )
        line.mark(self.small_middle)

    def attend_back(self, line):
        self.dq, *grads = attend_back(
            self.query,
            self.keys,
            self.values,
            self.augs,
            self.log_total,
            self.context,
            self.grad_context,
            line.last,
        )
        self.dk, self.dv = grads[:2], grads[2:]
        line.mark(self.dq)

    def input_grad_parts(self, line, flags):
        span = self.query.shape[0]
        mine, theirs = back_grad(
            flags, (self.dk[1], self.dv[1]), self.weight_qkv, (1, 2), span, line.last
        )
        arrived = swap(theirs, "mp", 1)
        self.own, theirs = back_grad(
            flags, (self.dq, self.dk[0], self.dv[0]), self.weight_qkv, (0, 1, 2), span, (theirs,)
        )
        rest = add_low(mine, arrived)
        self.far = [swap(rest[j], "seq", 2 * (j + 1)) for j in range(rest.shape[0])]
        self.near = swap(theirs, "mp", 1)
        line.mark(rest, theirs)

    def input_grad(self):
        half = self.own[0].astype(f32) + self.near[0].astype(f32)
        half = (half + sum(f.astype(f32) for f in self.far)).astype(bf16)
        return (self.grad_attended, half, swap(half, "mp", 1))

    qk_pairs = (((0, 2),), ((0, 3), (1, 4)))
    vo_pairs = (((0, 3), (1, 4)), ((2, 5),))

    def value_out_grad(self, line, pair):
        arrays = (self.low_own, self.low_rest, self.low_attended, *self.dv, self.context)
        pair.start(line, arrays, self.vo_pairs)

    def query_key_grad(self, line, pair):
        arrays = (self.low_own, self.low_rest, self.dq, *self.dk)
        pair.start(line, arrays, self.qk_pairs)

    def small(self):
        return (self.dq, *self.dv, self.small_feed, self.small_middle)


def layer_part(index, params):
    parts = [array[index] for array in params]
    for i in (3, 7, 9):
        parts[i] = parts[i].reshape(1, -1)
    for i in (4, 5):
        parts[i] = parts[i][:, None, :]
    return tuple(parts)


def stack_pair(first_part, second_part):
    return jnp.stack([first_part, second_part])


def local(
    tokens,
    segments,
    dropped,
    qkv_weight,
    qv_bias,
    out_weight,
    out_bias,
    norm_gain,
    norm_shift,
    up_weight,
    up_bias,
    down_weight,
    down_bias,
    cotangent,
):
    params = (
        qkv_weight,
        qv_bias,
        out_weight,
        out_bias,
        norm_gain,
        norm_shift,
        up_weight,
        up_bias,
        down_weight,
        down_bias,
    )
    first = layer_part(0, params)
    second = layer_part(1, params)
    rows_here, span, width = tokens.shape
    assert rows_here == 2
    places = lax.axis_size("seq")
    place = lax.axis_index("seq")
    row = place & 1
    halves_of = tokens.reshape(rows_here, 2, span // 2, width)
    halves_of = pick(halves_of, lax.axis_index("mp"), 1)
    half_mine, half_partner = pick(halves_of, row, 0), pick(halves_of, 1 - row, 0)
    arrived = [swap((half_mine, half_partner)[c % 2], "seq", c) for c in range(1, places)]
    rest = both_halves(jnp.stack(arrived), axis=1)
    low_own = jnp.concatenate([pick(tokens, row, 0), rest[0]])
    low_rest = rest[1:].reshape(-1, width)
    seg_row = pick(segments, row, 0).reshape(places, span)
    for bit in range(bits_of("seq")):
        shaped = seg_row.reshape(places >> (bit + 1), 2, 1 << bit, span)
        seg_row = jnp.where(place_bit("seq", bit) == 1, shaped[:, ::-1], shaped).reshape(places, span)
    seg_keys = seg_row.reshape(places * span, 1)
    lane = lax.broadcasted_iota(jnp.int32, (1, PAIR), 1) % HEAD
    used = lane < SEGMENTS
    kaug = jnp.where(used & (seg_keys != lane), 1.0, 0.0).astype(bf16)
    qaug = jnp.where(used & (seg_keys[: 2 * span] == lane), -FAR, 0.0).astype(bf16)
    augs = (qaug, kaug[: 2 * span], kaug[2 * span :])
    cot_far = swap(my_half(pick(cotangent, 1 - row, 0)), "seq", 1)
    kept = 1 - pick(dropped, lax.axis_index("dp") * rows_here + row, 0)
    flags = jnp.stack([kept, lax.axis_index("mp")])

    one, two = Layer(first, augs), Layer(second, augs)
    one.open(low_own)
    hidden_one, low_one = one.forward(low_own, low_rest)
    low_half = my_half(low_one)
    arrived = [swap(low_half, "seq", c) for c in range(2, places, 2)]
    two.open(low_one)
    cot = jnp.concatenate([pick(cotangent, row, 0), both_halves(cot_far)])
    rest = both_halves(jnp.stack(arrived), axis=1)
    result_two, _ = two.forward(hidden_one, rest.reshape(-1, width))
    result = jnp.where(kept > 0, result_two, hidden_one)

    class Return:
        def __init__(self, value):
            self.mine = value[:span]
            self.arrived = swap(my_half(value[span:].astype(bf16)), "seq", 1)
            self.other = swap(self.arrived, "mp", 1)

        def whole(self):
            core = lax.axis_index("mp") == 0
            far = jnp.where(
                core,
                jnp.concatenate([self.arrived, self.other]),
                jnp.concatenate([self.other, self.arrived]),
            ).astype(f32)
            return jnp.where(row == 0, jnp.stack([self.mine, far]), jnp.stack([far, self.mine]))

    PACE[0] = MAIN
    line = Order()
    outputs = Return(result)
    two.feed_back(line, flags, None, cot)
    feed_two, attn_two, feed_one, attn_one = Pair(), Pair(), Pair(), Pair()
    two.down_grad(line, feed_two)
    two.up_grad(line, feed_two)
    line.mark(*line.last, outputs.arrived)
    two.middle_back(line)
    line.mark(*line.last, outputs.other)
    two.attend_back(line)
    two.input_grad_parts(line, flags)
    two.value_out_grad(line, attn_two)
    two.query_key_grad(line, attn_two)
    share(line, feed_two)
    base = two.input_grad()
    one.feed_back(line, flags, base, cot)
    one.down_grad(line, feed_one)
    one.up_grad(line, feed_one)
    one.middle_back(line)
    share(line, attn_two)
    one.attend_back(line)
    PACE[0] = LATE
    one.value_out_grad(line, attn_one)
    one.query_key_grad(line, attn_one)
    for _ in range(1, bits_of("dp")):
        pair_two = share(line, feed_two, *([attn_two] if feed_two.bit == 1 else []))
    twice = bits_of("seq") == 2 and width // lax.axis_size("dp") % 64 == 0
    if twice:
        feed_one.split(line)
        attn_one.split(line)
    share(line, feed_one)
    one.input_grad_parts(line, flags)
    share(line, attn_one)
    tail_two = Tail(line, pair_two, False)
    for _ in range(1, bits_of("dp")):
        pair_one = share(line, feed_one, *([attn_one] if feed_one.bit == 1 else []))
    tail_two.gather(line)
    small = pack(one.small(), two.small(), line.last)
    line.mark(*line.last, small)
    base, own_half, other_half = one.input_grad()
    for bit in range(bits_of("seq")):
        small = small + swap(small, "seq", 1 << bit)
    line.mark(*line.last, own_half, small)
    first_core = lax.axis_index("mp") == 0
    grad_tokens = base + jnp.where(
        first_core,
        jnp.concatenate([own_half, other_half]),
        jnp.concatenate([other_half, own_half]),
    ).astype(f32)
    tokens_grad = Return(grad_tokens)
    tail_one = Tail(line, pair_one, twice)
    for bit in range(bits_of("dp")):
        small = small + swap(small, "dp", 1 << bit)
    whole_two = tail_two.finish()
    outputs, tokens_grad = outputs.whole(), tokens_grad.whole()
    tail_one.gather(line)
    whole_one = tail_one.finish()
    small = small.reshape(2, 16, width)
    halves = width // 2
    qv_sum = small[:, 0].reshape(2, 2, halves)
    out_bias_sum = small[:, 1]
    gain_sum, shift_sum = small[:, 2:4], small[:, 4:6]
    up_bias_sum = small[:, 6:8].reshape(2, 2 * width)
    down_bias_sum = small[:, 8]

    local_width = qkv_weight.shape[3]
    units = up_weight.shape[2]

    def parts(whole):
        down, up = whole
        value, out = down[:, units : units + local_width], down[:, units + local_width :]
        query, key = up[:, units : units + local_width], up[:, units + local_width :]
        return jnp.stack([query, key, value]), out.T, up[:, :units], down[:, :units].T

    qkv_sum, out_sum, up_sum, down_sum = map(stack_pair, parts(whole_one), parts(whole_two))
    return (
        outputs,
        tokens_grad,
        qkv_sum,
        qv_sum,
        out_sum,
        out_bias_sum,
        gain_sum,
        shift_sum,
        up_sum,
        up_bias_sum,
        down_sum,
        down_bias_sum,
    )


def solution(mesh):
    placed = (
        P("dp", "seq", None),
        P("dp", None),
        P(),
        P(None, None, None, "mp"),
        P(None, None, "mp"),
        P(None, "mp", None),
        P(),
        P(),
        P(),
        P(None, None, "mp"),
        P(None, "mp"),
        P(None, "mp", None),
        P(),
        P("dp", "seq", None),
    )
    return jax.shard_map(
        local,
        mesh=mesh,
        in_specs=placed,
        out_specs=(
            P("dp", "seq", None),
            P("dp", "seq", None),
            P(None, None, "dp", "mp"),
            P(None, None, "mp"),
            P(None, "mp", "dp"),
            P(),
            P(),
            P(),
            P(None, "dp", "mp"),
            P(None, "mp"),
            P(None, "mp", "dp"),
            P(),
        ),
        check_vma=False,
    )
```

```python
import functools

import jax
import jax.numpy as jnp
from jax import lax
from jax.experimental import pallas as pl
from jax.experimental.pallas import tpu as pltpu
from jax.sharding import PartitionSpec as P

HEAD = 64
PAIR = 2 * HEAD
SEGMENTS = 4
FAR = 1e30
eps_norm = 1e-05
root_half = 0.7071067811865476
inv_root_tau = 0.3989422804014327
scale_two = 0.125 * 1.4426950408889634
f32 = jnp.float32
bf16 = jnp.bfloat16
COSTS = (1.5, 1.5, 7, 6, 1.5, 1.5, 1, 1.5, 7, 6, 1.5, 18, 4.2, 4.2, 7.5, 28.5, 4.5, 4.5, 4.2, 4.2, 6, 6, 18, 4.2, 4.2, 7.5, 6, 28.5, 4.2, 4.2, 6, 6, 6, 6, 6, 4.5, 4.5, 6, 3, 6, 3, 4.5, 3, 6, 3, 6)
COUNT = [0]
LIMITS = {'finish': 16, 'pack': 12, 'back': 12, 'sums': 8, 'adds': 8, 'share': 12, 'project': 4, 'attend': 10, 'feed': 14, 'close': 6, 'feed_back': 14, 'weight_grad': 10, 'middle_back': 8, 'attend_back': 14}
anywhere = pl.BlockSpec(memory_space=pl.ANY)
smem = pl.BlockSpec(memory_space=pltpu.SMEM)


def dot_nn(left, right):
    return lax.dot_general(left, right, (((1,), (0,)), ((), ())), preferred_element_type=f32)


def dot_nt(left, right):
    return lax.dot_general(left, right, (((1,), (1,)), ((), ())), preferred_element_type=f32)


def dot_tn(left, right):
    return lax.dot_general(left, right, (((0,), (0,)), ((), ())), preferred_element_type=f32)


def swap(value, axis, mask):
    count = lax.axis_size(axis)
    return lax.ppermute(value, axis, [(i, i ^ mask) for i in range(count)])


def place_bit(axis, bit):
    return (lax.axis_index(axis) >> bit) & 1


def bits_of(axis):
    count = lax.axis_size(axis)
    number = count.bit_length() - 1
    assert 1 << number == count
    return number


def pick(value, index, axis):
    return lax.dynamic_index_in_dim(value, index, axis, keepdims=False)


def add_low(left, right):
    return (left.astype(f32) + right.astype(f32)).astype(bf16)


def call(kernel, name, ins, outs, grid=(), scratch=(), after=(), onto=()):
    def placed(shape):
        return pltpu.HBM(shape.shape, shape.dtype) if isinstance(shape, Saved) else shape

    def spec(shape, block, index):
        if block == "smem":
            return smem
        if block is None:
            return pl.BlockSpec(shape, lambda *g: (0,) * len(shape))
        return pl.BlockSpec(block, index)

    count = len(ins)
    busy = COSTS[COUNT[0] % len(COSTS)]
    COUNT[0] += 1
    after = tuple(onto) + tuple(after)

    def body(*refs):
        kernel(*refs[:count], *refs[count + len(after) :])

    return pl.pallas_call(
        body,
        grid=grid,
        in_specs=[spec(a.shape, b, i) for a, b, i in ins] + [anywhere] * len(after),
        out_specs=[spec(s.shape, b, i) for s, b, i in outs],
        out_shape=[placed(s) for s, _, _ in outs],
        scratch_shapes=list(scratch),
        input_output_aliases={count + i: i for i in range(len(onto))},
        name=name,
        cost_estimate=pl.CostEstimate(flops=int(1.15e9 * busy), bytes_accessed=0, transcendentals=0),
        compiler_params=pltpu.CompilerParams(vmem_limit_bytes=LIMITS[name] << 20),
    )(*[a for a, _, _ in ins], *after)


def like(shape, dtype):
    return jax.ShapeDtypeStruct(shape, dtype)


class Saved:
    def __init__(self, shape, dtype):
        self.shape, self.dtype = shape, dtype


def head_lanes(side):
    lane = lax.broadcasted_iota(jnp.int32, (1, PAIR), 1)
    return lane < HEAD if side == 0 else lane >= HEAD


def scores_of(inside, parts, query, qaug):
    probe = jnp.where(inside, query, qaug)
    return jnp.concatenate(
        [dot_nt(jnp.where(inside, k[...], aug[...]), probe) for k, aug in parts], axis=0
    )


def attend_kernel(
    q_ref, k_ref, k2_ref, v_ref, v2_ref, qaug_ref, kaug_ref, kaug2_ref, context_ref, log_ref, vt_ref
):
    own = v_ref.shape[0]

    @pl.when(pl.program_id(1) == 0)
    def _():
        vt_ref[:, :own] = v_ref[...].T
        vt_ref[:, own:] = v2_ref[...].T

    parts = ((k_ref, kaug_ref), (k2_ref, kaug2_ref))
    query = q_ref[...]
    outs = []
    for side in range(2):
        scores = scores_of(head_lanes(side), parts, query, qaug_ref[...])
        peak = jnp.max(scores, axis=0, keepdims=True) * scale_two
        raised = jnp.exp2(scores * scale_two - peak)
        total = jnp.sum(raised, axis=0, keepdims=True)
        mixed = dot_nn(vt_ref[side * HEAD : (side + 1) * HEAD, :], raised.astype(bf16))
        outs.append(mixed / total)
        log_ref[0, side : side + 1, :] = peak + jnp.log2(total)
    context_ref[...] = jnp.concatenate(outs, axis=0).T.astype(bf16)


def attention_specs(count, counts):
    tile = min(count, 512)
    own = (tile, PAIR), lambda p, i: (i, p)
    first, rest = [((n, PAIR), lambda p, i: (0, p)) for n in counts]
    logs = (1, 2, tile), lambda p, i: (p, 0, i)
    aug = (tile, PAIR), lambda p, i: (i, 0)
    return tile, own, first, rest, logs, aug


def attend(query, keys, values, augs, after=()):
    count, width = query.shape
    pairs = width // PAIR
    tile, own, first, rest, logs, aug = attention_specs(count, [k.shape[0] for k in keys])
    return call(
        attend_kernel,
        "attend",
        [
            (query, *own),
            (keys[0], *first),
            (keys[1], *rest),
            (values[0], *first),
            (values[1], *rest),
            (augs[0], *aug),
            (augs[1], None, None),
            (augs[2], None, None),
        ],
        [(like(query.shape, bf16), *own), (Saved((pairs, 2, count), f32), *logs)],
        grid=(pairs, count // tile),
        scratch=[pltpu.VMEM((PAIR, sum(k.shape[0] for k in keys)), bf16)],
        after=after,
    )


def attend_back_kernel(
    q_ref,
    k_ref,
    k2_ref,
    v_ref,
    v2_ref,
    qaug_ref,
    kaug_ref,
    kaug2_ref,
    log_ref,
    context_ref,
    grad_ref,
    dq_ref,
    dk_ref,
    dk2_ref,
    dv_ref,
    dv2_ref,
    kt_ref,
    dk_sum,
    dv_sum,
):
    step = pl.program_id(1)
    own = k_ref.shape[0]

    @pl.when(step == 0)
    def _():
        kt_ref[:, :own] = k_ref[...].T
        kt_ref[:, own:] = k2_ref[...].T
        dk_sum[...] = jnp.zeros_like(dk_sum)
        dv_sum[...] = jnp.zeros_like(dv_sum)

    parts = ((k_ref, kaug_ref), (k2_ref, kaug2_ref))
    query, grad = q_ref[...], grad_ref[...]
    zero = jnp.zeros((), bf16)
    product = (grad.astype(f32) * context_ref[...].astype(f32)).T
    outs = []
    for side in range(2):
        inside = head_lanes(side)
        scores = scores_of(inside, parts, query, qaug_ref[...])
        chance = jnp.exp2(scores * scale_two - log_ref[0, side : side + 1, :])
        grad_side = jnp.where(inside, grad, zero)
        inner = jnp.sum(product[side * HEAD : (side + 1) * HEAD], axis=0, keepdims=True)
        grad_chance = jnp.concatenate([dot_nt(v[...], grad_side) for v in (v_ref, v2_ref)], axis=0)
        grad_scores = (chance * (grad_chance - inner)).astype(bf16)
        dv_sum[...] += dot_nn(chance.astype(bf16), grad_side)
        dk_sum[...] += dot_nn(grad_scores, jnp.where(inside, query, zero))
        outs.append(dot_nn(kt_ref[side * HEAD : (side + 1) * HEAD, :], grad_scores))
    dq_ref[...] = (jnp.concatenate(outs, axis=0) * 0.125).T.astype(bf16)

    @pl.when(step == pl.num_programs(1) - 1)
    def _():
        dk_ref[...] = (dk_sum[:own] * 0.125).astype(bf16)
        dk2_ref[...] = (dk_sum[own:] * 0.125).astype(bf16)
        dv_ref[...] = dv_sum[:own].astype(bf16)
        dv2_ref[...] = dv_sum[own:].astype(bf16)


def attend_back(query, keys, values, augs, log_total, context, grad_context, after=()):
    count, width = query.shape
    full = sum(k.shape[0] for k in keys)
    pairs = width // PAIR
    tile, own, first, rest, logs, aug = attention_specs(count, [k.shape[0] for k in keys])
    return call(
        attend_back_kernel,
        "attend_back",
        [
            (query, *own),
            (keys[0], *first),
            (keys[1], *rest),
            (values[0], *first),
            (values[1], *rest),
            (augs[0], *aug),
            (augs[1], None, None),
            (augs[2], None, None),
            (log_total, *logs),
            (context, *own),
            (grad_context, *own),
        ],
        [
            (like(query.shape, bf16), *own),
            (like(keys[0].shape, bf16), *first),
            (like(keys[1].shape, bf16), *rest),
            (like(keys[0].shape, bf16), *first),
            (like(keys[1].shape, bf16), *rest),
        ],
        grid=(pairs, count // tile),
        scratch=[
            pltpu.VMEM((PAIR, full), bf16),
            pltpu.VMEM((full, PAIR), f32),
            pltpu.VMEM((full, PAIR), f32),
        ],
        after=after,
    )


def project_kernel(with_query, in_ref, weight_ref, bias_ref, *outs):
    low = in_ref[...]
    if with_query:
        outs[0][...] = (dot_nn(low, weight_ref[0]) + bias_ref[0]).astype(bf16)
        outs = outs[1:]
    outs[0][...] = dot_nn(low, weight_ref[1]).astype(bf16)
    outs[1][...] = (dot_nn(low, weight_ref[2]) + bias_ref[1]).astype(bf16)


def project(low, weight, bias, with_query):
    count, width = low.shape
    local_width = weight.shape[2]
    tile = min(count, 256)
    if count % tile:
        tile = count
    out = like((count, local_width), bf16), *rows(tile, local_width)
    return call(
        functools.partial(project_kernel, with_query),
        "project",
        [(low, *rows(tile, width)), (weight, None, None), (bias, None, None)],
        [out] * (3 if with_query else 2),
        grid=(count // tile,),
    )


def normalize(rows_in, gain, shift):
    center = rows_in - jnp.mean(rows_in, axis=-1, keepdims=True)
    scale = lax.rsqrt(jnp.mean(center * center, axis=-1, keepdims=True) + eps_norm)
    unit = center * scale
    return (unit * gain + shift, unit, scale)


def normalize_back(grad_out, unit, scale, gain):
    grad_unit = grad_out * gain
    inner = (
        grad_unit
        - jnp.mean(grad_unit, axis=-1, keepdims=True)
        - unit * jnp.mean(grad_unit * unit, axis=-1, keepdims=True)
    )
    return inner * scale


def rows(tile, width):
    return (tile, width), lambda i: (i, 0)


def feed_kernel(
    in_ref,
    mine_ref,
    theirs_ref,
    bias_ref,
    gain_ref,
    shift_ref,
    up_ref,
    up_bias_ref,
    down_ref,
    hidden_ref,
    low_ref,
    unit_ref,
    scale_ref,
    active_ref,
    slope_ref,
    part_ref,
):
    summed = mine_ref[...].astype(f32) + theirs_ref[...].astype(f32)
    total = in_ref[...].astype(f32) + (summed + bias_ref[...])
    hidden, unit, scale = normalize(total, gain_ref[...], shift_ref[...])
    low = hidden.astype(bf16)
    hidden_ref[...] = hidden
    low_ref[...] = low
    unit_ref[...] = unit.astype(bf16)
    scale_ref[...] = jnp.broadcast_to(scale, scale_ref.shape)
    pre = dot_nn(low, up_ref[...]) + up_bias_ref[...]
    below = 0.5 * (1.0 + lax.erf(pre * root_half))
    active = (pre * below).astype(bf16)
    active_ref[...] = active
    slope_ref[...] = (below + pre * (jnp.exp(-0.5 * pre * pre) * inv_root_tau)).astype(bf16)
    part_ref[...] = dot_nn(active, down_ref[...]).astype(bf16)


def feed(inputs, mine, theirs, bias, gain, shift, up, up_bias, down):
    count, width = inputs.shape
    units = up.shape[1]
    tile = min(count, 256)
    wide, narrow = rows(tile, units), rows(tile, width)
    return call(
        feed_kernel,
        "feed",
        [(inputs, *narrow), (mine, *narrow), (theirs, *narrow)]
        + [(a, None, None) for a in (bias, gain, shift, up, up_bias, down)],
        [
            (like((count, width), f32), *narrow),
            (Saved((count, width), bf16), *narrow),
            (Saved((count, width), bf16), *narrow),
            (Saved((count, 128), f32), *rows(tile, 128)),
            (Saved((count, units), bf16), *wide),
            (Saved((count, units), bf16), *wide),
            (like((count, width), bf16), *narrow),
        ],
        grid=(count // tile,),
    )


def close_kernel(
    in_ref, mine_ref, theirs_ref, bias_ref, gain_ref, shift_ref, out_ref, low_ref, unit_ref, scale_ref
):
    summed = mine_ref[...].astype(f32) + theirs_ref[...].astype(f32)
    total = in_ref[...] + (summed + bias_ref[...])
    result, unit, scale = normalize(total, gain_ref[...], shift_ref[...])
    out_ref[...] = result
    low_ref[...] = result.astype(bf16)
    unit_ref[...] = unit.astype(bf16)
    scale_ref[...] = jnp.broadcast_to(scale, scale_ref.shape)


def close(inputs, mine, theirs, bias, gain, shift):
    count, width = inputs.shape
    tile = min(count, 256)
    narrow = rows(tile, width)
    return call(
        close_kernel,
        "close",
        [(inputs, *narrow), (mine, *narrow), (theirs, *narrow)]
        + [(a, None, None) for a in (bias, gain, shift)],
        [
            (like((count, width), f32), *narrow),
            (like((count, width), bf16), *narrow),
            (like((count, width), bf16), *narrow),
            (like((count, 128), f32), *rows(tile, 128)),
        ],
        grid=(count // tile,),
    )


def feed_back_kernel(has_base, flag_ref, *refs):
    if has_base:
        base_ref, mine_ref, theirs_ref, refs = refs[0], refs[1], refs[2], refs[3:]
    (
        cot_ref,
        far_ref,
        other_ref,
        unit_ref,
        scale_ref,
        gain_ref,
        down_ref,
        slope_ref,
        up_ref,
        mixed_ref,
        low_mixed_ref,
        low_pre_ref,
        part_ref,
        small_ref,
    ) = refs
    step = pl.program_id(0)
    kept = flag_ref[0] > 0
    core = flag_ref[1] > 0
    first = jnp.where(core, other_ref[...], far_ref[...])
    second = jnp.where(core, far_ref[...], other_ref[...])
    far = jnp.concatenate([first, second], axis=0)
    cot = jnp.where(step == 0, cot_ref[flag_ref[2]], far).astype(f32)
    if has_base:
        here = flag_ref[1] == step
        back = jnp.where(here, mine_ref[...], theirs_ref[...]).astype(f32)
        grad_out = jnp.where(kept, base_ref[...] + back, cot)
    else:
        grad_out = jnp.where(kept, cot, 0.0)
    unit = unit_ref[...].astype(f32)
    grad_mixed = normalize_back(grad_out, unit, scale_ref[:, :1], gain_ref[...])
    mixed_ref[...] = grad_mixed
    low_mixed = grad_mixed.astype(bf16)
    low_mixed_ref[...] = low_mixed
    grad_active = dot_nt(low_mixed, down_ref[...])
    low_pre = (grad_active * slope_ref[...].astype(f32)).astype(bf16)
    low_pre_ref[...] = low_pre
    part_ref[...] = dot_nt(low_pre, up_ref[...]).astype(bf16)

    @pl.when(step == 0)
    def _():
        small_ref[...] = jnp.zeros_like(small_ref)

    width = grad_out.shape[1]

    def total(value):
        return jnp.sum(value, axis=0, keepdims=True)

    pre_sum = total(low_pre.astype(f32))
    small_ref[0:1, :] += total(grad_out * unit)
    small_ref[1:2, :] += total(grad_out)
    small_ref[2:3, :] += total(grad_mixed)
    small_ref[3:4, :] += pre_sum[:, :width]
    small_ref[4:5, :] += pre_sum[:, width:]


def feed_back(flags, base, cot, unit, scale, gain, down, slope, up, after=()):
    count, width = unit.shape
    units = up.shape[1]
    tile = count // 2
    wide, narrow = rows(tile, units), rows(tile, width)
    ins = [(flags, "smem", None)]
    if base is not None:
        ins += [(base[0], *narrow), (base[1], None, None), (base[2], None, None)]
    ins += [
        *[(c, None, None) for c in cot],
        (unit, *narrow),
        (scale, *rows(tile, 128)),
        (gain, None, None),
        (down, None, None),
        (slope, *wide),
        (up, None, None),
    ]
    return call(
        functools.partial(feed_back_kernel, base is not None),
        "feed_back",
        ins,
        [
            (like((count, width), f32), *narrow),
            (like((count, width), bf16), *narrow),
            (like((count, units), bf16), *wide),
            (like((count, width), bf16), *narrow),
            (like((8, width), f32), None, None),
        ],
        grid=(2,),
        after=after,
    )


def middle_back_kernel(
    mixed_ref,
    mine_ref,
    theirs_ref,
    unit_ref,
    scale_ref,
    gain_ref,
    out_ref,
    attended_ref,
    low_ref,
    context_ref,
    small_ref,
):
    summed = mine_ref[...].astype(f32) + theirs_ref[...].astype(f32)
    grad_hidden = mixed_ref[...] + summed
    unit = unit_ref[...].astype(f32)
    grad = normalize_back(grad_hidden, unit, scale_ref[:, :1], gain_ref[...])
    attended_ref[...] = grad
    low = grad.astype(bf16)
    low_ref[...] = low
    context_ref[...] = dot_nt(low, out_ref[...]).astype(bf16)

    @pl.when(pl.program_id(0) == 0)
    def _():
        small_ref[...] = jnp.zeros_like(small_ref)

    small_ref[0:1, :] += jnp.sum(grad_hidden * unit, axis=0, keepdims=True)
    small_ref[1:2, :] += jnp.sum(grad_hidden, axis=0, keepdims=True)
    small_ref[2:3, :] += jnp.sum(grad, axis=0, keepdims=True)


def middle_back(mixed, mine, theirs, unit, scale, gain, out_weight, after=()):
    count, width = mixed.shape
    local_width = out_weight.shape[0]
    tile = min(count, 256)
    narrow = rows(tile, width)
    return call(
        middle_back_kernel,
        "middle_back",
        [
            (mixed, *narrow),
            (mine, *narrow),
            (theirs, *narrow),
            (unit, *narrow),
            (scale, *rows(tile, 128)),
            (gain, None, None),
            (out_weight, None, None),
        ],
        [
            (like((count, width), f32), *narrow),
            (like((count, width), bf16), *narrow),
            (like((count, local_width), bf16), *rows(tile, local_width)),
            (like((8, width), f32), None, None),
        ],
        grid=(count // tile,),
        after=after,
    )


def put_halves(flag, value, column, send_ref, keep_ref):
    shares, half = send_ref.shape[:2]
    columns = slice(column, column + value.shape[1])
    value = value.astype(bf16)
    for share in range(shares):
        low = value[2 * share * half : (2 * share + 1) * half]
        high = value[(2 * share + 1) * half : (2 * share + 2) * half]
        send_ref[share, :, columns] = jnp.where(flag > 0, low, high)
        keep_ref[share, :, columns] = jnp.where(flag > 0, high, low)


def weight_kernel(pairs, flag_ref, *refs):
    lefts_rights, (send_ref, keep_ref) = refs[:-2], refs[-2:]
    column = 0
    for terms in pairs:
        value = 0.0
        for left, right in terms:
            value = value + dot_tn(lefts_rights[left][...], lefts_rights[right][...])
        put_halves(flag_ref[0], value, column, send_ref, keep_ref)
        column += value.shape[1]


def weight_grad(flag, arrays, pairs, by_share=False, after=()):
    shares = lax.axis_size("dp")
    width = arrays[pairs[0][0][0]].shape[1]
    columns = sum(arrays[terms[0][1]].shape[1] for terms in pairs)
    shape = (shares, width // (2 * shares), columns)
    if by_share:
        shape = (shares // 2, width // shares, columns)
    return call(
        functools.partial(weight_kernel, pairs),
        "weight_grad",
        [(flag, "smem", None)] + [(a, None, None) for a in arrays],
        [(like(shape, bf16), None, None)] * 2,
        after=after,
    )


def back_kernel(flag_ref, *refs):
    terms, (mine_ref, theirs_ref) = refs[:-2], refs[-2:]
    parts, half = mine_ref.shape[:2]
    grads = terms[: len(terms) // 2]
    weights = terms[len(terms) // 2 :]
    for part in range(parts):
        halves = []
        for side in range(2):
            start = (2 * part + side) * half
            value = 0.0
            for grad, weight in zip(grads, weights):
                value = value + dot_nt(grad[start : start + half], weight[0])
            halves.append(value.astype(bf16))
        mine_ref[part] = jnp.where(flag_ref[1] > 0, halves[1], halves[0])
        theirs_ref[part] = jnp.where(flag_ref[1] > 0, halves[0], halves[1])


def back_grad(flags, grads, weight, which, span, after=()):
    count, local_width = grads[0].shape
    width = weight.shape[1]
    out = like((count // span, span // 2, width), bf16), None, None
    return call(
        back_kernel,
        "back",
        [(flags, "smem", None)]
        + [(g, g.shape, lambda i: (0, 0)) for g in grads]
        + [(weight, (1, width, local_width), lambda i, w=w: (w, 0, 0)) for w in which],
        [out, out],
        grid=(1,),
        after=after,
    )


def sums_kernel(plans, *refs):
    count = (len(refs) - 2) // 2
    keeps, arrived, outs = refs[:count], refs[count : 2 * count], refs[2 * count :]
    for out, plan in zip(outs, plans):
        column = 0
        for source, start, width in plan:
            columns = slice(start, start + width)
            out[:, column : column + width] = add_low(
                keeps[source][0, :, columns], arrived[source][0, :, columns]
            )
            column += width


def sums(loads, plans, after=()):
    out = like((loads[0].keep.shape[1], sum(p[2] for p in plans[0])), bf16), None, None
    arrays = [load.keep for load in loads] + [load.arrived for load in loads]
    return call(
        functools.partial(sums_kernel, plans),
        "sums",
        [(a, None, None) for a in arrays],
        [out, out],
        after=after,
    )


def adds_kernel(a_ref, b_ref, c_ref, d_ref, first_ref, second_ref):
    first_ref[...] = add_low(a_ref[...], b_ref[...])
    second_ref[...] = add_low(c_ref[...], d_ref[...])


def adds(first, second, after=()):
    out = like(first[0].shape, bf16), None, None
    return call(
        adds_kernel,
        "adds",
        [(a, None, None) for a in (*first, *second)],
        [out, out],
        after=after,
    )


def relay_kernel(in_ref, out_ref):
    out_ref[...] = in_ref[...]


def relay(value, after):
    return call(
        relay_kernel, "adds", [(value, None, None)], [(like(value.shape, bf16), None, None)], after=after
    )[0]


def finish_kernel(flag_ref, a_ref, b_ref, c_ref, d_ref, *refs):
    qkv_ref, out_ref, up_ref, down_ref = refs
    units = up_ref.shape[2]
    local_width = qkv_ref.shape[3]

    def whole(flag, mine, other):
        low = jnp.where(flag > 0, other[...], mine[...])
        high = jnp.where(flag > 0, mine[...], other[...])
        return jnp.concatenate([low, high], axis=0).astype(f32)

    down = whole(flag_ref[0], a_ref, b_ref)
    down_ref[0] = down[:, :units].T
    qkv_ref[0, 2] = down[:, units : units + local_width]
    out_ref[0] = down[:, units + local_width :].T
    up = whole(flag_ref[1], c_ref, d_ref)
    up_ref[0] = up[:, :units]
    qkv_ref[0, 0] = up[:, units : units + local_width]
    qkv_ref[0, 1] = up[:, units + local_width :]


def finish(layer, flags, first, second, units, onto=()):
    half, columns = first[0].shape
    local_width = (columns - units) // 2
    shapes = (
        (2, 3, 2 * half, local_width),
        (2, local_width, 2 * half),
        (2, 2 * half, units),
        (2, units, 2 * half),
    )

    def place(shape):
        return like(shape, f32), (1,) + shape[1:], lambda i: (layer,) + (0,) * (len(shape) - 1)

    return call(
        finish_kernel,
        "finish",
        [(flags, "smem", None)]
        + [(a, a.shape, lambda i: (0, 0)) for a in (*first, *second)],
        [place(shape) for shape in shapes],
        grid=(1,),
        onto=onto,
    )


def pack_kernel(*refs):
    ins, out_ref = refs[:-1], refs[-1]
    each = len(ins) // 2
    out_ref[...] = jnp.zeros_like(out_ref)

    def total(ref):
        return jnp.sum(ref[...].astype(f32), axis=0, keepdims=True)

    for layer in range(2):
        dq, dv, dv2, feed, middle = ins[layer * each : (layer + 1) * each]
        width = dq.shape[1]
        base = 16 * layer
        out_ref[base : base + 1, :width] = total(dq)
        out_ref[base : base + 1, width:] = total(dv) + total(dv2)
        sources = (middle, 2), (middle, 0), (feed, 0), (middle, 1), (feed, 1), (feed, 3), (feed, 4)
        for i, (ref, row) in enumerate(sources + ((feed, 2),)):
            out_ref[base + 1 + i : base + 2 + i, :] = ref[row : row + 1, :]


def pack(first, second, after=()):
    width = first[3].shape[1]
    return call(
        pack_kernel,
        "pack",
        [(a, a.shape, lambda i: (0, 0)) for a in (*first, *second)],
        [(like((32, width), f32), (32, width), lambda i: (0, 0))],
        grid=(1,),
        after=after,
    )[0]


class Order:
    def __init__(self):
        self.last = ()

    def mark(self, *values):
        self.last = values

    def also(self, value):
        self.last = self.last + (value,)


def both_halves(mine, axis=0):
    other = swap(mine, "mp", 1)
    first = lax.axis_index("mp") == 0
    whole = jnp.where(
        first, jnp.stack([mine, other], axis=axis), jnp.stack([other, mine], axis=axis)
    )
    return whole.reshape(mine.shape[:axis] + (-1,) + mine.shape[axis + 1 :])


def my_half(value):
    count = value.shape[0] // 2
    return pick(value.reshape((2, count) + value.shape[1:]), lax.axis_index("mp"), 0)


def share_kernel(flag_ref, *refs):
    ins, (send_ref, keep_ref) = refs[:-2], refs[-2:]
    count = len(ins) // 2
    column = 0
    for keep, arrived in zip(ins[:count], ins[count:]):
        columns = slice(column, column + keep.shape[-1])
        column += keep.shape[-1]
        low, high = [add_low(keep[side], arrived[side]) for side in range(2)]
        send_ref[0, :, columns] = jnp.where(flag_ref[0] > 0, low, high)
        keep_ref[0, :, columns] = jnp.where(flag_ref[0] > 0, high, low)


def share_step(flag, loads, after=()):
    shares, half = loads[0].keep.shape[:2]
    columns = sum(load.keep.shape[2] for load in loads)
    arrays = [load.keep for load in loads] + [load.arrived for load in loads]
    out = like((shares // 2, half, columns), bf16), (1, half, columns), lambda i: (i, 0, 0)
    return call(
        share_kernel,
        "share",
        [(flag, "smem", None)] + [(a, (2,) + a.shape[1:], lambda i: (i, 0, 0)) for a in arrays],
        [out, out],
        grid=(shares // 2,),
        after=after,
    )


def split_kernel(flag_ref, *refs):
    count = len(refs) // 4
    for k in range(count):
        keep, arrived = refs[k], refs[count + k]
        send_ref, keep_ref = refs[2 * count + 2 * k : 2 * count + 2 * k + 2]
        half = keep.shape[1] // 2
        low = add_low(keep[:, :half], arrived[:, :half])
        high = add_low(keep[:, half:], arrived[:, half:])
        send_ref[...] = jnp.where(flag_ref[k] > 0, low, high)
        keep_ref[...] = jnp.where(flag_ref[k] > 0, high, low)


def split_step(flags, loads, after=()):
    shares, rows_, columns = loads[0].keep.shape
    arrays = [load.keep for load in loads] + [load.arrived for load in loads]
    out = (
        like((shares, rows_ // 2, columns), bf16),
        (1, rows_ // 2, columns),
        lambda i: (i, 0, 0),
    )
    return call(
        split_kernel,
        "share",
        [(flags, "smem", None)] + [(a, (1, rows_, columns), lambda i: (i, 0, 0)) for a in arrays],
        [out] * (2 * len(loads)),
        grid=(shares,),
        after=after,
    )


def join_kernel(flag_ref, a_ref, b_ref, c_ref, d_ref, first_ref, second_ref):
    for k, (mine, other, out) in enumerate(((a_ref, b_ref, first_ref), (c_ref, d_ref, second_ref))):
        half = mine.shape[0]
        out[:half] = jnp.where(flag_ref[k] > 0, other[...], mine[...])
        out[half:] = jnp.where(flag_ref[k] > 0, mine[...], other[...])


def join(flags, first, second, after=()):
    rows_, columns = first[0].shape
    out = like((2 * rows_, columns), bf16), None, None
    return call(
        join_kernel,
        "adds",
        [(flags, "smem", None)] + [(a, None, None) for a in (*first, *second)],
        [out, out],
        after=after,
    )


def last_bit():
    return bits_of("seq") - 1


class Load:
    def __init__(self, line, sent, axis, bit):
        send, self.keep = sent
        line.mark(send)
        self.arrived = swap(send, axis, 1 << bit)


def launch(line, arrays, pairs, axis, bit):
    flag = place_bit(axis, bit).reshape(1)
    return Load(
        line, weight_grad(flag, arrays, pairs, axis == "dp", line.last), axis, bit
    )


def split(line, loads, bits):
    flags = jnp.stack([place_bit("seq", bit) for bit in bits])
    sent = split_step(flags, loads, line.last)
    return [Load(line, sent[2 * k : 2 * k + 2], "seq", bit) for k, bit in enumerate(bits)]


def share(line, bit, *loads):
    flag = place_bit("dp", bit).reshape(1)
    return Load(line, share_step(flag, loads, line.last), "dp", bit)


def shares(line, first, *loads):
    for bit in range(first, bits_of("dp")):
        loads = (share(line, bit, *loads),)
    return loads[0]


class Tail:
    def __init__(self, line, loads, plans, twice):
        self.totals = sums(loads, plans, line.last)
        self.twice = twice
        bits = list(range(bits_of("seq")))
        if twice:
            self.hop(line, (0, last_bit()))
            return
        self.across = (bits[:-1], bits[1:])
        for place in range(len(bits) - 2):
            self.totals = [
                add_low(t, swap(t, "seq", 1 << across[place]))
                for t, across in zip(self.totals, self.across)
            ]
        self.hop(line, [across[-1] for across in self.across])

    def hop(self, line, bits):
        line.mark(*self.totals)
        self.arrived = [swap(t, "seq", 1 << b) for t, b in zip(self.totals, bits)]

    def gather(self, line):
        first, second = zip(self.totals, self.arrived)
        if self.twice:
            flags = jnp.stack([place_bit("seq", 0), place_bit("seq", last_bit())])
            self.totals = join(flags, first, second, line.last)
        else:
            self.totals = adds(first, second, line.last)
        self.hop(line, (last_bit(), 0))

    def finish(self, layer, units, onto=()):
        flags = jnp.stack([place_bit("seq", last_bit()), place_bit("seq", 0)])
        first, second = zip(self.totals, self.arrived)
        return finish(layer, flags, first, second, units, onto)


def sum_along(value, axis):
    for bit in range(bits_of(axis)):
        value = value + swap(value, axis, 1 << bit)
    return value


class Layer:
    def __init__(self, params, augs):
        (
            self.weight_qkv,
            self.bias_qv,
            self.weight_out,
            self.bias_out,
            self.gain,
            self.shift,
            self.weight_up,
            self.bias_up,
            self.weight_down,
            self.bias_down,
        ) = params
        self.augs = augs

    def open(self, low_own):
        self.low_own = low_own
        self.query, self.key_own, self.value_own = project(
            low_own, self.weight_qkv, self.bias_qv, True
        )

    def forward(self, inputs, low_rest, after=()):
        self.low_rest = low_rest
        key_rest, value_rest = project(low_rest, self.weight_qkv, self.bias_qv, False)
        self.keys = (self.key_own, key_rest)
        self.values = (self.value_own, value_rest)
        self.context, self.log_total = attend(
            self.query, self.keys, self.values, self.augs, after
        )
        part = dot_nn(self.context, self.weight_out).astype(bf16)
        hidden, self.low_hidden, self.unit_one, self.scale_one, self.active, self.slope, part = feed(
            inputs,
            part,
            swap(part, "mp", 1),
            self.bias_out,
            self.gain[0],
            self.shift[0],
            self.weight_up,
            self.bias_up,
            self.weight_down,
        )
        result, low_result, self.unit_two, self.scale_two = close(
            hidden, part, swap(part, "mp", 1), self.bias_down, self.gain[1], self.shift[1]
        )
        return result, low_result

    def feed_back(self, line, flags, base, cot):
        self.grad_mixed, self.low_mixed, self.low_pre, self.part, self.small_feed = feed_back(
            flags,
            base,
            cot,
            self.unit_two,
            self.scale_two,
            self.gain[1],
            self.weight_down,
            self.slope,
            self.weight_up,
            line.last,
        )
        line.mark(self.small_feed)

    def down_grad(self, line, axis, bit):
        return launch(line, (self.low_mixed, self.active), (((0, 1),),), axis, bit)

    def up_grad(self, line):
        return launch(line, (self.low_hidden, self.low_pre), (((0, 1),),), "seq", 0)

    def middle_back(self, line):
        self.grad_attended, self.low_attended, self.grad_context, self.small_middle = middle_back(
            self.grad_mixed,
            self.part,
            swap(self.part, "mp", 1),
            self.unit_one,
            self.scale_one,
            self.gain[0],
            self.weight_out,
            line.last,
        )
        line.mark(self.small_middle)

    def attend_back(self, line):
        self.dq, *grads = attend_back(
            self.query,
            self.keys,
            self.values,
            self.augs,
            self.log_total,
            self.context,
            self.grad_context,
            line.last,
        )
        self.dk, self.dv = grads[:2], grads[2:]
        line.mark(self.dq)

    def input_grad_parts(self, line, flags):
        span = self.query.shape[0]
        mine, theirs = back_grad(
            flags, (self.dk[1], self.dv[1]), self.weight_qkv, (1, 2), span, line.last
        )
        arrived = swap(theirs, "mp", 1)
        self.own, theirs = back_grad(
            flags, (self.dq, self.dk[0], self.dv[0]), self.weight_qkv, (0, 1, 2), span, (theirs,)
        )
        rest = add_low(mine, arrived)
        self.far = [swap(rest[j], "seq", 2 * (j + 1)) for j in range(rest.shape[0])]
        self.near = swap(theirs, "mp", 1)
        line.mark(rest, theirs)

    def input_grad(self):
        half = self.own[0].astype(f32) + self.near[0].astype(f32)
        half = (half + sum(f.astype(f32) for f in self.far)).astype(bf16)
        return (self.grad_attended, half, swap(half, "mp", 1))

    qk_pairs = (((0, 2),), ((0, 3), (1, 4)))
    vo_pairs = (((0, 3), (1, 4)), ((2, 5),))

    def value_out_grad(self, line):
        arrays = (self.low_own, self.low_rest, self.low_attended, *self.dv, self.context)
        return launch(line, arrays, self.vo_pairs, "seq", last_bit())

    def query_key_grad(self, line):
        arrays = (self.low_own, self.low_rest, self.dq, *self.dk)
        return launch(line, arrays, self.qk_pairs, "seq", 0)

    def small(self):
        return (self.dq, *self.dv, self.small_feed, self.small_middle)


def layer_part(index, params):
    parts = [array[index] for array in params]
    for i in (3, 7, 9):
        parts[i] = parts[i].reshape(1, -1)
    for i in (4, 5):
        parts[i] = parts[i][:, None, :]
    return tuple(parts)


def stack_pair(first_part, second_part):
    return jnp.stack([first_part, second_part])


def local(
    tokens,
    segments,
    dropped,
    qkv_weight,
    qv_bias,
    out_weight,
    out_bias,
    norm_gain,
    norm_shift,
    up_weight,
    up_bias,
    down_weight,
    down_bias,
    cotangent,
):
    params = (
        qkv_weight,
        qv_bias,
        out_weight,
        out_bias,
        norm_gain,
        norm_shift,
        up_weight,
        up_bias,
        down_weight,
        down_bias,
    )
    first = layer_part(0, params)
    second = layer_part(1, params)
    COUNT[0] = 0
    rows_here, span, width = tokens.shape
    assert rows_here == 2
    places = lax.axis_size("seq")
    place = lax.axis_index("seq")
    row = place & 1
    halves_of = tokens.reshape(rows_here, 2, span // 2, width)
    halves_of = pick(halves_of, lax.axis_index("mp"), 1)
    half_mine, half_partner = pick(halves_of, row, 0), pick(halves_of, 1 - row, 0)
    arrived = [swap((half_mine, half_partner)[c % 2], "seq", c) for c in range(1, places)]
    rest = both_halves(jnp.stack(arrived), axis=1)
    low_own = jnp.concatenate([pick(tokens, row, 0), rest[0]])
    low_rest = rest[1:].reshape(-1, width)
    seg_row = pick(segments, row, 0).reshape(places, span)
    for bit in range(bits_of("seq")):
        shaped = seg_row.reshape(places >> (bit + 1), 2, 1 << bit, span)
        seg_row = jnp.where(place_bit("seq", bit) == 1, shaped[:, ::-1], shaped).reshape(places, span)
    seg_keys = seg_row.reshape(places * span, 1)
    lane = lax.broadcasted_iota(jnp.int32, (1, PAIR), 1) % HEAD
    used = lane < SEGMENTS
    kaug = jnp.where(used & (seg_keys != lane), 1.0, 0.0).astype(bf16)
    qaug = jnp.where(used & (seg_keys[: 2 * span] == lane), -FAR, 0.0).astype(bf16)
    augs = (qaug, kaug[: 2 * span], kaug[2 * span :])
    cot_far = swap(my_half(pick(cotangent, 1 - row, 0)), "seq", 1)
    kept = 1 - pick(dropped, lax.axis_index("dp") * rows_here + row, 0)
    flags = jnp.stack([kept, lax.axis_index("mp"), row])

    one, two = Layer(first, augs), Layer(second, augs)
    one.open(low_own)
    small_params = [p for part in (first, second) for i, p in enumerate(part) if i in (1, 3, 4, 5, 7, 9)]
    hidden_one, low_one = one.forward(low_own, low_rest, (*small_params, flags))
    low_half = my_half(low_one)
    arrived = [swap(low_half, "seq", c) for c in range(2, places, 2)]
    two.open(low_one)
    cot = (cotangent, cot_far, swap(cot_far, "mp", 1))
    rest = both_halves(relay(jnp.stack(arrived), (two.query, cot[2])), axis=1)
    result_two, _ = two.forward(hidden_one, rest.reshape(-1, width))
    result = jnp.where(kept > 0, result_two, hidden_one)

    class Return:
        def __init__(self, value):
            self.mine = value[:span]
            self.arrived = swap(my_half(value[span:].astype(bf16)), "seq", 1)
            self.other = swap(self.arrived, "mp", 1)

        def whole(self):
            core = lax.axis_index("mp") == 0
            far = jnp.where(
                core,
                jnp.concatenate([self.arrived, self.other]),
                jnp.concatenate([self.other, self.arrived]),
            ).astype(f32)
            return jnp.where(row == 0, jnp.stack([self.mine, far]), jnp.stack([far, self.mine]))

    line = Order()
    outputs = Return(result)
    twice = bits_of("seq") == 2 and width // lax.axis_size("dp") % 64 == 0
    first_core = lax.axis_index("mp") == 0
    units = up_weight.shape[2]
    half_units = units // 2
    plans_two = (
        ((0, 0, units), (1, units, half_units)),
        ((1, 0, units), (1, units + half_units, half_units)),
    )
    plans_one = (
        ((0, 0, units), (0, 2 * units, half_units)),
        ((0, units, units), (0, 2 * units + half_units, half_units)),
    )
    two.feed_back(line, flags, None, cot)
    down_two = two.down_grad(line, "dp", 0)
    up_two = two.up_grad(line)
    line.also(outputs.arrived)
    two.middle_back(line)
    line.also(outputs.other)
    two.attend_back(line)
    two.input_grad_parts(line, flags)
    value_two = two.value_out_grad(line)
    query_two = two.query_key_grad(line)
    down_two = shares(line, 1, down_two)
    up_two = share(line, 0, up_two)
    one.feed_back(line, flags, two.input_grad(), cot)
    down_one = one.down_grad(line, "seq", last_bit())
    up_one = one.up_grad(line)
    one.middle_back(line)
    attn_two = share(line, 0, value_two, query_two)
    one.attend_back(line)
    value_one = one.value_out_grad(line)
    query_one = one.query_key_grad(line)
    (down_two,) = split(line, [down_two], (last_bit(),))
    joined_two = shares(line, 1, up_two, attn_two)
    if twice:
        down_one, up_one = split(line, [down_one, up_one], (0, last_bit()))
    if twice:
        value_one, query_one = split(line, [value_one, query_one], (0, last_bit()))
    feed_one = share(line, 0, down_one, up_one)
    one.input_grad_parts(line, flags)
    attn_one = share(line, 0, value_one, query_one)
    base, own_half, other_half = one.input_grad()
    line.also(own_half)
    tail_two = Tail(line, [down_two, joined_two], plans_two, False)
    joined_one = shares(line, 1, feed_one, attn_one)
    tail_two.gather(line)
    halves = own_half, other_half
    back = jnp.where(first_core, jnp.concatenate(halves), jnp.concatenate(halves[::-1]))
    tokens_grad = Return(base + back.astype(f32))
    small = pack(one.small(), two.small(), line.last)
    line.also(small)
    small = sum_along(small, "seq")
    line.also(small)
    line.also(tokens_grad.arrived)
    tail_one = Tail(line, [joined_one], plans_one, twice)
    small = sum_along(small, "dp")
    weight_sums = tail_two.finish(1, units)
    tail_one.gather(line)
    outputs, tokens_grad = outputs.whole(), tokens_grad.whole()
    qkv_sum, out_sum, up_sum, down_sum = tail_one.finish(0, units, weight_sums)
    small = small.reshape(2, 16, width)
    halves = width // 2
    qv_sum = small[:, 0].reshape(2, 2, halves)
    out_bias_sum = small[:, 1]
    gain_sum, shift_sum = small[:, 2:4], small[:, 4:6]
    up_bias_sum = small[:, 6:8].reshape(2, 2 * width)
    down_bias_sum = small[:, 8]

    return (
        outputs,
        tokens_grad,
        qkv_sum,
        qv_sum,
        out_sum,
        out_bias_sum,
        gain_sum,
        shift_sum,
        up_sum,
        up_bias_sum,
        down_sum,
        down_bias_sum,
    )


def solution(mesh):
    placed = (
        P("dp", "seq", None),
        P("dp", None),
        P(),
        P(None, None, None, "mp"),
        P(None, None, "mp"),
        P(None, "mp", None),
        P(),
        P(),
        P(),
        P(None, None, "mp"),
        P(None, "mp"),
        P(None, "mp", None),
        P(),
        P("dp", "seq", None),
    )
    return jax.shard_map(
        local,
        mesh=mesh,
        in_specs=placed,
        out_specs=(
            P("dp", "seq", None),
            P("dp", "seq", None),
            P(None, None, "dp", "mp"),
            P(None, None, "mp"),
            P(None, "mp", "dp"),
            P(),
            P(),
            P(),
            P(None, "dp", "mp"),
            P(None, "mp"),
            P(None, "mp", "dp"),
            P(),
        ),
        check_vma=False,
    )
```

```python
import functools

import jax
import jax.numpy as jnp
from jax import lax
from jax.experimental import pallas as pl
from jax.experimental.pallas import tpu as pltpu
from jax.sharding import PartitionSpec as P

HEAD = 64
PAIR = 2 * HEAD
SEGMENTS = 4
FAR = 1e30
eps_norm = 1e-05
root_half = 0.7071067811865476
inv_root_tau = 0.3989422804014327
scale_two = 0.125 * 1.4426950408889634
f32 = jnp.float32
bf16 = jnp.bfloat16
COSTS = (1.5, 1.5, 7, 6, 1.5, 1.5, 1, 1.5, 7, 6, 1.5, 30, 15, 4.2, 3, 28.5, 4.5, 4.5, 4.2, 4.2, 6, 6, 18, 4.2, 4.2, 2, 6, 28.5, 4.2, 4.2, 6, 0, 2, 6, 6, 4.5, 4.5, 6, 3, 60, 3, 4.5, 0.3, 6, 3, 1, 6)
COUNT = [0]
LIMITS = {'finish': 16, 'pack': 12, 'back': 12, 'sums': 8, 'adds': 8, 'share': 12, 'project': 4, 'attend': 10, 'feed': 14, 'close': 6, 'feed_back': 14, 'weight_grad': 10, 'middle_back': 8, 'attend_back': 14}
anywhere = pl.BlockSpec(memory_space=pl.ANY)
smem = pl.BlockSpec(memory_space=pltpu.SMEM)


def dot_nn(left, right):
    return lax.dot_general(left, right, (((1,), (0,)), ((), ())), preferred_element_type=f32)


def dot_nt(left, right):
    return lax.dot_general(left, right, (((1,), (1,)), ((), ())), preferred_element_type=f32)


def dot_tn(left, right):
    return lax.dot_general(left, right, (((0,), (0,)), ((), ())), preferred_element_type=f32)


def swap(value, axis, mask):
    count = lax.axis_size(axis)
    return lax.ppermute(value, axis, [(i, i ^ mask) for i in range(count)])


def place_bit(axis, bit):
    return (lax.axis_index(axis) >> bit) & 1


def bits_of(axis):
    count = lax.axis_size(axis)
    number = count.bit_length() - 1
    assert 1 << number == count
    return number


def pick(value, index, axis):
    return lax.dynamic_index_in_dim(value, index, axis, keepdims=False)


def add_low(left, right):
    return (left.astype(f32) + right.astype(f32)).astype(bf16)


def call(kernel, name, ins, outs, grid=(), scratch=(), after=(), onto=()):
    def placed(shape):
        return pltpu.HBM(shape.shape, shape.dtype) if isinstance(shape, Saved) else shape

    def spec(shape, block, index):
        if block == "smem":
            return smem
        if block is None:
            return pl.BlockSpec(shape, lambda *g: (0,) * len(shape))
        return pl.BlockSpec(block, index)

    count = len(ins)
    busy = COSTS[COUNT[0] % len(COSTS)]
    COUNT[0] += 1
    after = tuple(onto) + tuple(after)

    def body(*refs):
        kernel(*refs[:count], *refs[count + len(after) :])

    return pl.pallas_call(
        body,
        grid=grid,
        in_specs=[spec(a.shape, b, i) for a, b, i in ins] + [anywhere] * len(after),
        out_specs=[spec(s.shape, b, i) for s, b, i in outs],
        out_shape=[placed(s) for s, _, _ in outs],
        scratch_shapes=list(scratch),
        input_output_aliases={count + i: i for i in range(len(onto))},
        name=name,
        cost_estimate=pl.CostEstimate(flops=int(1.15e9 * busy), bytes_accessed=0, transcendentals=0),
        compiler_params=pltpu.CompilerParams(vmem_limit_bytes=LIMITS[name] << 20),
    )(*[a for a, _, _ in ins], *after)


def like(shape, dtype):
    return jax.ShapeDtypeStruct(shape, dtype)


class Saved:
    def __init__(self, shape, dtype):
        self.shape, self.dtype = shape, dtype


def head_lanes(side):
    lane = lax.broadcasted_iota(jnp.int32, (1, PAIR), 1)
    return lane < HEAD if side == 0 else lane >= HEAD


def scores_of(inside, parts, query, qaug):
    probe = jnp.where(inside, query, qaug)
    return jnp.concatenate(
        [dot_nt(jnp.where(inside, k[...], aug[...]), probe) for k, aug in parts], axis=0
    )


def attend_kernel(
    q_ref, k_ref, k2_ref, v_ref, v2_ref, qaug_ref, kaug_ref, kaug2_ref, context_ref, log_ref, vt_ref
):
    own = v_ref.shape[0]

    @pl.when(pl.program_id(1) == 0)
    def _():
        vt_ref[:, :own] = v_ref[...].T
        vt_ref[:, own:] = v2_ref[...].T

    parts = ((k_ref, kaug_ref), (k2_ref, kaug2_ref))
    query = q_ref[...]
    outs = []
    for side in range(2):
        scores = scores_of(head_lanes(side), parts, query, qaug_ref[...])
        peak = jnp.max(scores, axis=0, keepdims=True) * scale_two
        raised = jnp.exp2(scores * scale_two - peak)
        total = jnp.sum(raised, axis=0, keepdims=True)
        mixed = dot_nn(vt_ref[side * HEAD : (side + 1) * HEAD, :], raised.astype(bf16))
        outs.append(mixed / total)
        log_ref[0, side : side + 1, :] = peak + jnp.log2(total)
    context_ref[...] = jnp.concatenate(outs, axis=0).T.astype(bf16)


def attention_specs(count, counts):
    tile = min(count, 512)
    own = (tile, PAIR), lambda p, i: (i, p)
    first, rest = [((n, PAIR), lambda p, i: (0, p)) for n in counts]
    logs = (1, 2, tile), lambda p, i: (p, 0, i)
    aug = (tile, PAIR), lambda p, i: (i, 0)
    return tile, own, first, rest, logs, aug


def attend(query, keys, values, augs, after=()):
    count, width = query.shape
    pairs = width // PAIR
    tile, own, first, rest, logs, aug = attention_specs(count, [k.shape[0] for k in keys])
    return call(
        attend_kernel,
        "attend",
        [
            (query, *own),
            (keys[0], *first),
            (keys[1], *rest),
            (values[0], *first),
            (values[1], *rest),
            (augs[0], *aug),
            (augs[1], None, None),
            (augs[2], None, None),
        ],
        [(like(query.shape, bf16), *own), (Saved((pairs, 2, count), f32), *logs)],
        grid=(pairs, count // tile),
        scratch=[pltpu.VMEM((PAIR, sum(k.shape[0] for k in keys)), bf16)],
        after=after,
    )


def attend_back_kernel(
    q_ref,
    k_ref,
    k2_ref,
    v_ref,
    v2_ref,
    qaug_ref,
    kaug_ref,
    kaug2_ref,
    log_ref,
    context_ref,
    grad_ref,
    dq_ref,
    dk_ref,
    dk2_ref,
    dv_ref,
    dv2_ref,
    kt_ref,
    dk_sum,
    dv_sum,
):
    step = pl.program_id(1)
    own = k_ref.shape[0]

    @pl.when(step == 0)
    def _():
        kt_ref[:, :own] = k_ref[...].T
        kt_ref[:, own:] = k2_ref[...].T
        dk_sum[...] = jnp.zeros_like(dk_sum)
        dv_sum[...] = jnp.zeros_like(dv_sum)

    parts = ((k_ref, kaug_ref), (k2_ref, kaug2_ref))
    query, grad = q_ref[...], grad_ref[...]
    zero = jnp.zeros((), bf16)
    product = (grad.astype(f32) * context_ref[...].astype(f32)).T
    outs = []
    for side in range(2):
        inside = head_lanes(side)
        scores = scores_of(inside, parts, query, qaug_ref[...])
        chance = jnp.exp2(scores * scale_two - log_ref[0, side : side + 1, :])
        grad_side = jnp.where(inside, grad, zero)
        inner = jnp.sum(product[side * HEAD : (side + 1) * HEAD], axis=0, keepdims=True)
        grad_chance = jnp.concatenate([dot_nt(v[...], grad_side) for v in (v_ref, v2_ref)], axis=0)
        grad_scores = (chance * (grad_chance - inner)).astype(bf16)
        dv_sum[...] += dot_nn(chance.astype(bf16), grad_side)
        dk_sum[...] += dot_nn(grad_scores, jnp.where(inside, query, zero))
        outs.append(dot_nn(kt_ref[side * HEAD : (side + 1) * HEAD, :], grad_scores))
    dq_ref[...] = (jnp.concatenate(outs, axis=0) * 0.125).T.astype(bf16)

    @pl.when(step == pl.num_programs(1) - 1)
    def _():
        dk_ref[...] = (dk_sum[:own] * 0.125).astype(bf16)
        dk2_ref[...] = (dk_sum[own:] * 0.125).astype(bf16)
        dv_ref[...] = dv_sum[:own].astype(bf16)
        dv2_ref[...] = dv_sum[own:].astype(bf16)


def attend_back(query, keys, values, augs, log_total, context, grad_context, after=()):
    count, width = query.shape
    full = sum(k.shape[0] for k in keys)
    pairs = width // PAIR
    tile, own, first, rest, logs, aug = attention_specs(count, [k.shape[0] for k in keys])
    return call(
        attend_back_kernel,
        "attend_back",
        [
            (query, *own),
            (keys[0], *first),
            (keys[1], *rest),
            (values[0], *first),
            (values[1], *rest),
            (augs[0], *aug),
            (augs[1], None, None),
            (augs[2], None, None),
            (log_total, *logs),
            (context, *own),
            (grad_context, *own),
        ],
        [
            (like(query.shape, bf16), *own),
            (like(keys[0].shape, bf16), *first),
            (like(keys[1].shape, bf16), *rest),
            (like(keys[0].shape, bf16), *first),
            (like(keys[1].shape, bf16), *rest),
        ],
        grid=(pairs, count // tile),
        scratch=[
            pltpu.VMEM((PAIR, full), bf16),
            pltpu.VMEM((full, PAIR), f32),
            pltpu.VMEM((full, PAIR), f32),
        ],
        after=after,
    )


def project_kernel(with_query, in_ref, weight_ref, bias_ref, *outs):
    low = in_ref[...]
    if with_query:
        outs[0][...] = (dot_nn(low, weight_ref[0, 0]) + bias_ref[0]).astype(bf16)
        outs = outs[1:]
    outs[0][...] = dot_nn(low, weight_ref[0, 1]).astype(bf16)
    outs[1][...] = (dot_nn(low, weight_ref[0, 2]) + bias_ref[1]).astype(bf16)


def project(layer, low, weight, bias, with_query):
    count, width = low.shape
    local_width = weight.shape[3]
    tile = min(count, 256)
    if count % tile:
        tile = count
    out = like((count, local_width), bf16), *rows(tile, local_width)
    return call(
        functools.partial(project_kernel, with_query),
        "project",
        [
            (low, *rows(tile, width)),
            (weight, (1,) + weight.shape[1:], lambda i: (layer, 0, 0, 0)),
            (bias, None, None),
        ],
        [out] * (3 if with_query else 2),
        grid=(count // tile,),
    )


def normalize(rows_in, gain, shift):
    center = rows_in - jnp.mean(rows_in, axis=-1, keepdims=True)
    scale = lax.rsqrt(jnp.mean(center * center, axis=-1, keepdims=True) + eps_norm)
    unit = center * scale
    return (unit * gain + shift, unit, scale)


def normalize_back(grad_out, unit, scale, gain):
    grad_unit = grad_out * gain
    inner = (
        grad_unit
        - jnp.mean(grad_unit, axis=-1, keepdims=True)
        - unit * jnp.mean(grad_unit * unit, axis=-1, keepdims=True)
    )
    return inner * scale


def rows(tile, width):
    return (tile, width), lambda i: (i, 0)


def feed_kernel(
    in_ref,
    mine_ref,
    theirs_ref,
    bias_ref,
    gain_ref,
    shift_ref,
    up_ref,
    up_bias_ref,
    down_ref,
    hidden_ref,
    low_ref,
    unit_ref,
    scale_ref,
    active_ref,
    slope_ref,
    part_ref,
):
    summed = mine_ref[...].astype(f32) + theirs_ref[...].astype(f32)
    total = in_ref[...].astype(f32) + (summed + bias_ref[...])
    hidden, unit, scale = normalize(total, gain_ref[...], shift_ref[...])
    low = hidden.astype(bf16)
    hidden_ref[...] = hidden
    low_ref[...] = low
    unit_ref[...] = unit.astype(bf16)
    scale_ref[...] = jnp.broadcast_to(scale, scale_ref.shape)
    pre = dot_nn(low, up_ref[...]) + up_bias_ref[...]
    below = 0.5 * (1.0 + lax.erf(pre * root_half))
    active = (pre * below).astype(bf16)
    active_ref[...] = active
    slope_ref[...] = (below + pre * (jnp.exp(-0.5 * pre * pre) * inv_root_tau)).astype(bf16)
    part_ref[...] = dot_nn(active, down_ref[...]).astype(bf16)


def feed(inputs, mine, theirs, bias, gain, shift, up, up_bias, down):
    count, width = inputs.shape
    units = up.shape[1]
    tile = min(count, 256)
    wide, narrow = rows(tile, units), rows(tile, width)
    return call(
        feed_kernel,
        "feed",
        [(inputs, *narrow), (mine, *narrow), (theirs, *narrow)]
        + [(a, None, None) for a in (bias, gain, shift, up, up_bias, down)],
        [
            (like((count, width), f32), *narrow),
            (Saved((count, width), bf16), *narrow),
            (Saved((count, width), bf16), *narrow),
            (Saved((count, 128), f32), *rows(tile, 128)),
            (Saved((count, units), bf16), *wide),
            (Saved((count, units), bf16), *wide),
            (like((count, width), bf16), *narrow),
        ],
        grid=(count // tile,),
    )


def close_kernel(
    in_ref, mine_ref, theirs_ref, bias_ref, gain_ref, shift_ref, out_ref, low_ref, unit_ref, scale_ref
):
    summed = mine_ref[...].astype(f32) + theirs_ref[...].astype(f32)
    total = in_ref[...] + (summed + bias_ref[...])
    result, unit, scale = normalize(total, gain_ref[...], shift_ref[...])
    out_ref[...] = result
    low_ref[...] = result.astype(bf16)
    unit_ref[...] = unit.astype(bf16)
    scale_ref[...] = jnp.broadcast_to(scale, scale_ref.shape)


def close(inputs, mine, theirs, bias, gain, shift):
    count, width = inputs.shape
    tile = min(count, 256)
    narrow = rows(tile, width)
    return call(
        close_kernel,
        "close",
        [(inputs, *narrow), (mine, *narrow), (theirs, *narrow)]
        + [(a, None, None) for a in (bias, gain, shift)],
        [
            (like((count, width), f32), *narrow),
            (like((count, width), bf16), *narrow),
            (like((count, width), bf16), *narrow),
            (like((count, 128), f32), *rows(tile, 128)),
        ],
        grid=(count // tile,),
    )


def feed_back_kernel(has_base, flag_ref, *refs):
    if has_base:
        base_ref, mine_ref, theirs_ref, refs = refs[0], refs[1], refs[2], refs[3:]
    (
        cot_ref,
        far_ref,
        other_ref,
        unit_ref,
        scale_ref,
        gain_ref,
        down_ref,
        slope_ref,
        up_ref,
        mixed_ref,
        low_mixed_ref,
        low_pre_ref,
        part_ref,
        small_ref,
    ) = refs
    step = pl.program_id(0)
    kept = flag_ref[0] > 0
    core = flag_ref[1] > 0
    first = jnp.where(core, other_ref[...], far_ref[...])
    second = jnp.where(core, far_ref[...], other_ref[...])
    far = jnp.concatenate([first, second], axis=0)
    cot = jnp.where(step == 0, cot_ref[flag_ref[2]], far).astype(f32)
    if has_base:
        here = flag_ref[1] == step
        back = jnp.where(here, mine_ref[...], theirs_ref[...]).astype(f32)
        grad_out = jnp.where(kept, base_ref[...] + back, cot)
    else:
        grad_out = jnp.where(kept, cot, 0.0)
    unit = unit_ref[...].astype(f32)
    grad_mixed = normalize_back(grad_out, unit, scale_ref[:, :1], gain_ref[...])
    mixed_ref[...] = grad_mixed
    low_mixed = grad_mixed.astype(bf16)
    low_mixed_ref[...] = low_mixed
    grad_active = dot_nt(low_mixed, down_ref[...])
    low_pre = (grad_active * slope_ref[...].astype(f32)).astype(bf16)
    low_pre_ref[...] = low_pre
    part_ref[...] = dot_nt(low_pre, up_ref[...]).astype(bf16)

    @pl.when(step == 0)
    def _():
        small_ref[...] = jnp.zeros_like(small_ref)

    width = grad_out.shape[1]

    def total(value):
        return jnp.sum(value, axis=0, keepdims=True)

    pre_sum = total(low_pre.astype(f32))
    small_ref[0:1, :] += total(grad_out * unit)
    small_ref[1:2, :] += total(grad_out)
    small_ref[2:3, :] += total(grad_mixed)
    small_ref[3:4, :] += pre_sum[:, :width]
    small_ref[4:5, :] += pre_sum[:, width:]


def feed_back(flags, base, cot, unit, scale, gain, down, slope, up, after=()):
    count, width = unit.shape
    units = up.shape[1]
    tile = count // 2
    wide, narrow = rows(tile, units), rows(tile, width)
    ins = [(flags, "smem", None)]
    if base is not None:
        ins += [(base[0], *narrow), (base[1], None, None), (base[2], None, None)]
    ins += [
        *[(c, None, None) for c in cot],
        (unit, *narrow),
        (scale, *rows(tile, 128)),
        (gain, None, None),
        (down, None, None),
        (slope, *wide),
        (up, None, None),
    ]
    return call(
        functools.partial(feed_back_kernel, base is not None),
        "feed_back",
        ins,
        [
            (like((count, width), f32), *narrow),
            (like((count, width), bf16), *narrow),
            (like((count, units), bf16), *wide),
            (like((count, width), bf16), *narrow),
            (like((8, width), f32), None, None),
        ],
        grid=(2,),
        after=after,
    )


def middle_back_kernel(
    mixed_ref,
    mine_ref,
    theirs_ref,
    unit_ref,
    scale_ref,
    gain_ref,
    out_ref,
    attended_ref,
    low_ref,
    context_ref,
    small_ref,
):
    summed = mine_ref[...].astype(f32) + theirs_ref[...].astype(f32)
    grad_hidden = mixed_ref[...] + summed
    unit = unit_ref[...].astype(f32)
    grad = normalize_back(grad_hidden, unit, scale_ref[:, :1], gain_ref[...])
    attended_ref[...] = grad
    low = grad.astype(bf16)
    low_ref[...] = low
    context_ref[...] = dot_nt(low, out_ref[...]).astype(bf16)

    @pl.when(pl.program_id(0) == 0)
    def _():
        small_ref[...] = jnp.zeros_like(small_ref)

    small_ref[0:1, :] += jnp.sum(grad_hidden * unit, axis=0, keepdims=True)
    small_ref[1:2, :] += jnp.sum(grad_hidden, axis=0, keepdims=True)
    small_ref[2:3, :] += jnp.sum(grad, axis=0, keepdims=True)


def middle_back(mixed, mine, theirs, unit, scale, gain, out_weight, after=()):
    count, width = mixed.shape
    local_width = out_weight.shape[0]
    tile = min(count, 256)
    narrow = rows(tile, width)
    return call(
        middle_back_kernel,
        "middle_back",
        [
            (mixed, *narrow),
            (mine, *narrow),
            (theirs, *narrow),
            (unit, *narrow),
            (scale, *rows(tile, 128)),
            (gain, None, None),
            (out_weight, None, None),
        ],
        [
            (like((count, width), f32), *narrow),
            (like((count, width), bf16), *narrow),
            (like((count, local_width), bf16), *rows(tile, local_width)),
            (like((8, width), f32), None, None),
        ],
        grid=(count // tile,),
        after=after,
    )


def put_halves(flag, value, column, send_ref, keep_ref):
    shares, half = send_ref.shape[:2]
    columns = slice(column, column + value.shape[1])
    value = value.astype(bf16)
    for share in range(shares):
        low = value[2 * share * half : (2 * share + 1) * half]
        high = value[(2 * share + 1) * half : (2 * share + 2) * half]
        send_ref[share, :, columns] = jnp.where(flag > 0, low, high)
        keep_ref[share, :, columns] = jnp.where(flag > 0, high, low)


def weight_kernel(pairs, flag_ref, *refs):
    lefts_rights, (send_ref, keep_ref) = refs[:-2], refs[-2:]
    column = 0
    for terms in pairs:
        value = 0.0
        for left, right in terms:
            value = value + dot_tn(lefts_rights[left][...], lefts_rights[right][...])
        put_halves(flag_ref[0], value, column, send_ref, keep_ref)
        column += value.shape[1]


def weight_grad(flag, arrays, pairs, by_share=False, after=()):
    shares = lax.axis_size("dp")
    width = arrays[pairs[0][0][0]].shape[1]
    columns = sum(arrays[terms[0][1]].shape[1] for terms in pairs)
    shape = (shares, width // (2 * shares), columns)
    if by_share:
        shape = (shares // 2, width // shares, columns)
    return call(
        functools.partial(weight_kernel, pairs),
        "weight_grad",
        [(flag, "smem", None)] + [(a, None, None) for a in arrays],
        [(like(shape, bf16), None, None)] * 2,
        after=after,
    )


def back_kernel(flag_ref, *refs):
    terms, (mine_ref, theirs_ref) = refs[:-2], refs[-2:]
    parts, half = mine_ref.shape[:2]
    grads = terms[: len(terms) // 2]
    weights = terms[len(terms) // 2 :]
    for part in range(parts):
        halves = []
        for side in range(2):
            start = (2 * part + side) * half
            value = 0.0
            for grad, weight in zip(grads, weights):
                value = value + dot_nt(grad[start : start + half], weight[0, 0])
            halves.append(value.astype(bf16))
        mine_ref[part] = jnp.where(flag_ref[1] > 0, halves[1], halves[0])
        theirs_ref[part] = jnp.where(flag_ref[1] > 0, halves[0], halves[1])


def back_grad(layer, flags, grads, weight, which, span, after=()):
    count, local_width = grads[0].shape
    width = weight.shape[2]
    out = like((count // span, span // 2, width), bf16), None, None
    return call(
        back_kernel,
        "back",
        [(flags, "smem", None)]
        + [(g, g.shape, lambda i: (0, 0)) for g in grads]
        + [(weight, (1, 1, width, local_width), lambda i, w=w: (layer, w, 0, 0)) for w in which],
        [out, out],
        grid=(1,),
        after=after,
    )


def sums_kernel(plans, *refs):
    count = (len(refs) - 2) // 2
    keeps, arrived, outs = refs[:count], refs[count : 2 * count], refs[2 * count :]
    for out, plan in zip(outs, plans):
        column = 0
        for source, start, width in plan:
            columns = slice(start, start + width)
            out[:, column : column + width] = add_low(
                keeps[source][0, :, columns], arrived[source][0, :, columns]
            )
            column += width


def sums(loads, plans, after=()):
    out = like((loads[0].keep.shape[1], sum(p[2] for p in plans[0])), bf16), None, None
    arrays = [load.keep for load in loads] + [load.arrived for load in loads]
    return call(
        functools.partial(sums_kernel, plans),
        "sums",
        [(a, None, None) for a in arrays],
        [out, out],
        after=after,
    )


def adds_kernel(a_ref, b_ref, c_ref, d_ref, first_ref, second_ref):
    first_ref[...] = add_low(a_ref[...], b_ref[...])
    second_ref[...] = add_low(c_ref[...], d_ref[...])


def adds(first, second, after=()):
    out = like(first[0].shape, bf16), None, None
    return call(
        adds_kernel,
        "adds",
        [(a, None, None) for a in (*first, *second)],
        [out, out],
        after=after,
    )


def relay_kernel(in_ref, out_ref):
    out_ref[...] = in_ref[...]


def relay(value, after):
    return call(
        relay_kernel, "adds", [(value, None, None)], [(like(value.shape, value.dtype), None, None)], after=after
    )[0]


def finish_kernel(flag_ref, a_ref, b_ref, c_ref, d_ref, *refs):
    qkv_ref, out_ref, up_ref, down_ref = refs
    units = up_ref.shape[2]
    local_width = qkv_ref.shape[3]

    def whole(flag, mine, other):
        low = jnp.where(flag > 0, other[...], mine[...])
        high = jnp.where(flag > 0, mine[...], other[...])
        return jnp.concatenate([low, high], axis=0).astype(f32)

    down = whole(flag_ref[0], a_ref, b_ref)
    down_ref[0] = down[:, :units]
    qkv_ref[0, 2] = down[:, units : units + local_width]
    out_ref[0] = down[:, units + local_width :]
    up = whole(flag_ref[1], c_ref, d_ref)
    up_ref[0] = up[:, :units]
    qkv_ref[0, 0] = up[:, units : units + local_width]
    qkv_ref[0, 1] = up[:, units + local_width :]


def finish(layer, flags, first, second, units, onto=()):
    half, columns = first[0].shape
    local_width = (columns - units) // 2
    shapes = (
        (2, 3, 2 * half, local_width),
        (2, 2 * half, local_width),
        (2, 2 * half, units),
        (2, 2 * half, units),
    )

    def place(shape):
        return like(shape, f32), (1,) + shape[1:], lambda i: (layer,) + (0,) * (len(shape) - 1)

    return call(
        finish_kernel,
        "finish",
        [(flags, "smem", None)]
        + [(a, a.shape, lambda i: (0, 0)) for a in (*first, *second)],
        [place(shape) for shape in shapes],
        grid=(1,),
        onto=onto,
    )


def pack_kernel(*refs):
    ins, out_ref = refs[:-1], refs[-1]
    each = len(ins) // 2
    out_ref[...] = jnp.zeros_like(out_ref)

    def total(ref):
        return jnp.sum(ref[...].astype(f32), axis=0, keepdims=True)

    for layer in range(2):
        dq, dv, dv2, feed, middle = ins[layer * each : (layer + 1) * each]
        width = dq.shape[1]
        base = 16 * layer
        out_ref[base : base + 1, :width] = total(dq)
        out_ref[base : base + 1, width:] = total(dv) + total(dv2)
        sources = (middle, 2), (middle, 0), (feed, 0), (middle, 1), (feed, 1), (feed, 3), (feed, 4)
        for i, (ref, row) in enumerate(sources + ((feed, 2),)):
            out_ref[base + 1 + i : base + 2 + i, :] = ref[row : row + 1, :]


def pack(first, second, after=()):
    width = first[3].shape[1]
    return call(
        pack_kernel,
        "pack",
        [(a, a.shape, lambda i: (0, 0)) for a in (*first, *second)],
        [(like((32, width), f32), (32, width), lambda i: (0, 0))],
        grid=(1,),
        after=after,
    )[0]


class Order:
    def __init__(self):
        self.last = ()

    def mark(self, *values):
        self.last = values

    def also(self, value):
        self.last = self.last + (value,)


def both_halves(mine, axis=0):
    other = swap(mine, "mp", 1)
    first = lax.axis_index("mp") == 0
    whole = jnp.where(
        first, jnp.stack([mine, other], axis=axis), jnp.stack([other, mine], axis=axis)
    )
    return whole.reshape(mine.shape[:axis] + (-1,) + mine.shape[axis + 1 :])


def my_half(value):
    count = value.shape[0] // 2
    return pick(value.reshape((2, count) + value.shape[1:]), lax.axis_index("mp"), 0)


def share_kernel(flag_ref, *refs):
    ins, (send_ref, keep_ref) = refs[:-2], refs[-2:]
    count = len(ins) // 2
    column = 0
    for keep, arrived in zip(ins[:count], ins[count:]):
        columns = slice(column, column + keep.shape[-1])
        column += keep.shape[-1]
        low, high = [add_low(keep[side], arrived[side]) for side in range(2)]
        send_ref[0, :, columns] = jnp.where(flag_ref[0] > 0, low, high)
        keep_ref[0, :, columns] = jnp.where(flag_ref[0] > 0, high, low)


def share_step(flag, loads, after=()):
    shares, half = loads[0].keep.shape[:2]
    columns = sum(load.keep.shape[2] for load in loads)
    arrays = [load.keep for load in loads] + [load.arrived for load in loads]
    out = like((shares // 2, half, columns), bf16), (1, half, columns), lambda i: (i, 0, 0)
    return call(
        share_kernel,
        "share",
        [(flag, "smem", None)] + [(a, (2,) + a.shape[1:], lambda i: (i, 0, 0)) for a in arrays],
        [out, out],
        grid=(shares // 2,),
        after=after,
    )


def split_kernel(flag_ref, *refs):
    count = len(refs) // 4
    for k in range(count):
        keep, arrived = refs[k], refs[count + k]
        send_ref, keep_ref = refs[2 * count + 2 * k : 2 * count + 2 * k + 2]
        half = keep.shape[1] // 2
        low = add_low(keep[:, :half], arrived[:, :half])
        high = add_low(keep[:, half:], arrived[:, half:])
        send_ref[...] = jnp.where(flag_ref[k] > 0, low, high)
        keep_ref[...] = jnp.where(flag_ref[k] > 0, high, low)


def split_step(flags, loads, after=()):
    shares, rows_, columns = loads[0].keep.shape
    arrays = [load.keep for load in loads] + [load.arrived for load in loads]
    out = (
        like((shares, rows_ // 2, columns), bf16),
        (1, rows_ // 2, columns),
        lambda i: (i, 0, 0),
    )
    return call(
        split_kernel,
        "share",
        [(flags, "smem", None)] + [(a, (1, rows_, columns), lambda i: (i, 0, 0)) for a in arrays],
        [out] * (2 * len(loads)),
        grid=(shares,),
        after=after,
    )


def join_kernel(flag_ref, a_ref, b_ref, c_ref, d_ref, first_ref, second_ref):
    for k, (mine, other, out) in enumerate(((a_ref, b_ref, first_ref), (c_ref, d_ref, second_ref))):
        half = mine.shape[0]
        out[:half] = jnp.where(flag_ref[k] > 0, other[...], mine[...])
        out[half:] = jnp.where(flag_ref[k] > 0, mine[...], other[...])


def join(flags, first, second, after=()):
    rows_, columns = first[0].shape
    out = like((2 * rows_, columns), bf16), None, None
    return call(
        join_kernel,
        "adds",
        [(flags, "smem", None)] + [(a, None, None) for a in (*first, *second)],
        [out, out],
        after=after,
    )


def last_bit():
    return bits_of("seq") - 1


class Load:
    def __init__(self, line, sent, axis, bit):
        send, self.keep = sent
        line.mark(send)
        self.arrived = swap(send, axis, 1 << bit)


def launch(line, arrays, pairs, axis, bit):
    flag = place_bit(axis, bit).reshape(1)
    return Load(
        line, weight_grad(flag, arrays, pairs, axis == "dp", line.last), axis, bit
    )


def split(line, loads, bits):
    flags = jnp.stack([place_bit("seq", bit) for bit in bits])
    sent = split_step(flags, loads, line.last)
    return [Load(line, sent[2 * k : 2 * k + 2], "seq", bit) for k, bit in enumerate(bits)]


def share(line, bit, *loads):
    flag = place_bit("dp", bit).reshape(1)
    return Load(line, share_step(flag, loads, line.last), "dp", bit)


def shares(line, first, *loads):
    for bit in range(first, bits_of("dp")):
        loads = (share(line, bit, *loads),)
    return loads[0]


class Tail:
    def __init__(self, line, loads, plans, twice):
        self.totals = sums(loads, plans, line.last)
        self.twice = twice
        bits = list(range(bits_of("seq")))
        if twice:
            self.hop(line, (0, last_bit()))
            return
        self.across = (bits[:-1], bits[1:])
        for place in range(len(bits) - 2):
            self.totals = [
                add_low(t, swap(t, "seq", 1 << across[place]))
                for t, across in zip(self.totals, self.across)
            ]
        self.hop(line, [across[-1] for across in self.across])

    def hop(self, line, bits):
        line.mark(*self.totals)
        self.arrived = [swap(t, "seq", 1 << b) for t, b in zip(self.totals, bits)]

    def gather(self, line):
        first, second = zip(self.totals, self.arrived)
        if self.twice:
            flags = jnp.stack([place_bit("seq", 0), place_bit("seq", last_bit())])
            self.totals = join(flags, first, second, line.last)
        else:
            self.totals = adds(first, second, line.last)
        self.hop(line, (last_bit(), 0))

    def finish(self, layer, units, onto=()):
        flags = jnp.stack([place_bit("seq", last_bit()), place_bit("seq", 0)])
        first, second = zip(self.totals, self.arrived)
        return finish(layer, flags, first, second, units, onto)


class Layer:
    def __init__(self, layer, params, weight_qkv, augs):
        self.layer = layer
        (
            _,
            self.bias_qv,
            self.weight_out,
            self.bias_out,
            self.gain,
            self.shift,
            self.weight_up,
            self.bias_up,
            self.weight_down,
            self.bias_down,
        ) = params
        self.weight_qkv = weight_qkv
        self.augs = augs

    def open(self, low_own):
        self.low_own = low_own
        self.query, self.key_own, self.value_own = project(
            self.layer, low_own, self.weight_qkv, self.bias_qv, True
        )

    def forward(self, inputs, low_rest, after=()):
        self.low_rest = low_rest
        key_rest, value_rest = project(
            self.layer, low_rest, self.weight_qkv, self.bias_qv, False
        )
        self.keys = (self.key_own, key_rest)
        self.values = (self.value_own, value_rest)
        self.context, self.log_total = attend(
            self.query, self.keys, self.values, self.augs, after
        )
        part = dot_nn(self.context, self.weight_out).astype(bf16)
        hidden, self.low_hidden, self.unit_one, self.scale_one, self.active, self.slope, part = feed(
            inputs,
            part,
            swap(part, "mp", 1),
            self.bias_out,
            self.gain[0],
            self.shift[0],
            self.weight_up,
            self.bias_up,
            self.weight_down,
        )
        result, low_result, self.unit_two, self.scale_two = close(
            hidden, part, swap(part, "mp", 1), self.bias_down, self.gain[1], self.shift[1]
        )
        return result, low_result

    def feed_back(self, line, flags, base, cot):
        self.grad_mixed, self.low_mixed, self.low_pre, self.part, self.small_feed = feed_back(
            flags,
            base,
            cot,
            self.unit_two,
            self.scale_two,
            self.gain[1],
            self.weight_down,
            self.slope,
            self.weight_up,
            line.last,
        )
        line.mark(self.small_feed)

    def down_grad(self, line, axis, bit):
        return launch(line, (self.low_mixed, self.active), (((0, 1),),), axis, bit)

    def up_grad(self, line):
        return launch(line, (self.low_hidden, self.low_pre), (((0, 1),),), "seq", 0)

    def middle_back(self, line):
        self.grad_attended, self.low_attended, self.grad_context, self.small_middle = middle_back(
            self.grad_mixed,
            self.part,
            swap(self.part, "mp", 1),
            self.unit_one,
            self.scale_one,
            self.gain[0],
            self.weight_out,
            line.last,
        )
        line.mark(self.small_middle)

    def attend_back(self, line):
        self.dq, *grads = attend_back(
            self.query,
            self.keys,
            self.values,
            self.augs,
            self.log_total,
            self.context,
            self.grad_context,
            line.last,
        )
        self.dk, self.dv = grads[:2], grads[2:]
        line.mark(self.dq)

    def input_grad_parts(self, line, flags):
        span = self.query.shape[0]
        mine, theirs = back_grad(
            self.layer, flags, (self.dk[1], self.dv[1]), self.weight_qkv, (1, 2), span, line.last
        )
        arrived = swap(theirs, "mp", 1)
        self.own, theirs = back_grad(
            self.layer, flags, (self.dq, self.dk[0], self.dv[0]), self.weight_qkv, (0, 1, 2), span, (theirs,)
        )
        rest = add_low(mine, arrived)
        self.far = [swap(rest[j], "seq", 2 * (j + 1)) for j in range(rest.shape[0])]
        self.near = swap(theirs, "mp", 1)
        line.mark(rest, theirs)

    def input_grad(self):
        half = self.own[0].astype(f32) + self.near[0].astype(f32)
        half = (half + sum(f.astype(f32) for f in self.far)).astype(bf16)
        return (self.grad_attended, half, swap(half, "mp", 1))

    qk_pairs = (((0, 2),), ((0, 3), (1, 4)))
    vo_pairs = (((0, 3), (1, 4)), ((2, 5),))

    def value_out_grad(self, line):
        arrays = (self.low_own, self.low_rest, self.low_attended, *self.dv, self.context)
        return launch(line, arrays, self.vo_pairs, "seq", last_bit())

    def query_key_grad(self, line):
        arrays = (self.low_own, self.low_rest, self.dq, *self.dk)
        return launch(line, arrays, self.qk_pairs, "seq", 0)

    def small(self):
        return (self.dq, *self.dv, self.small_feed, self.small_middle)


def layer_part(index, params):
    parts = [array[index] for array in params]
    for i in (3, 7, 9):
        parts[i] = parts[i].reshape(1, -1)
    for i in (4, 5):
        parts[i] = parts[i][:, None, :]
    return tuple(parts)


def stack_pair(first_part, second_part):
    return jnp.stack([first_part, second_part])


def local(
    tokens,
    segments,
    dropped,
    qkv_weight,
    qv_bias,
    out_weight,
    out_bias,
    norm_gain,
    norm_shift,
    up_weight,
    up_bias,
    down_weight,
    down_bias,
    cotangent,
):
    params = (
        qkv_weight,
        qv_bias,
        out_weight,
        out_bias,
        norm_gain,
        norm_shift,
        up_weight,
        up_bias,
        down_weight,
        down_bias,
    )
    first = layer_part(0, params)
    second = layer_part(1, params)
    COUNT[0] = 0
    rows_here, span, width = tokens.shape
    assert rows_here == 2
    places = lax.axis_size("seq")
    place = lax.axis_index("seq")
    row = place & 1
    halves_of = tokens.reshape(rows_here, 2, span // 2, width)
    halves_of = pick(halves_of, lax.axis_index("mp"), 1)
    half_mine, half_partner = pick(halves_of, row, 0), pick(halves_of, 1 - row, 0)
    arrived = [swap((half_mine, half_partner)[c % 2], "seq", c) for c in range(1, places)]
    rest = both_halves(jnp.stack(arrived), axis=1)
    low_own = jnp.concatenate([pick(tokens, row, 0), rest[0]])
    low_rest = rest[1:].reshape(-1, width)
    seg_row = pick(segments, row, 0).reshape(places, span)
    for bit in range(bits_of("seq")):
        shaped = seg_row.reshape(places >> (bit + 1), 2, 1 << bit, span)
        seg_row = jnp.where(place_bit("seq", bit) == 1, shaped[:, ::-1], shaped).reshape(places, span)
    seg_keys = seg_row.reshape(places * span, 1)
    lane = lax.broadcasted_iota(jnp.int32, (1, PAIR), 1) % HEAD
    used = lane < SEGMENTS
    kaug = jnp.where(used & (seg_keys != lane), 1.0, 0.0).astype(bf16)
    qaug = jnp.where(used & (seg_keys[: 2 * span] == lane), -FAR, 0.0).astype(bf16)
    augs = (qaug, kaug[: 2 * span], kaug[2 * span :])
    cot_far = swap(my_half(pick(cotangent, 1 - row, 0)), "seq", 1)
    kept = 1 - pick(dropped, lax.axis_index("dp") * rows_here + row, 0)
    flags = jnp.stack([kept, lax.axis_index("mp"), row])

    one, two = Layer(0, first, qkv_weight, augs), Layer(1, second, qkv_weight, augs)
    one.open(low_own)
    small_params = [p for part in (first, second) for i, p in enumerate(part) if i in (1, 3, 4, 5, 7, 9)]
    hidden_one, low_one = one.forward(low_own, low_rest, (*small_params, flags))
    low_half = my_half(low_one)
    arrived = [swap(low_half, "seq", c) for c in range(2, places, 2)]
    two.open(low_one)
    cot = (cotangent, cot_far, swap(cot_far, "mp", 1))
    rest = both_halves(relay(jnp.stack(arrived), (two.query, cot[2])), axis=1)
    result_two, _ = two.forward(hidden_one, rest.reshape(-1, width))
    result = jnp.where(kept > 0, result_two, hidden_one)

    class Return:
        def __init__(self, value):
            self.mine = value[:span]
            self.arrived = swap(my_half(value[span:].astype(bf16)), "seq", 1)
            self.other = swap(self.arrived, "mp", 1)

        def whole(self):
            core = lax.axis_index("mp") == 0
            far = jnp.where(
                core,
                jnp.concatenate([self.arrived, self.other]),
                jnp.concatenate([self.other, self.arrived]),
            ).astype(f32)
            return jnp.where(row == 0, jnp.stack([self.mine, far]), jnp.stack([far, self.mine]))

    line = Order()
    outputs = Return(result)
    twice = bits_of("seq") == 2 and width // lax.axis_size("dp") % 64 == 0
    first_core = lax.axis_index("mp") == 0
    units = up_weight.shape[2]
    half_units = units // 2
    plans_two = (
        ((0, 0, units), (1, units, half_units)),
        ((1, 0, units), (1, units + half_units, half_units)),
    )
    plans_one = (
        ((0, 0, units), (0, 2 * units, half_units)),
        ((0, units, units), (0, 2 * units + half_units, half_units)),
    )
    two.feed_back(line, flags, None, cot)
    down_two = two.down_grad(line, "dp", 0)
    up_two = two.up_grad(line)
    line.also(outputs.arrived)
    two.middle_back(line)
    line.also(outputs.other)
    two.attend_back(line)
    two.input_grad_parts(line, flags)
    value_two = two.value_out_grad(line)
    down_two = shares(line, 1, down_two)
    query_two = two.query_key_grad(line)
    up_two = share(line, 0, up_two)
    one.feed_back(line, flags, two.input_grad(), cot)
    down_one = one.down_grad(line, "seq", last_bit())
    up_one = one.up_grad(line)
    one.middle_back(line)
    attn_two = share(line, 0, value_two, query_two)
    one.attend_back(line)
    value_one = one.value_out_grad(line)
    query_one = one.query_key_grad(line)
    joined_two = shares(line, 1, up_two, attn_two)
    if twice:
        down_one, up_one = split(line, [down_one, up_one], (0, last_bit()))
    if twice:
        value_one, query_one = split(line, [value_one, query_one], (0, last_bit()))
    (down_two,) = split(line, [down_two], (last_bit(),))
    feed_one = share(line, 0, down_one, up_one)
    one.input_grad_parts(line, flags)
    attn_one = share(line, 0, value_one, query_one)
    base, own_half, other_half = one.input_grad()
    line.also(own_half)
    tail_two = Tail(line, [down_two, joined_two], plans_two, False)
    joined_one = shares(line, 1, feed_one, attn_one)
    tail_two.gather(line)
    halves = own_half, other_half
    back = jnp.where(first_core, jnp.concatenate(halves), jnp.concatenate(halves[::-1]))
    tokens_grad = Return(base + back.astype(f32))
    small = pack(one.small(), two.small(), line.last)
    line.also(small)
    for bit in range(bits_of("seq")):
        small = small + swap(small, "seq", 1 << bit)
    line.also(small)
    line.also(tokens_grad.arrived)
    tail_one = Tail(line, [joined_one], plans_one, twice)
    small = small + swap(small, "dp", 1)
    weight_sums = tail_two.finish(1, units)
    tail_one.gather(line)
    outputs, tokens_grad = outputs.whole(), tokens_grad.whole()
    small = relay(small, line.last)
    for bit in range(1, bits_of("dp")):
        small = small + swap(small, "dp", 1 << bit)
    qkv_sum, out_sum, up_sum, down_sum = tail_one.finish(0, units, weight_sums)
    out_sum, down_sum = out_sum.swapaxes(1, 2), down_sum.swapaxes(1, 2)
    small = small.reshape(2, 16, width)
    halves = width // 2
    qv_sum = small[:, 0].reshape(2, 2, halves)
    out_bias_sum = small[:, 1]
    gain_sum, shift_sum = small[:, 2:4], small[:, 4:6]
    up_bias_sum = small[:, 6:8].reshape(2, 2 * width)
    down_bias_sum = small[:, 8]

    return (
        outputs,
        tokens_grad,
        qkv_sum,
        qv_sum,
        out_sum,
        out_bias_sum,
        gain_sum,
        shift_sum,
        up_sum,
        up_bias_sum,
        down_sum,
        down_bias_sum,
    )


def solution(mesh):
    placed = (
        P("dp", "seq", None),
        P("dp", None),
        P(),
        P(None, None, None, "mp"),
        P(None, None, "mp"),
        P(None, "mp", None),
        P(),
        P(),
        P(),
        P(None, None, "mp"),
        P(None, "mp"),
        P(None, "mp", None),
        P(),
        P("dp", "seq", None),
    )
    return jax.shard_map(
        local,
        mesh=mesh,
        in_specs=placed,
        out_specs=(
            P("dp", "seq", None),
            P("dp", "seq", None),
            P(None, None, "dp", "mp"),
            P(None, None, "mp"),
            P(None, "mp", "dp"),
            P(),
            P(),
            P(),
            P(None, "dp", "mp"),
            P(None, "mp"),
            P(None, "mp", "dp"),
            P(),
        ),
        check_vma=False,
    )
```

```python
import functools

import jax
import jax.numpy as jnp
from jax import lax
from jax.experimental import pallas as pl
from jax.experimental.pallas import tpu as pltpu
from jax.sharding import PartitionSpec as P

HEAD = 64
PAIR = 2 * HEAD
SEGMENTS = 4
FAR = 1e30
eps_norm = 1e-05
root_half = 0.7071067811865476
inv_root_tau = 0.3989422804014327
scale_two = 0.125 * 1.4426950408889634
f32 = jnp.float32
bf16 = jnp.bfloat16
COSTS = (3, 1.5, 7, 2, 1.5, 1.5, 1, 1.5, 7, 30, 1.5, 30, 15, 4.2, 3, 28.5, 4.5, 4.5, 4.2, 4.2, 6, 6, 18, 4.2, 4.2, 2, 6, 28.5, 4.2, 4.2, 6, 0, 2, 6, 6, 4.5, 4.5, 6, 3, 2, 30, 4.5, 0.3, 6, 3, 1, 6)
COUNT = [0]
LIMITS = {'finish': 16, 'pack': 12, 'back': 12, 'sums': 8, 'adds': 8, 'share': 12, 'project': 4, 'attend': 10, 'feed': 14, 'close': 6, 'feed_back': 14, 'weight_grad': 10, 'middle_back': 8, 'attend_back': 14}
anywhere = pl.BlockSpec(memory_space=pl.ANY)
smem = pl.BlockSpec(memory_space=pltpu.SMEM)


def dot_nn(left, right):
    return lax.dot_general(left, right, (((1,), (0,)), ((), ())), preferred_element_type=f32)


def dot_nt(left, right):
    return lax.dot_general(left, right, (((1,), (1,)), ((), ())), preferred_element_type=f32)


def dot_tn(left, right):
    return lax.dot_general(left, right, (((0,), (0,)), ((), ())), preferred_element_type=f32)


def swap(value, axis, mask):
    count = lax.axis_size(axis)
    return lax.ppermute(value, axis, [(i, i ^ mask) for i in range(count)])


def place_bit(axis, bit):
    return (lax.axis_index(axis) >> bit) & 1


def bits_of(axis):
    count = lax.axis_size(axis)
    number = count.bit_length() - 1
    assert 1 << number == count
    return number


def pick(value, index, axis):
    return lax.dynamic_index_in_dim(value, index, axis, keepdims=False)


def add_low(left, right):
    return (left.astype(f32) + right.astype(f32)).astype(bf16)


def call(kernel, name, ins, outs, grid=(), scratch=(), after=(), onto=()):
    def placed(shape):
        return pltpu.HBM(shape.shape, shape.dtype) if isinstance(shape, Saved) else shape

    def spec(shape, block, index):
        if block == "smem":
            return smem
        if block is None:
            return pl.BlockSpec(shape, lambda *g: (0,) * len(shape))
        return pl.BlockSpec(block, index)

    count = len(ins)
    busy = COSTS[COUNT[0] % len(COSTS)]
    COUNT[0] += 1
    after = tuple(onto) + tuple(after)

    def body(*refs):
        kernel(*refs[:count], *refs[count + len(after) :])

    return pl.pallas_call(
        body,
        grid=grid,
        in_specs=[spec(a.shape, b, i) for a, b, i in ins] + [anywhere] * len(after),
        out_specs=[spec(s.shape, b, i) for s, b, i in outs],
        out_shape=[placed(s) for s, _, _ in outs],
        scratch_shapes=list(scratch),
        input_output_aliases={count + i: i for i in range(len(onto))},
        name=name,
        cost_estimate=pl.CostEstimate(flops=int(1.15e9 * busy), bytes_accessed=0, transcendentals=0),
        compiler_params=pltpu.CompilerParams(vmem_limit_bytes=LIMITS[name] << 20),
    )(*[a for a, _, _ in ins], *after)


def like(shape, dtype):
    return jax.ShapeDtypeStruct(shape, dtype)


class Saved:
    def __init__(self, shape, dtype):
        self.shape, self.dtype = shape, dtype


def head_lanes(side):
    lane = lax.broadcasted_iota(jnp.int32, (1, PAIR), 1)
    return lane < HEAD if side == 0 else lane >= HEAD


def scores_of(inside, parts, query, qaug):
    probe = jnp.where(inside, query, qaug)
    return jnp.concatenate(
        [dot_nt(jnp.where(inside, k[...], aug[...]), probe) for k, aug in parts], axis=0
    )


def attend_kernel(
    q_ref, k_ref, k2_ref, v_ref, v2_ref, qaug_ref, kaug_ref, kaug2_ref, context_ref, log_ref, vt_ref
):
    own = v_ref.shape[0]

    @pl.when(pl.program_id(1) == 0)
    def _():
        vt_ref[:, :own] = v_ref[...].T
        vt_ref[:, own:] = v2_ref[...].T

    parts = ((k_ref, kaug_ref), (k2_ref, kaug2_ref))
    query = q_ref[...]
    outs = []
    for side in range(2):
        scores = scores_of(head_lanes(side), parts, query, qaug_ref[...])
        peak = jnp.max(scores, axis=0, keepdims=True) * scale_two
        raised = jnp.exp2(scores * scale_two - peak)
        total = jnp.sum(raised, axis=0, keepdims=True)
        mixed = dot_nn(vt_ref[side * HEAD : (side + 1) * HEAD, :], raised.astype(bf16))
        outs.append(mixed / total)
        log_ref[0, side : side + 1, :] = peak + jnp.log2(total)
    context_ref[...] = jnp.concatenate(outs, axis=0).T.astype(bf16)


def attention_specs(count, counts):
    tile = min(count, 512)
    own = (tile, PAIR), lambda p, i: (i, p)
    first, rest = [((n, PAIR), lambda p, i: (0, p)) for n in counts]
    logs = (1, 2, tile), lambda p, i: (p, 0, i)
    aug = (tile, PAIR), lambda p, i: (i, 0)
    return tile, own, first, rest, logs, aug


def attend(query, keys, values, augs, after=()):
    count, width = query.shape
    pairs = width // PAIR
    tile, own, first, rest, logs, aug = attention_specs(count, [k.shape[0] for k in keys])
    return call(
        attend_kernel,
        "attend",
        [
            (query, *own),
            (keys[0], *first),
            (keys[1], *rest),
            (values[0], *first),
            (values[1], *rest),
            (augs[0], *aug),
            (augs[1], None, None),
            (augs[2], None, None),
        ],
        [(like(query.shape, bf16), *own), (Saved((pairs, 2, count), f32), *logs)],
        grid=(pairs, count // tile),
        scratch=[pltpu.VMEM((PAIR, sum(k.shape[0] for k in keys)), bf16)],
        after=after,
    )


def attend_back_kernel(
    q_ref,
    k_ref,
    k2_ref,
    v_ref,
    v2_ref,
    qaug_ref,
    kaug_ref,
    kaug2_ref,
    log_ref,
    context_ref,
    grad_ref,
    dq_ref,
    dk_ref,
    dk2_ref,
    dv_ref,
    dv2_ref,
    kt_ref,
    dk_sum,
    dv_sum,
):
    step = pl.program_id(1)
    own = k_ref.shape[0]

    @pl.when(step == 0)
    def _():
        kt_ref[:, :own] = k_ref[...].T
        kt_ref[:, own:] = k2_ref[...].T
        dk_sum[...] = jnp.zeros_like(dk_sum)
        dv_sum[...] = jnp.zeros_like(dv_sum)

    parts = ((k_ref, kaug_ref), (k2_ref, kaug2_ref))
    query, grad = q_ref[...], grad_ref[...]
    zero = jnp.zeros((), bf16)
    product = (grad.astype(f32) * context_ref[...].astype(f32)).T
    outs = []
    for side in range(2):
        inside = head_lanes(side)
        scores = scores_of(inside, parts, query, qaug_ref[...])
        chance = jnp.exp2(scores * scale_two - log_ref[0, side : side + 1, :])
        grad_side = jnp.where(inside, grad, zero)
        inner = jnp.sum(product[side * HEAD : (side + 1) * HEAD], axis=0, keepdims=True)
        grad_chance = jnp.concatenate([dot_nt(v[...], grad_side) for v in (v_ref, v2_ref)], axis=0)
        grad_scores = (chance * (grad_chance - inner)).astype(bf16)
        dv_sum[...] += dot_nn(chance.astype(bf16), grad_side)
        dk_sum[...] += dot_nn(grad_scores, jnp.where(inside, query, zero))
        outs.append(dot_nn(kt_ref[side * HEAD : (side + 1) * HEAD, :], grad_scores))
    dq_ref[...] = (jnp.concatenate(outs, axis=0) * 0.125).T.astype(bf16)

    @pl.when(step == pl.num_programs(1) - 1)
    def _():
        dk_ref[...] = (dk_sum[:own] * 0.125).astype(bf16)
        dk2_ref[...] = (dk_sum[own:] * 0.125).astype(bf16)
        dv_ref[...] = dv_sum[:own].astype(bf16)
        dv2_ref[...] = dv_sum[own:].astype(bf16)


def attend_back(query, keys, values, augs, log_total, context, grad_context, after=()):
    count, width = query.shape
    full = sum(k.shape[0] for k in keys)
    pairs = width // PAIR
    tile, own, first, rest, logs, aug = attention_specs(count, [k.shape[0] for k in keys])
    return call(
        attend_back_kernel,
        "attend_back",
        [
            (query, *own),
            (keys[0], *first),
            (keys[1], *rest),
            (values[0], *first),
            (values[1], *rest),
            (augs[0], *aug),
            (augs[1], None, None),
            (augs[2], None, None),
            (log_total, *logs),
            (context, *own),
            (grad_context, *own),
        ],
        [
            (like(query.shape, bf16), *own),
            (like(keys[0].shape, bf16), *first),
            (like(keys[1].shape, bf16), *rest),
            (like(keys[0].shape, bf16), *first),
            (like(keys[1].shape, bf16), *rest),
        ],
        grid=(pairs, count // tile),
        scratch=[
            pltpu.VMEM((PAIR, full), bf16),
            pltpu.VMEM((full, PAIR), f32),
            pltpu.VMEM((full, PAIR), f32),
        ],
        after=after,
    )


def project_kernel(with_query, in_ref, weight_ref, bias_ref, *outs):
    low = in_ref[...]
    if with_query:
        outs[0][...] = (dot_nn(low, weight_ref[0, 0]) + bias_ref[0]).astype(bf16)
        outs = outs[1:]
    outs[0][...] = dot_nn(low, weight_ref[0, 1]).astype(bf16)
    outs[1][...] = (dot_nn(low, weight_ref[0, 2]) + bias_ref[1]).astype(bf16)


def project(layer, low, weight, bias, with_query):
    count, width = low.shape
    local_width = weight.shape[3]
    tile = min(count, 256)
    if count % tile:
        tile = count
    out = like((count, local_width), bf16), *rows(tile, local_width)
    return call(
        functools.partial(project_kernel, with_query),
        "project",
        [
            (low, *rows(tile, width)),
            (weight, (1,) + weight.shape[1:], lambda i: (layer, 0, 0, 0)),
            (bias, None, None),
        ],
        [out] * (3 if with_query else 2),
        grid=(count // tile,),
    )


def normalize(rows_in, gain, shift):
    center = rows_in - jnp.mean(rows_in, axis=-1, keepdims=True)
    scale = lax.rsqrt(jnp.mean(center * center, axis=-1, keepdims=True) + eps_norm)
    unit = center * scale
    return (unit * gain + shift, unit, scale)


def normalize_back(grad_out, unit, scale, gain):
    grad_unit = grad_out * gain
    inner = (
        grad_unit
        - jnp.mean(grad_unit, axis=-1, keepdims=True)
        - unit * jnp.mean(grad_unit * unit, axis=-1, keepdims=True)
    )
    return inner * scale


def rows(tile, width):
    return (tile, width), lambda i: (i, 0)


def feed_kernel(
    in_ref,
    mine_ref,
    theirs_ref,
    bias_ref,
    gain_ref,
    shift_ref,
    up_ref,
    up_bias_ref,
    down_ref,
    hidden_ref,
    low_ref,
    unit_ref,
    scale_ref,
    active_ref,
    slope_ref,
    part_ref,
):
    summed = mine_ref[...].astype(f32) + theirs_ref[...].astype(f32)
    total = in_ref[...].astype(f32) + (summed + bias_ref[...])
    hidden, unit, scale = normalize(total, gain_ref[...], shift_ref[...])
    low = hidden.astype(bf16)
    hidden_ref[...] = hidden
    low_ref[...] = low
    unit_ref[...] = unit.astype(bf16)
    scale_ref[...] = jnp.broadcast_to(scale, scale_ref.shape)
    pre = dot_nn(low, up_ref[...]) + up_bias_ref[...]
    below = 0.5 * (1.0 + lax.erf(pre * root_half))
    active = (pre * below).astype(bf16)
    active_ref[...] = active
    slope_ref[...] = (below + pre * (jnp.exp(-0.5 * pre * pre) * inv_root_tau)).astype(bf16)
    part_ref[...] = dot_nn(active, down_ref[...]).astype(bf16)


def feed(inputs, mine, theirs, bias, gain, shift, up, up_bias, down):
    count, width = inputs.shape
    units = up.shape[1]
    tile = min(count, 256)
    wide, narrow = rows(tile, units), rows(tile, width)
    return call(
        feed_kernel,
        "feed",
        [(inputs, *narrow), (mine, *narrow), (theirs, *narrow)]
        + [(a, None, None) for a in (bias, gain, shift, up, up_bias, down)],
        [
            (like((count, width), f32), *narrow),
            (Saved((count, width), bf16), *narrow),
            (Saved((count, width), bf16), *narrow),
            (Saved((count, 128), f32), *rows(tile, 128)),
            (Saved((count, units), bf16), *wide),
            (Saved((count, units), bf16), *wide),
            (like((count, width), bf16), *narrow),
        ],
        grid=(count // tile,),
    )


def close_kernel(
    in_ref, mine_ref, theirs_ref, bias_ref, gain_ref, shift_ref, out_ref, unit_ref, scale_ref, *low
):
    summed = mine_ref[...].astype(f32) + theirs_ref[...].astype(f32)
    total = in_ref[...] + (summed + bias_ref[...])
    result, unit, scale = normalize(total, gain_ref[...], shift_ref[...])
    out_ref[...] = result
    if low:
        low[0][...] = result.astype(bf16)
    unit_ref[...] = unit.astype(bf16)
    scale_ref[...] = jnp.broadcast_to(scale, scale_ref.shape)


def close(inputs, mine, theirs, bias, gain, shift, low):
    count, width = inputs.shape
    tile = min(count, 256)
    narrow = rows(tile, width)
    return call(
        close_kernel,
        "close",
        [(inputs, *narrow), (mine, *narrow), (theirs, *narrow)]
        + [(a, None, None) for a in (bias, gain, shift)],
        [
            (like((count, width), f32), *narrow),
            (like((count, width), bf16), *narrow),
            (like((count, 128), f32), *rows(tile, 128)),
        ]
        + [(like((count, width), bf16), *narrow)] * low,
        grid=(count // tile,),
    )


def feed_back_kernel(has_base, flag_ref, *refs):
    if has_base:
        base_ref, mine_ref, theirs_ref, refs = refs[0], refs[1], refs[2], refs[3:]
    (
        cot_ref,
        far_ref,
        other_ref,
        unit_ref,
        scale_ref,
        gain_ref,
        down_ref,
        slope_ref,
        up_ref,
        mixed_ref,
        low_mixed_ref,
        low_pre_ref,
        part_ref,
        small_ref,
    ) = refs
    step = pl.program_id(0)
    kept = flag_ref[0] > 0
    core = flag_ref[1] > 0
    first = jnp.where(core, other_ref[...], far_ref[...])
    second = jnp.where(core, far_ref[...], other_ref[...])
    far = jnp.concatenate([first, second], axis=0)
    cot = jnp.where(step == 0, cot_ref[flag_ref[2]], far).astype(f32)
    if has_base:
        here = flag_ref[1] == step
        back = jnp.where(here, mine_ref[...], theirs_ref[...]).astype(f32)
        grad_out = jnp.where(kept, base_ref[...] + back, cot)
    else:
        grad_out = jnp.where(kept, cot, 0.0)
    unit = unit_ref[...].astype(f32)
    grad_mixed = normalize_back(grad_out, unit, scale_ref[:, :1], gain_ref[...])
    mixed_ref[...] = grad_mixed
    low_mixed = grad_mixed.astype(bf16)
    low_mixed_ref[...] = low_mixed
    grad_active = dot_nt(low_mixed, down_ref[...])
    low_pre = (grad_active * slope_ref[...].astype(f32)).astype(bf16)
    low_pre_ref[...] = low_pre
    part_ref[...] = dot_nt(low_pre, up_ref[...]).astype(bf16)

    @pl.when(step == 0)
    def _():
        small_ref[...] = jnp.zeros_like(small_ref)

    width = grad_out.shape[1]

    def total(value):
        return jnp.sum(value, axis=0, keepdims=True)

    pre_sum = total(low_pre.astype(f32))
    small_ref[0:1, :] += total(grad_out * unit)
    small_ref[1:2, :] += total(grad_out)
    small_ref[2:3, :] += total(grad_mixed)
    small_ref[3:4, :] += pre_sum[:, :width]
    small_ref[4:5, :] += pre_sum[:, width:]


def feed_back(flags, base, cot, unit, scale, gain, down, slope, up, after=()):
    count, width = unit.shape
    units = up.shape[1]
    tile = count // 2
    wide, narrow = rows(tile, units), rows(tile, width)
    ins = [(flags, "smem", None)]
    if base is not None:
        ins += [(base[0], *narrow), (base[1], None, None), (base[2], None, None)]
    ins += [
        *[(c, None, None) for c in cot],
        (unit, *narrow),
        (scale, *rows(tile, 128)),
        (gain, None, None),
        (down, None, None),
        (slope, *wide),
        (up, None, None),
    ]
    return call(
        functools.partial(feed_back_kernel, base is not None),
        "feed_back",
        ins,
        [
            (like((count, width), f32), *narrow),
            (like((count, width), bf16), *narrow),
            (like((count, units), bf16), *wide),
            (like((count, width), bf16), *narrow),
            (like((8, width), f32), None, None),
        ],
        grid=(2,),
        after=after,
    )


def middle_back_kernel(
    mixed_ref,
    mine_ref,
    theirs_ref,
    unit_ref,
    scale_ref,
    gain_ref,
    out_ref,
    attended_ref,
    low_ref,
    context_ref,
    small_ref,
):
    summed = mine_ref[...].astype(f32) + theirs_ref[...].astype(f32)
    grad_hidden = mixed_ref[...] + summed
    unit = unit_ref[...].astype(f32)
    grad = normalize_back(grad_hidden, unit, scale_ref[:, :1], gain_ref[...])
    attended_ref[...] = grad
    low = grad.astype(bf16)
    low_ref[...] = low
    context_ref[...] = dot_nt(low, out_ref[...]).astype(bf16)

    @pl.when(pl.program_id(0) == 0)
    def _():
        small_ref[...] = jnp.zeros_like(small_ref)

    small_ref[0:1, :] += jnp.sum(grad_hidden * unit, axis=0, keepdims=True)
    small_ref[1:2, :] += jnp.sum(grad_hidden, axis=0, keepdims=True)
    small_ref[2:3, :] += jnp.sum(grad, axis=0, keepdims=True)


def middle_back(mixed, mine, theirs, unit, scale, gain, out_weight, after=()):
    count, width = mixed.shape
    local_width = out_weight.shape[0]
    tile = min(count, 256)
    narrow = rows(tile, width)
    return call(
        middle_back_kernel,
        "middle_back",
        [
            (mixed, *narrow),
            (mine, *narrow),
            (theirs, *narrow),
            (unit, *narrow),
            (scale, *rows(tile, 128)),
            (gain, None, None),
            (out_weight, None, None),
        ],
        [
            (like((count, width), f32), *narrow),
            (like((count, width), bf16), *narrow),
            (like((count, local_width), bf16), *rows(tile, local_width)),
            (like((8, width), f32), None, None),
        ],
        grid=(count // tile,),
        after=after,
    )


def put_halves(flag, value, column, send_ref, keep_ref):
    shares, half = send_ref.shape[:2]
    columns = slice(column, column + value.shape[1])
    value = value.astype(bf16)
    for share in range(shares):
        low = value[2 * share * half : (2 * share + 1) * half]
        high = value[(2 * share + 1) * half : (2 * share + 2) * half]
        send_ref[share, :, columns] = jnp.where(flag > 0, low, high)
        keep_ref[share, :, columns] = jnp.where(flag > 0, high, low)


def weight_kernel(pairs, flag_ref, *refs):
    lefts_rights, (send_ref, keep_ref) = refs[:-2], refs[-2:]
    column = 0
    for terms in pairs:
        value = 0.0
        for left, right in terms:
            value = value + dot_tn(lefts_rights[left][...], lefts_rights[right][...])
        put_halves(flag_ref[0], value, column, send_ref, keep_ref)
        column += value.shape[1]


def weight_grad(flag, arrays, pairs, by_share=False, after=()):
    shares = lax.axis_size("dp")
    width = arrays[pairs[0][0][0]].shape[1]
    columns = sum(arrays[terms[0][1]].shape[1] for terms in pairs)
    shape = (shares, width // (2 * shares), columns)
    if by_share:
        shape = (shares // 2, width // shares, columns)
    return call(
        functools.partial(weight_kernel, pairs),
        "weight_grad",
        [(flag, "smem", None)] + [(a, None, None) for a in arrays],
        [(like(shape, bf16), None, None)] * 2,
        after=after,
    )


def back_kernel(flag_ref, *refs):
    terms, (mine_ref, theirs_ref) = refs[:-2], refs[-2:]
    parts, half = mine_ref.shape[:2]
    grads = terms[: len(terms) // 2]
    weights = terms[len(terms) // 2 :]
    for part in range(parts):
        halves = []
        for side in range(2):
            start = (2 * part + side) * half
            value = 0.0
            for grad, weight in zip(grads, weights):
                value = value + dot_nt(grad[start : start + half], weight[0, 0])
            halves.append(value.astype(bf16))
        mine_ref[part] = jnp.where(flag_ref[1] > 0, halves[1], halves[0])
        theirs_ref[part] = jnp.where(flag_ref[1] > 0, halves[0], halves[1])


def back_grad(layer, flags, grads, weight, which, span, after=()):
    count, local_width = grads[0].shape
    width = weight.shape[2]
    out = like((count // span, span // 2, width), bf16), None, None
    return call(
        back_kernel,
        "back",
        [(flags, "smem", None)]
        + [(g, g.shape, lambda i: (0, 0)) for g in grads]
        + [(weight, (1, 1, width, local_width), lambda i, w=w: (layer, w, 0, 0)) for w in which],
        [out, out],
        grid=(1,),
        after=after,
    )


def sums_kernel(plans, *refs):
    count = (len(refs) - 2) // 2
    keeps, arrived, outs = refs[:count], refs[count : 2 * count], refs[2 * count :]
    for out, plan in zip(outs, plans):
        column = 0
        for source, start, width in plan:
            columns = slice(start, start + width)
            out[:, column : column + width] = add_low(
                keeps[source][0, :, columns], arrived[source][0, :, columns]
            )
            column += width


def sums(loads, plans, after=()):
    out = like((loads[0].keep.shape[1], sum(p[2] for p in plans[0])), bf16), None, None
    arrays = [load.keep for load in loads] + [load.arrived for load in loads]
    return call(
        functools.partial(sums_kernel, plans),
        "sums",
        [(a, None, None) for a in arrays],
        [out, out],
        after=after,
    )


def adds_kernel(a_ref, b_ref, c_ref, d_ref, first_ref, second_ref):
    first_ref[...] = add_low(a_ref[...], b_ref[...])
    second_ref[...] = add_low(c_ref[...], d_ref[...])


def adds(first, second, after=()):
    out = like(first[0].shape, bf16), None, None
    return call(
        adds_kernel,
        "adds",
        [(a, None, None) for a in (*first, *second)],
        [out, out],
        after=after,
    )


def relay_kernel(in_ref, out_ref):
    out_ref[...] = in_ref[...]


def relay(value, after):
    return call(
        relay_kernel, "adds", [(value, None, None)], [(like(value.shape, value.dtype), None, None)], after=after
    )[0]


def finish_kernel(flag_ref, a_ref, b_ref, c_ref, d_ref, *refs):
    qkv_ref, out_ref, up_ref, down_ref = refs
    units = up_ref.shape[2]
    local_width = qkv_ref.shape[3]

    def whole(flag, mine, other):
        low = jnp.where(flag > 0, other[...], mine[...])
        high = jnp.where(flag > 0, mine[...], other[...])
        return jnp.concatenate([low, high], axis=0).astype(f32)

    down = whole(flag_ref[0], a_ref, b_ref)
    down_ref[0] = down[:, :units]
    qkv_ref[0, 2] = down[:, units : units + local_width]
    out_ref[0] = down[:, units + local_width :]
    up = whole(flag_ref[1], c_ref, d_ref)
    up_ref[0] = up[:, :units]
    qkv_ref[0, 0] = up[:, units : units + local_width]
    qkv_ref[0, 1] = up[:, units + local_width :]


def finish(layer, flags, first, second, units, onto=()):
    half, columns = first[0].shape
    local_width = (columns - units) // 2
    shapes = (
        (2, 3, 2 * half, local_width),
        (2, 2 * half, local_width),
        (2, 2 * half, units),
        (2, 2 * half, units),
    )

    def place(shape):
        return like(shape, f32), (1,) + shape[1:], lambda i: (layer,) + (0,) * (len(shape) - 1)

    return call(
        finish_kernel,
        "finish",
        [(flags, "smem", None)]
        + [(a, a.shape, lambda i: (0, 0)) for a in (*first, *second)],
        [place(shape) for shape in shapes],
        grid=(1,),
        onto=onto,
    )


def pack_kernel(*refs):
    ins, out_ref = refs[:-1], refs[-1]
    each = len(ins) // 2
    out_ref[...] = jnp.zeros_like(out_ref)

    def total(ref):
        return jnp.sum(ref[...].astype(f32), axis=0, keepdims=True)

    for layer in range(2):
        dq, dv, dv2, feed, middle = ins[layer * each : (layer + 1) * each]
        width = dq.shape[1]
        base = 16 * layer
        out_ref[base : base + 1, :width] = total(dq)
        out_ref[base : base + 1, width:] = total(dv) + total(dv2)
        sources = (middle, 2), (middle, 0), (feed, 0), (middle, 1), (feed, 1), (feed, 3), (feed, 4)
        for i, (ref, row) in enumerate(sources + ((feed, 2),)):
            out_ref[base + 1 + i : base + 2 + i, :] = ref[row : row + 1, :]


def pack(first, second, after=()):
    width = first[3].shape[1]
    return call(
        pack_kernel,
        "pack",
        [(a, a.shape, lambda i: (0, 0)) for a in (*first, *second)],
        [(like((32, width), f32), (32, width), lambda i: (0, 0))],
        grid=(1,),
        after=after,
    )[0]


class Order:
    def __init__(self):
        self.last = ()

    def mark(self, *values):
        self.last = values

    def also(self, value):
        self.last = self.last + (value,)


def both_halves(mine, axis=0):
    other = swap(mine, "mp", 1)
    first = lax.axis_index("mp") == 0
    whole = jnp.where(
        first, jnp.stack([mine, other], axis=axis), jnp.stack([other, mine], axis=axis)
    )
    return whole.reshape(mine.shape[:axis] + (-1,) + mine.shape[axis + 1 :])


def my_half(value):
    count = value.shape[0] // 2
    return pick(value.reshape((2, count) + value.shape[1:]), lax.axis_index("mp"), 0)


def share_kernel(flag_ref, *refs):
    ins, (send_ref, keep_ref) = refs[:-2], refs[-2:]
    count = len(ins) // 2
    column = 0
    for keep, arrived in zip(ins[:count], ins[count:]):
        columns = slice(column, column + keep.shape[-1])
        column += keep.shape[-1]
        low, high = [add_low(keep[side], arrived[side]) for side in range(2)]
        send_ref[0, :, columns] = jnp.where(flag_ref[0] > 0, low, high)
        keep_ref[0, :, columns] = jnp.where(flag_ref[0] > 0, high, low)


def share_step(flag, loads, after=()):
    shares, half = loads[0].keep.shape[:2]
    columns = sum(load.keep.shape[2] for load in loads)
    arrays = [load.keep for load in loads] + [load.arrived for load in loads]
    out = like((shares // 2, half, columns), bf16), (1, half, columns), lambda i: (i, 0, 0)
    return call(
        share_kernel,
        "share",
        [(flag, "smem", None)] + [(a, (2,) + a.shape[1:], lambda i: (i, 0, 0)) for a in arrays],
        [out, out],
        grid=(shares // 2,),
        after=after,
    )


def split_kernel(flag_ref, *refs):
    count = len(refs) // 4
    for k in range(count):
        keep, arrived = refs[k], refs[count + k]
        send_ref, keep_ref = refs[2 * count + 2 * k : 2 * count + 2 * k + 2]
        half = keep.shape[1] // 2
        low = add_low(keep[:, :half], arrived[:, :half])
        high = add_low(keep[:, half:], arrived[:, half:])
        send_ref[...] = jnp.where(flag_ref[k] > 0, low, high)
        keep_ref[...] = jnp.where(flag_ref[k] > 0, high, low)


def split_step(flags, loads, after=()):
    shares, rows_, columns = loads[0].keep.shape
    arrays = [load.keep for load in loads] + [load.arrived for load in loads]
    out = (
        like((shares, rows_ // 2, columns), bf16),
        (1, rows_ // 2, columns),
        lambda i: (i, 0, 0),
    )
    return call(
        split_kernel,
        "share",
        [(flags, "smem", None)] + [(a, (1, rows_, columns), lambda i: (i, 0, 0)) for a in arrays],
        [out] * (2 * len(loads)),
        grid=(shares,),
        after=after,
    )


def join_kernel(flag_ref, a_ref, b_ref, c_ref, d_ref, first_ref, second_ref):
    for k, (mine, other, out) in enumerate(((a_ref, b_ref, first_ref), (c_ref, d_ref, second_ref))):
        half = mine.shape[0]
        out[:half] = jnp.where(flag_ref[k] > 0, other[...], mine[...])
        out[half:] = jnp.where(flag_ref[k] > 0, mine[...], other[...])


def join(flags, first, second, after=()):
    rows_, columns = first[0].shape
    out = like((2 * rows_, columns), bf16), None, None
    return call(
        join_kernel,
        "adds",
        [(flags, "smem", None)] + [(a, None, None) for a in (*first, *second)],
        [out, out],
        after=after,
    )


def last_bit():
    return bits_of("seq") - 1


class Load:
    def __init__(self, line, sent, axis, bit):
        send, self.keep = sent
        line.mark(send)
        self.arrived = swap(send, axis, 1 << bit)


def launch(line, arrays, pairs, axis, bit):
    flag = place_bit(axis, bit).reshape(1)
    return Load(
        line, weight_grad(flag, arrays, pairs, axis == "dp", line.last), axis, bit
    )


def split(line, loads, bits):
    flags = jnp.stack([place_bit("seq", bit) for bit in bits])
    sent = split_step(flags, loads, line.last)
    return [Load(line, sent[2 * k : 2 * k + 2], "seq", bit) for k, bit in enumerate(bits)]


def share(line, bit, *loads):
    flag = place_bit("dp", bit).reshape(1)
    return Load(line, share_step(flag, loads, line.last), "dp", bit)


def shares(line, first, *loads):
    for bit in range(first, bits_of("dp")):
        loads = (share(line, bit, *loads),)
    return loads[0]


class Tail:
    def __init__(self, line, loads, plans, twice):
        self.totals = sums(loads, plans, line.last)
        self.twice = twice
        bits = list(range(bits_of("seq")))
        if twice:
            self.hop(line, (0, last_bit()))
            return
        self.across = (bits[:-1], bits[1:])
        for place in range(len(bits) - 2):
            self.totals = [
                add_low(t, swap(t, "seq", 1 << across[place]))
                for t, across in zip(self.totals, self.across)
            ]
        self.hop(line, [across[-1] for across in self.across])

    def hop(self, line, bits):
        line.mark(*self.totals)
        self.arrived = [swap(t, "seq", 1 << b) for t, b in zip(self.totals, bits)]

    def gather(self, line):
        first, second = zip(self.totals, self.arrived)
        if self.twice:
            flags = jnp.stack([place_bit("seq", 0), place_bit("seq", last_bit())])
            self.totals = join(flags, first, second, line.last)
        else:
            self.totals = adds(first, second, line.last)
        self.hop(line, (last_bit(), 0))

    def finish(self, layer, units, onto=()):
        flags = jnp.stack([place_bit("seq", last_bit()), place_bit("seq", 0)])
        first, second = zip(self.totals, self.arrived)
        return finish(layer, flags, first, second, units, onto)


class Layer:
    def __init__(self, layer, params, weight_qkv, augs):
        self.layer = layer
        (
            _,
            self.bias_qv,
            self.weight_out,
            self.bias_out,
            self.gain,
            self.shift,
            self.weight_up,
            self.bias_up,
            self.weight_down,
            self.bias_down,
        ) = params
        self.weight_qkv = weight_qkv
        self.augs = augs

    def open(self, low_own):
        self.low_own = low_own
        self.query, self.key_own, self.value_own = project(
            self.layer, low_own, self.weight_qkv, self.bias_qv, True
        )

    def forward(self, inputs, low_rest, after=()):
        self.low_rest = low_rest
        key_rest, value_rest = project(
            self.layer, low_rest, self.weight_qkv, self.bias_qv, False
        )
        self.keys = (self.key_own, key_rest)
        self.values = (self.value_own, value_rest)
        self.context, self.log_total = attend(
            self.query, self.keys, self.values, self.augs, after
        )
        part = dot_nn(self.context, self.weight_out).astype(bf16)
        hidden, self.low_hidden, self.unit_one, self.scale_one, self.active, self.slope, part = feed(
            inputs,
            part,
            swap(part, "mp", 1),
            self.bias_out,
            self.gain[0],
            self.shift[0],
            self.weight_up,
            self.bias_up,
            self.weight_down,
        )
        result, self.unit_two, self.scale_two, *low_result = close(
            hidden,
            part,
            swap(part, "mp", 1),
            self.bias_down,
            self.gain[1],
            self.shift[1],
            self.layer == 0,
        )
        return result, low_result

    def feed_back(self, line, flags, base, cot):
        self.grad_mixed, self.low_mixed, self.low_pre, self.part, self.small_feed = feed_back(
            flags,
            base,
            cot,
            self.unit_two,
            self.scale_two,
            self.gain[1],
            self.weight_down,
            self.slope,
            self.weight_up,
            line.last,
        )
        line.mark(self.small_feed)

    def down_grad(self, line, axis, bit):
        return launch(line, (self.low_mixed, self.active), (((0, 1),),), axis, bit)

    def up_grad(self, line):
        return launch(line, (self.low_hidden, self.low_pre), (((0, 1),),), "seq", 0)

    def middle_back(self, line):
        self.grad_attended, self.low_attended, self.grad_context, self.small_middle = middle_back(
            self.grad_mixed,
            self.part,
            swap(self.part, "mp", 1),
            self.unit_one,
            self.scale_one,
            self.gain[0],
            self.weight_out,
            line.last,
        )
        line.mark(self.small_middle)

    def attend_back(self, line):
        self.dq, *grads = attend_back(
            self.query,
            self.keys,
            self.values,
            self.augs,
            self.log_total,
            self.context,
            self.grad_context,
            line.last,
        )
        self.dk, self.dv = grads[:2], grads[2:]
        line.mark(self.dq)

    def input_grad_parts(self, line, flags):
        span = self.query.shape[0]
        mine, theirs = back_grad(
            self.layer, flags, (self.dk[1], self.dv[1]), self.weight_qkv, (1, 2), span, line.last
        )
        arrived = swap(theirs, "mp", 1)
        self.own, theirs = back_grad(
            self.layer, flags, (self.dq, self.dk[0], self.dv[0]), self.weight_qkv, (0, 1, 2), span, (theirs,)
        )
        rest = add_low(mine, arrived)
        self.far = [swap(rest[j], "seq", 2 * (j + 1)) for j in range(rest.shape[0])]
        self.near = swap(theirs, "mp", 1)
        line.mark(rest, theirs)

    def input_grad(self):
        half = self.own[0].astype(f32) + self.near[0].astype(f32)
        half = (half + sum(f.astype(f32) for f in self.far)).astype(bf16)
        return (self.grad_attended, half, swap(half, "mp", 1))

    qk_pairs = (((0, 2),), ((0, 3), (1, 4)))
    vo_pairs = (((0, 3), (1, 4)), ((2, 5),))

    def value_out_grad(self, line):
        arrays = (self.low_own, self.low_rest, self.low_attended, *self.dv, self.context)
        return launch(line, arrays, self.vo_pairs, "seq", last_bit())

    def query_key_grad(self, line):
        arrays = (self.low_own, self.low_rest, self.dq, *self.dk)
        return launch(line, arrays, self.qk_pairs, "seq", 0)

    def small(self):
        return (self.dq, *self.dv, self.small_feed, self.small_middle)


def layer_part(index, params):
    parts = [array[index] for array in params]
    for i in (3, 7, 9):
        parts[i] = parts[i].reshape(1, -1)
    for i in (4, 5):
        parts[i] = parts[i][:, None, :]
    return tuple(parts)


def stack_pair(first_part, second_part):
    return jnp.stack([first_part, second_part])


def local(
    tokens,
    segments,
    dropped,
    qkv_weight,
    qv_bias,
    out_weight,
    out_bias,
    norm_gain,
    norm_shift,
    up_weight,
    up_bias,
    down_weight,
    down_bias,
    cotangent,
):
    params = (
        qkv_weight,
        qv_bias,
        out_weight,
        out_bias,
        norm_gain,
        norm_shift,
        up_weight,
        up_bias,
        down_weight,
        down_bias,
    )
    first = layer_part(0, params)
    second = layer_part(1, params)
    COUNT[0] = 0
    rows_here, span, width = tokens.shape
    assert rows_here == 2
    places = lax.axis_size("seq")
    place = lax.axis_index("seq")
    row = place & 1
    halves_of = tokens.reshape(rows_here, 2, span // 2, width)
    halves_of = pick(halves_of, lax.axis_index("mp"), 1)
    half_mine, half_partner = pick(halves_of, row, 0), pick(halves_of, 1 - row, 0)
    arrived = [swap((half_mine, half_partner)[c % 2], "seq", c) for c in range(1, places)]
    rest = both_halves(jnp.stack(arrived), axis=1)
    low_own = jnp.concatenate([pick(tokens, row, 0), rest[0]])
    low_rest = rest[1:].reshape(-1, width)
    seg_row = pick(segments, row, 0).reshape(places, span)
    for bit in range(bits_of("seq")):
        shaped = seg_row.reshape(places >> (bit + 1), 2, 1 << bit, span)
        seg_row = jnp.where(place_bit("seq", bit) == 1, shaped[:, ::-1], shaped).reshape(places, span)
    seg_keys = seg_row.reshape(places * span, 1)
    lane = lax.broadcasted_iota(jnp.int32, (1, PAIR), 1) % HEAD
    used = lane < SEGMENTS
    kaug = jnp.where(used & (seg_keys != lane), 1.0, 0.0).astype(bf16)
    qaug = jnp.where(used & (seg_keys[: 2 * span] == lane), -FAR, 0.0).astype(bf16)
    augs = (qaug, kaug[: 2 * span], kaug[2 * span :])
    cot_far = swap(my_half(pick(cotangent, 1 - row, 0)), "seq", 1)
    kept = 1 - pick(dropped, lax.axis_index("dp") * rows_here + row, 0)
    flags = jnp.stack([kept, lax.axis_index("mp"), row])

    one, two = Layer(0, first, qkv_weight, augs), Layer(1, second, qkv_weight, augs)
    one.open(low_own)
    small_params = [p for part in (first, second) for i, p in enumerate(part) if i in (1, 3, 4, 5, 7, 9)]
    hidden_one, (low_one,) = one.forward(low_own, low_rest, (*small_params, flags))
    low_half = my_half(low_one)
    arrived = [swap(low_half, "seq", c) for c in range(2, places, 2)]
    two.open(low_one)
    cot = (cotangent, cot_far, swap(cot_far, "mp", 1))
    rest = both_halves(relay(jnp.stack(arrived), (two.query, cot[2])), axis=1)
    result_two, _ = two.forward(hidden_one, rest.reshape(-1, width))
    result = jnp.where(kept > 0, result_two, hidden_one)

    class Return:
        def __init__(self, value):
            self.mine = value[:span]
            self.arrived = swap(my_half(value[span:].astype(bf16)), "seq", 1)
            self.other = swap(self.arrived, "mp", 1)

        def whole(self):
            core = lax.axis_index("mp") == 0
            far = jnp.where(
                core,
                jnp.concatenate([self.arrived, self.other]),
                jnp.concatenate([self.other, self.arrived]),
            ).astype(f32)
            return jnp.where(row == 0, jnp.stack([self.mine, far]), jnp.stack([far, self.mine]))

    line = Order()
    outputs = Return(result)
    twice = bits_of("seq") == 2 and width // lax.axis_size("dp") % 64 == 0
    first_core = lax.axis_index("mp") == 0
    units = up_weight.shape[2]
    half_units = units // 2
    plans_two = (
        ((0, 0, units), (1, units, half_units)),
        ((1, 0, units), (1, units + half_units, half_units)),
    )
    plans_one = (
        ((0, 0, units), (0, 2 * units, half_units)),
        ((0, units, units), (0, 2 * units + half_units, half_units)),
    )
    two.feed_back(line, flags, None, cot)
    down_two = two.down_grad(line, "dp", 0)
    up_two = two.up_grad(line)
    line.also(outputs.arrived)
    two.middle_back(line)
    line.also(outputs.other)
    two.attend_back(line)
    two.input_grad_parts(line, flags)
    value_two = two.value_out_grad(line)
    down_two = shares(line, 1, down_two)
    query_two = two.query_key_grad(line)
    up_two = share(line, 0, up_two)
    one.feed_back(line, flags, two.input_grad(), cot)
    down_one = one.down_grad(line, "seq", last_bit())
    up_one = one.up_grad(line)
    one.middle_back(line)
    attn_two = share(line, 0, value_two, query_two)
    one.attend_back(line)
    value_one = one.value_out_grad(line)
    query_one = one.query_key_grad(line)
    joined_two = shares(line, 1, up_two, attn_two)
    if twice:
        down_one, up_one = split(line, [down_one, up_one], (0, last_bit()))
    if twice:
        value_one, query_one = split(line, [value_one, query_one], (0, last_bit()))
    (down_two,) = split(line, [down_two], (last_bit(),))
    feed_one = share(line, 0, down_one, up_one)
    one.input_grad_parts(line, flags)
    attn_one = share(line, 0, value_one, query_one)
    base, own_half, other_half = one.input_grad()
    line.also(own_half)
    tail_two = Tail(line, [down_two, joined_two], plans_two, False)
    joined_one = shares(line, 1, feed_one, attn_one)
    tail_two.gather(line)
    halves = own_half, other_half
    back = jnp.where(first_core, jnp.concatenate(halves), jnp.concatenate(halves[::-1]))
    tokens_grad = Return(base + back.astype(f32))
    small = pack(one.small(), two.small(), line.last)
    line.also(small)
    for bit in range(bits_of("seq")):
        small = small + swap(small, "seq", 1 << bit)
    line.also(small)
    line.also(tokens_grad.arrived)
    tail_one = Tail(line, [joined_one], plans_one, twice)
    small = small + swap(small, "dp", 1)
    weight_sums = tail_two.finish(1, units)
    tail_one.gather(line)
    outputs, tokens_grad = outputs.whole(), tokens_grad.whole()
    small = relay(small, line.last)
    for bit in range(1, bits_of("dp")):
        small = small + swap(small, "dp", 1 << bit)
    qkv_sum, out_sum, up_sum, down_sum = tail_one.finish(0, units, weight_sums)
    out_sum, down_sum = out_sum.swapaxes(1, 2), down_sum.swapaxes(1, 2)
    small = small.reshape(2, 16, width)
    halves = width // 2
    qv_sum = small[:, 0].reshape(2, 2, halves)
    out_bias_sum = small[:, 1]
    gain_sum, shift_sum = small[:, 2:4], small[:, 4:6]
    up_bias_sum = small[:, 6:8].reshape(2, 2 * width)
    down_bias_sum = small[:, 8]

    return (
        outputs,
        tokens_grad,
        qkv_sum,
        qv_sum,
        out_sum,
        out_bias_sum,
        gain_sum,
        shift_sum,
        up_sum,
        up_bias_sum,
        down_sum,
        down_bias_sum,
    )


def solution(mesh):
    placed = (
        P("dp", "seq", None),
        P("dp", None),
        P(),
        P(None, None, None, "mp"),
        P(None, None, "mp"),
        P(None, "mp", None),
        P(),
        P(),
        P(),
        P(None, None, "mp"),
        P(None, "mp"),
        P(None, "mp", None),
        P(),
        P("dp", "seq", None),
    )
    return jax.shard_map(
        local,
        mesh=mesh,
        in_specs=placed,
        out_specs=(
            P("dp", "seq", None),
            P("dp", "seq", None),
            P(None, None, "dp", "mp"),
            P(None, None, "mp"),
            P(None, "mp", "dp"),
            P(),
            P(),
            P(),
            P(None, "dp", "mp"),
            P(None, "mp"),
            P(None, "mp", "dp"),
            P(),
        ),
        check_vma=False,
    )
```
